32 devices in a mesh: gx: 4 (over y, core), gy: 8 (over z, x).
Axes of the slice: x: 2, y: 2, z: 4, core: 2. Of those that a mesh axis runs over, the one named last changes fastest.
Arguments:
- solute_load: bfloat16 [512, 64, 256], P(('gx', 'gy')), may hold values from 0.099609375 to 3
- walker_displacement: float32 [512, 3, 256], P(('gx', 'gy')), may hold values from -4 to 4
- local_kelvin: float32 [512, 256], P(('gx', 'gy')), may hold values from 0.5 to 2
- couple_kinetic_factor: float32 [32], replicated, may hold values from 0.3 to 3
- arrhenius_onset: float32 [32], replicated, may hold values from 0.2 to 1.5
- adjacent_cell_keys: int32 [512, 16], P(('gx', 'gy')), may hold values from 0 to 24, as said below
- downstream_zone: int32 [512, 1], P(('gx', 'gy')), may hold values from 0 to 7; in each aligned block of 16 rows (0 to 15, 16 to 31, ...) at most 2 rows name the same one
Outputs:
- arrived: bfloat16 [512, 64, 256], P(('gx', 'gy'))
The draws below stay inside these ranges and needn't reach their ends.
Inputs may be any that keep to these rules, and one draw needn't show every extreme that they name: `adjacent_cell_keys`: each row lists 16 different codes; code o stands for the bin o // 5 - 2 rows and o % 5 - 2 columns away, and the first entry is 12, the bin itself. `downstream_zone`: entry t hands the bin to the region with the same index along gx and index t along gy; at most 2 bins of one region name the same t.
All inputs are finite; a program needn't handle non-finite values.
Results may differ from the reference program's by a relative error of at most 0.0035.
Values may be sent and summed in bfloat16 or wider, within the bound.
No kernel may reach another device: no remote copies, remote signals or barrier semaphores. Data moves between devices by JAX's collectives and lax.ppermute only.
A program may use at most 128 MiB of HBM per device.

```python
import math
from functools import partial
import jax
import jax.numpy as jnp
import numpy as np
from jax import lax

BX = 4
BY = 4
CELL_WALKERS = 256
SPECIES = 64
NBR = 16
STEPS = 2
HALF = 32
REG_Y = 8
CELL_COUNT_ALL = 512
CAP = 2
N_GX = 4
N_GY = 8
DEVICES = 32


def draw_adjacent_cell_keys(key, part):
    row_count = BX * BY * DEVICES
    scores = jax.random.randint(key, (row_count, 24), 0, 1 << 20) * 32 + jnp.arange(24, dtype=jnp.int32)[None, :]
    picked = jnp.argsort(scores, axis=1)[:, :NBR - 1].astype(jnp.int32)
    others = jnp.where(picked >= 12, picked + 1, picked)
    selfcode = jnp.full((row_count, 1), 12, jnp.int32)
    return jnp.concatenate([selfcode, others], axis=1).astype(jnp.int32)


def level_of(key, shape, pieces, smallest, largest):
    def one(axis_at, blocks):
        steps = jax.random.uniform(jax.random.fold_in(jax.random.fold_in(key, 6), axis_at), (blocks,), jnp.float32, smallest / len(pieces), largest / len(pieces))
        return jnp.repeat(jnp.exp(steps), shape[axis_at] // blocks).reshape((-1,) + (1,) * (len(shape) - axis_at - 1))

    level = one(*pieces[0])
    for cut in pieces[1:]:
        level = level * one(*cut)
    return level


def routed_block(stream_key, own, number, rows, number_of, top, bound, lean):
    ranking = jax.random.permutation(stream_key, number_of)
    heavy_load, usual = shares(number_of, rows * top, bound, lean, True), shares(number_of, rows * top, bound, lean, False)
    places = jnp.arange(number_of)

    def named(lengths, offset_by):
        used = int((lengths > 0).sum())
        fixed = max(1, used // 4)
        shifted = fixed + (places - fixed + offset_by * (used - fixed)) % max(1, number_of - fixed)
        return jnp.zeros((number_of,), jnp.int32).at[ranking[jnp.where(places < fixed, places, shifted)]].set(jnp.asarray(lengths, jnp.int32))

    lengths = jnp.where(number % 4 == 0, named(heavy_load, number // 4), named(usual, number - number // 4 - 1))
    mixed = jax.random.permutation(jax.random.fold_in(own, 3), number_of)
    source_of, taker = mixed[0:number_of // 2 * 2:2], mixed[1:number_of // 2 * 2:2]
    room = jnp.minimum(lengths[source_of] - 1, bound - lengths[taker]) // 2
    room = jnp.where((source_of == ranking[0]) | (taker == ranking[0]) | (lengths[taker] == 0), 0, jnp.maximum(room, 0))
    shifted = jax.random.randint(jax.random.fold_in(own, 4), (number_of // 2,), 0, 1 << 20) % (room + 1)
    lengths = lengths.at[source_of].add(-shifted).at[taker].add(shifted)
    members = jnp.searchsorted(jnp.cumsum(lengths), jnp.arange(rows * top), side="right").astype(jnp.int32)
    grid = members.reshape(top, rows).T
    grid = grid[jax.random.permutation(jax.random.fold_in(own, 1), rows)]
    offset_by = jax.random.randint(jax.random.fold_in(own, 2), (rows, 1), 0, top)
    return jnp.take_along_axis(grid, (jnp.arange(top)[None, :] + offset_by) % top, axis=1)


def shares(amount, total, reach, lean, full):
    weights = [(1 << 20) // math.isqrt(standing ** lean) + 1 for standing in range(1, amount + 1)]
    largest = reach if full else min(reach, max(-(-total // amount), total * weights[0] // sum(weights)))
    least = 1 if total - largest >= amount - 1 else 0
    holding, surplus = [largest] + [least] * (amount - 1), total - largest - least * (amount - 1)
    while surplus > 0:
        free = [i for i in range(1, amount) if holding[i] < largest] or [i for i in range(1, amount) if holding[i] < reach]
        pool, budget = sum([weights[i] for i in free]), surplus
        for i in free:
            addition = min(reach - holding[i], max(1, budget * weights[i] // pool), surplus)
            holding[i] = holding[i] + addition
            surplus = surplus - addition
    return np.array(holding)


def bell_draw(rng, dims, width, most, cuts=(), kind=jnp.bfloat16):
    values = jax.random.normal(rng, dims, jnp.float32) * width
    if len(cuts) > 0:
        values = level_of(rng, dims, cuts, -0.22, 0.18) * values
    return jnp.clip(values, min=-most, max=most).astype(kind)


def setup_inputs(seed: int = 0) -> dict:
    key_list = jax.random.split(jax.random.key(seed), 8)
    solute_load = jnp.clip(jnp.exp(math.log(3.0) - 3.4051113 * jax.random.uniform(key_list[0], (CELL_COUNT_ALL, SPECIES, CELL_WALKERS), jnp.float32) ** level_of(key_list[0], (CELL_COUNT_ALL, SPECIES, CELL_WALKERS), ((0, 32),), -0.2, 0.2)), 0.099609375, 3.0).astype(jnp.bfloat16)
    walker_displacement = bell_draw(key_list[1], (CELL_COUNT_ALL, 3, CELL_WALKERS), 0.8, 4.0, ((0, 32),), jnp.float32)
    local_kelvin = jnp.clip(0.5 + 1.5 * jax.random.uniform(key_list[2], (CELL_COUNT_ALL, CELL_WALKERS), jnp.float32) ** level_of(key_list[2], (CELL_COUNT_ALL, CELL_WALKERS), ((0, 32),), -0.2, 0.2), 0.5, 2.0)
    couple_kinetic_factor = jnp.clip(jnp.exp(jax.random.uniform(key_list[3], (HALF,), jnp.float32, math.log(0.3), math.log(3.0))), 0.3, 3.0)
    arrhenius_onset = jnp.clip(jax.random.uniform(key_list[4], (HALF,), jnp.float32, 0.2, 1.5), 0.2, 1.5)
    adjacent_cell_keys = draw_adjacent_cell_keys(jax.random.fold_in(key_list[7], 71), 0)
    downstream_zone_keys = jax.random.split(jax.random.fold_in(key_list[6], 1), CELL_COUNT_ALL // (BX * BY))
    downstream_zone_turns = jax.random.permutation(jax.random.fold_in(key_list[6], 3), CELL_COUNT_ALL // (BX * BY))
    downstream_zone = jax.vmap(lambda own, number: routed_block(jax.random.fold_in(key_list[6], 2), own, number, BX * BY, REG_Y, 1, CAP, 2))(downstream_zone_keys, downstream_zone_turns).reshape((CELL_COUNT_ALL, 1))
    return dict(solute_load=solute_load, walker_displacement=walker_displacement, local_kelvin=local_kelvin, couple_kinetic_factor=couple_kinetic_factor, arrhenius_onset=arrhenius_onset, adjacent_cell_keys=adjacent_cell_keys, downstream_zone=downstream_zone)


inverse_width = 4.0


def mesh_sequence(flat_rows):
    trailing = flat_rows.shape[1:]
    shaped = flat_rows.reshape((N_GX, N_GY, BX, BY) + trailing)
    permuted_axes = (0, 2, 1, 3) + tuple(range(4, 4 + len(trailing)))
    return shaped.transpose(permuted_axes).reshape((N_GX * BX, N_GY * BY) + trailing)


def device_order(mesh_vertical):
    trailing = mesh_vertical.shape[2:]
    shaped = mesh_vertical.reshape((N_GX, BX, N_GY, BY) + trailing)
    permuted_axes = (0, 2, 1, 3) + tuple(range(4, 4 + len(trailing)))
    return shaped.transpose(permuted_axes).reshape((-1,) + trailing)


def react(mixture, warming_curve, couple_kinetic_factor, arrhenius_onset):
    halves = mixture.shape[1] // 2
    kind_one = mixture[:, :halves]
    kind_two = mixture[:, halves:]
    speeds = couple_kinetic_factor[None, :, None] * jnp.exp(-arrhenius_onset[None, :, None] / warming_curve[:, None, :])
    reacted = speeds * kind_one * kind_two / (1.0 + speeds * (kind_one + kind_two))
    return jnp.concatenate([kind_one - reacted, kind_two - reacted], axis=1).astype(jnp.bfloat16)


def mix_group(ext_species, ext_pos, couple_kinetic_factor, arrhenius_onset, packet):
    centre, neighbour_idx, offsets, inside, warming_curve = packet
    centre_pos = ext_pos[centre]
    neigh_pos = ext_pos[neighbour_idx]
    shift_along = (offsets // 5 - 2).astype(jnp.float32)
    shift_across = (offsets % 5 - 2).astype(jnp.float32)
    offset_gap = centre_pos[:, None, 0, :, None] - neigh_pos[:, :, 0, None, :] - shift_along[:, :, None, None]
    squared = offset_gap * offset_gap
    offset_gap = centre_pos[:, None, 1, :, None] - neigh_pos[:, :, 1, None, :] - shift_across[:, :, None, None]
    squared = squared + offset_gap * offset_gap
    offset_gap = centre_pos[:, None, 2, :, None] - neigh_pos[:, :, 2, None, :]
    squared = squared + offset_gap * offset_gap
    kernel = jnp.exp(-squared * inverse_width) * inside[:, :, None, None]
    row_total = jnp.sum(kernel, axis=(1, 3))
    weights = (kernel / row_total[:, None, :, None]).astype(jnp.bfloat16)
    sources = ext_species[neighbour_idx]
    mixture = jnp.einsum('gksq,gkpq->gsp', sources.astype(jnp.float32), weights.astype(jnp.float32))
    return react(mixture, warming_curve, couple_kinetic_factor, arrhenius_onset)


def reference(solute_load, walker_displacement, local_kelvin, couple_kinetic_factor, arrhenius_onset, adjacent_cell_keys, downstream_zone):
    mesh_vertical = N_GX * BX
    mesh_horizontal = N_GY * BY
    species_grid = mesh_sequence(solute_load)
    pos_grid = mesh_sequence(walker_displacement)
    warming_curve = mesh_sequence(local_kelvin).reshape(mesh_vertical * mesh_horizontal, CELL_WALKERS)
    offsets_list = mesh_sequence(adjacent_cell_keys).reshape(mesh_vertical * mesh_horizontal, NBR)
    coord_x = jnp.repeat(jnp.arange(mesh_vertical, dtype=jnp.int32), mesh_horizontal)
    coord_y = jnp.tile(jnp.arange(mesh_horizontal, dtype=jnp.int32), mesh_vertical)
    row_width = mesh_horizontal + 4
    centre = (coord_x + 2) * row_width + coord_y + 2
    target_x = coord_x[:, None] + offsets_list // 5 - 2
    target_y = coord_y[:, None] + offsets_list % 5 - 2
    neighbour_idx = (target_x + 2) * row_width + target_y + 2
    inside = ((target_x >= 0) & (target_x < mesh_vertical) & (target_y >= 0) & (target_y < mesh_horizontal)).astype(jnp.float32)
    padded_pos = jnp.pad(pos_grid, ((2, 2), (2, 2), (0, 0), (0, 0))).reshape(-1, 3, CELL_WALKERS)
    packets = tuple(member.reshape((-1, 16) + member.shape[1:]) for member in (centre, neighbour_idx, offsets_list, inside, warming_curve))
    for repeat in range(STEPS):
        padded = jnp.pad(species_grid, ((2, 2), (2, 2), (0, 0), (0, 0))).reshape(-1, SPECIES, CELL_WALKERS)
        result = lax.map(partial(mix_group, padded, padded_pos, couple_kinetic_factor, arrhenius_onset), packets)
        species_grid = result.reshape(mesh_vertical, mesh_horizontal, SPECIES, CELL_WALKERS)
    finished = device_order(species_grid)
    target = downstream_zone[:, 0].reshape(N_GX, N_GY, BX * BY)
    chosen = (target[..., None] == jnp.arange(N_GY, dtype=jnp.int32)).astype(jnp.int32)
    earlier_count = jnp.cumsum(chosen, axis=2) - chosen
    order_slot = jnp.sum(earlier_count * chosen, axis=3)
    band_ids = jnp.arange(N_GX, dtype=jnp.int32)[:, None, None]
    source_ids = jnp.arange(N_GY, dtype=jnp.int32)[None, :, None]
    row_index = ((band_ids * N_GY + target) * N_GY + source_ids) * CAP + order_slot
    arrived = jnp.zeros((N_GX * N_GY * N_GY * CAP, SPECIES, CELL_WALKERS), jnp.bfloat16)
    return arrived.at[row_index.reshape(-1)].set(finished)
```

```python
import functools
import math

import jax
import jax.numpy as jnp
from jax import lax
from jax.experimental import pallas as pl
from jax.experimental.pallas import tpu as pltpu
from jax.sharding import PartitionSpec as P

BX = 4
BY = 4
STEPS = 2
CAP = 2
HALO = 2
WIDTH = 2 * HALO + 1

inverse_width = 4.0
SCALE = math.sqrt(inverse_width * math.log2(math.e))
FAR = -1e30

f32 = jnp.float32
bf16 = jnp.bfloat16

OWN = BX * BY
SIDE = BX * HALO
BAND = HALO * (BY + 2 * HALO)
LEFT = OWN
RIGHT = LEFT + SIDE
UP = RIGHT + SIDE
DOWN = UP + BAND
EXT = DOWN + BAND


def chain(count):
    forward = [(i, i + 1) for i in range(count - 1)]
    return forward, [(b, a) for a, b in forward]


def exchange(block):
    trailing = block.shape[1:]
    grid = block.reshape((BX, BY) + trailing)
    forward, backward = chain(lax.axis_size("gy"))
    left = lax.ppermute(grid[:, BY - HALO :], "gy", forward)
    right = lax.ppermute(grid[:, :HALO], "gy", backward)
    rows = jnp.concatenate([left, grid, right], axis=1)
    forward, backward = chain(lax.axis_size("gx"))
    up = lax.ppermute(rows[BX - HALO :], "gx", forward)
    down = lax.ppermute(rows[:HALO], "gx", backward)
    flat = lambda x: x.reshape((-1,) + trailing)
    return block, flat(left), flat(right), flat(up), flat(down)


PIECES = (OWN, SIDE, SIDE, BAND, BAND)
STARTS = (0, LEFT, RIGHT, UP, DOWN)


def slot_of(ex, ey):
    wide = BY + 2 * HALO
    inner = jnp.where(
        ey < 0,
        LEFT + ex * HALO + ey + HALO,
        jnp.where(ey >= BY, RIGHT + ex * HALO + ey - BY, ex * BY + ey),
    )
    outer = jnp.where(
        ex < 0, UP + (ex + HALO) * wide + ey + HALO, DOWN + (ex - BX) * wide + ey + HALO
    )
    return jnp.where((ex >= 0) & (ex < BX), inner, outer)


def place_of(piece, i):
    wide = BY + 2 * HALO
    if piece == 0:
        return i // BY, i % BY
    if piece == 1:
        return i // HALO, i % HALO - HALO
    if piece == 2:
        return i // HALO, i % HALO + BY
    if piece == 3:
        return i // wide - HALO, i % wide - HALO
    return i // wide + BX, i % wide - HALO


def three_parts(x):
    high = x.astype(bf16).astype(f32)
    rest = x - high
    middle = rest.astype(bf16).astype(f32)
    return high, middle, rest - middle


def coordinates(pos, ex, ey):
    row = lax.broadcasted_iota(jnp.int32, (8, pos.shape[-1]), 0)
    padded = jnp.concatenate([pos, jnp.zeros((5, pos.shape[-1]), f32)], axis=0)
    middle = jnp.where(
        row == 0,
        ex.astype(f32) - (BX - 1) / 2,
        jnp.where(row == 1, ey.astype(f32) - (BY - 1) / 2, 0.0),
    )
    return (padded + middle) * SCALE, row


def features_of_source(pos, ex, ey, inside):
    v, row = coordinates(pos, ex, ey)
    norm = jnp.sum(v * v, axis=0, keepdims=True)
    high, middle, low = three_parts(v)
    nh, nm, nl = three_parts(norm)
    nh = jnp.where(inside, -nh, FAR)
    last = row == 3
    groups = (
        jnp.where(last, nh, high),
        jnp.where(last, -nm, high),
        jnp.where(last, -nl, middle),
        jnp.where(last, 1.0, high),
        jnp.where(last, 1.0, low),
        jnp.where(last, 1.0, middle),
    )
    return jnp.concatenate(groups, axis=0)


def features_of_target(pos, ex, ey):
    u, row = coordinates(pos, ex, ey)
    norm = jnp.sum(u * u, axis=0, keepdims=True)
    high, middle, low = three_parts(u)
    nh, nm, nl = three_parts(norm)
    last = row == 3
    groups = (
        jnp.where(last, 1.0, 2.0 * high),
        jnp.where(last, 1.0, 2.0 * middle),
        jnp.where(last, 1.0, 2.0 * high),
        jnp.where(last, -nh, 2.0 * low),
        jnp.where(last, -nm, 2.0 * high),
        jnp.where(last, -nl, 2.0 * middle),
    )
    return jnp.concatenate(groups, axis=0)


FEATURES = 48


def react(mixture, kelvin, factor, onset):
    half = mixture.shape[0] // 2
    u = mixture[:half]
    v = mixture[half:]
    speed = factor * jnp.exp(-onset / kelvin)
    reacted = speed * u * v / (1.0 + speed * (u + v))
    return jnp.concatenate([u - reacted, v - reacted], axis=0).astype(bf16)


def load_species(refs, buffer, sem):
    copies = [
        pltpu.make_async_copy(ref, buffer.at[pl.ds(start, count)], sem.at[i])
        for i, (ref, start, count) in enumerate(zip(refs, STARTS, PIECES))
    ]
    for copy in copies:
        copy.start()
    return copies


def first_step(
    near_ref,
    meta_ref,
    p0,
    p1,
    p2,
    p3,
    p4,
    s0,
    s1,
    s2,
    s3,
    s4,
    kelvin_ref,
    factor_ref,
    onset_ref,
    out_ref,
    w_ref,
    inv_ref,
    source,
    target,
    species,
    gathered,
    sem,
):
    b = pl.program_id(0)
    neighbours = near_ref.shape[0] // OWN
    parts = source.shape[1]

    @pl.when(b == 0)
    def _():
        copies = load_species((s0, s1, s2, s3, s4), species, sem)
        for piece, ref in enumerate((p0, p1, p2, p3, p4)):

            def one(i, _, piece=piece, ref=ref):
                ex, ey = place_of(piece, i)
                gx = meta_ref[0] + ex
                gy = meta_ref[1] + ey
                inside = (gx >= 0) & (gx < meta_ref[2]) & (gy >= 0) & (gy < meta_ref[3])
                pos = ref[i]
                f = features_of_source(pos, ex, ey, inside)
                source[STARTS[piece] + i] = f.T.astype(bf16)
                if piece == 0:
                    target[i] = features_of_target(pos, ex, ey).astype(bf16)
                return 0

            lax.fori_loop(0, PIECES[piece], one, 0)
        for copy in copies:
            copy.wait()

    f = target[b]
    total = jnp.zeros((8, parts), f32)
    for k in range(neighbours):
        q = near_ref[b * neighbours + k]
        e = jnp.dot(source[q], f, preferred_element_type=f32)
        w = jnp.exp2(e)
        total = total + w.reshape(parts // 8, 8, parts).sum(0)
        w_ref[0, pl.ds(k * parts, parts)] = w.astype(bf16)
        gathered[:, k * parts : (k + 1) * parts] = species[q]
    mixed = jnp.dot(gathered[...], w_ref[0], preferred_element_type=f32)
    inv = 1.0 / jnp.sum(total, axis=0, keepdims=True)
    inv_ref[0] = inv
    out_ref[0] = react(mixed * inv, kelvin_ref[0], factor_ref[...], onset_ref[...])


def last_step(
    near_ref,
    bin_ref,
    used_ref,
    s0,
    s1,
    s2,
    s3,
    s4,
    w_ref,
    inv_ref,
    kelvin_ref,
    factor_ref,
    onset_ref,
    out_ref,
    species,
    gathered,
    sem,
):
    s = pl.program_id(0)
    neighbours = near_ref.shape[0] // OWN
    parts = species.shape[2]

    @pl.when(s == 0)
    def _():
        for copy in load_species((s0, s1, s2, s3, s4), species, sem):
            copy.wait()

    @pl.when(used_ref[s] == 0)
    def _():
        out_ref[...] = jnp.zeros_like(out_ref)

    @pl.when(used_ref[s] != 0)
    def _():
        b = bin_ref[s]
        for k in range(neighbours):
            q = near_ref[b * neighbours + k]
            gathered[:, k * parts : (k + 1) * parts] = species[q]
        mixed = jnp.dot(gathered[...], w_ref[0], preferred_element_type=f32)
        out_ref[0] = react(mixed * inv_ref[0], kelvin_ref[0], factor_ref[...], onset_ref[...])


def body(
    solute_load,
    walker_displacement,
    local_kelvin,
    couple_kinetic_factor,
    arrhenius_onset,
    adjacent_cell_keys,
    downstream_zone,
):
    lane_count = lax.axis_size("gy")
    bins, kinds, parts = solute_load.shape
    neighbours = adjacent_cell_keys.shape[1]
    meta = jnp.stack(
        [
            lax.axis_index("gx") * BX,
            lax.axis_index("gy") * BY,
            jnp.int32(lax.axis_size("gx") * BX),
            jnp.int32(lane_count * BY),
        ]
    ).astype(jnp.int32)
    ids = jnp.arange(bins, dtype=jnp.int32)
    near = slot_of(
        (ids // BY)[:, None] + adjacent_cell_keys // WIDTH - HALO,
        (ids % BY)[:, None] + adjacent_cell_keys % WIDTH - HALO,
    ).reshape(-1)
    kelvin = local_kelvin.reshape(bins, 1, parts)
    factor = couple_kinetic_factor.reshape(-1, 1)
    onset = arrhenius_onset.reshape(-1, 1)

    anywhere = pl.BlockSpec(memory_space=pl.ANY)
    whole = lambda shape: pl.BlockSpec(shape, lambda *_: (0,) * len(shape))
    scratch = [
        pltpu.VMEM((EXT, kinds, parts), bf16),
        pltpu.VMEM((kinds, neighbours * parts), bf16),
        pltpu.SemaphoreType.DMA((5,)),
    ]
    positions = exchange(walker_displacement)
    species = exchange(solute_load)
    moved, weights, inv = pl.pallas_call(
        first_step,
        out_shape=(
            jax.ShapeDtypeStruct((bins, kinds, parts), bf16),
            jax.ShapeDtypeStruct((bins, neighbours * parts, parts), bf16),
            jax.ShapeDtypeStruct((bins, 1, parts), f32),
        ),
        grid_spec=pltpu.PrefetchScalarGridSpec(
            num_scalar_prefetch=2,
            grid=(bins,),
            in_specs=[whole(p.shape) for p in positions]
            + [anywhere] * 5
            + [
                pl.BlockSpec((1, 1, parts), lambda b, *_: (b, 0, 0)),
                whole(factor.shape),
                whole(onset.shape),
            ],
            out_specs=(
                pl.BlockSpec((1, kinds, parts), lambda b, *_: (b, 0, 0)),
                pl.BlockSpec((1, neighbours * parts, parts), lambda b, *_: (b, 0, 0)),
                pl.BlockSpec((1, 1, parts), lambda b, *_: (b, 0, 0)),
            ),
            scratch_shapes=[
                pltpu.VMEM((EXT, parts, FEATURES), bf16),
                pltpu.VMEM((bins, FEATURES, parts), bf16),
            ]
            + scratch,
        ),
        name="first_step",
    )(near, meta, *positions, *species, kelvin, factor, onset)

    target = downstream_zone[:, 0]
    earlier = (target[None, :] == target[:, None]) & (ids[None, :] < ids[:, None])
    slot_of_bin = target * CAP + jnp.sum(earlier.astype(jnp.int32), axis=1)
    slots = lane_count * CAP
    hit = slot_of_bin[None, :] == jnp.arange(slots, dtype=jnp.int32)[:, None]
    bin_of_slot = jnp.sum(jnp.where(hit, ids[None, :], 0), axis=1)
    used = jnp.sum(hit.astype(jnp.int32), axis=1)

    species = exchange(moved)
    by_bin = lambda s, near, bin_of, used: (bin_of[s], 0, 0)
    packed = pl.pallas_call(
        last_step,
        out_shape=jax.ShapeDtypeStruct((slots, kinds, parts), bf16),
        grid_spec=pltpu.PrefetchScalarGridSpec(
            num_scalar_prefetch=3,
            grid=(slots,),
            in_specs=[anywhere] * 5
            + [
                pl.BlockSpec((1, neighbours * parts, parts), by_bin),
                pl.BlockSpec((1, 1, parts), by_bin),
                pl.BlockSpec((1, 1, parts), by_bin),
                whole(factor.shape),
                whole(onset.shape),
            ],
            out_specs=pl.BlockSpec((1, kinds, parts), lambda s, *_: (s, 0, 0)),
            scratch_shapes=scratch,
        ),
        name="last_step",
    )(near, bin_of_slot, used, *species, weights, inv, kelvin, factor, onset)
    return lax.all_to_all(packed, "gy", split_axis=0, concat_axis=0, tiled=True)


def solution(mesh):
    in_specs = (
        P(("gx", "gy"), None, None),
        P(("gx", "gy"), None, None),
        P(("gx", "gy"), None),
        P(),
        P(),
        P(("gx", "gy"), None),
        P(("gx", "gy"), None),
    )
    out_specs = P(("gx", "gy"), None, None)
    return jax.shard_map(body, mesh=mesh, in_specs=in_specs, out_specs=out_specs, check_vma=False)
```

```python
import math

import jax
import jax.numpy as jnp
from jax import lax
from jax.experimental import pallas as pl
from jax.experimental.pallas import tpu as pltpu
from jax.sharding import PartitionSpec as P


BX = 4
BY = 4
CAP = 2
HALO = 2
WIDTH = 2 * HALO + 1

inverse_width = 4.0
SCALE = math.sqrt(inverse_width * math.log2(math.e))
FAR = -1e30
FEATURES = 48

f32 = jnp.float32
bf16 = jnp.bfloat16
i32 = jnp.int32

SIDE = BX * HALO
QUAD = HALO * HALO
BAND = 4 * QUAD
EXT = 4 * SIDE + 2 * BAND
COUNTS = (SIDE, SIDE, SIDE, SIDE, BAND, BAND)
STARTS = (0, SIDE, 2 * SIDE, 3 * SIDE, 4 * SIDE, 4 * SIDE + BAND)


def swaps(count):
    def both(first):
        out = []
        for i in range(first, count - 1, 2):
            out += [(i, i + 1), (i + 1, i)]
        return out

    return both(0), both(1)


def slot_of(ex, ey, odd_lane, odd_band):
    low = ey < BY // 2
    by_a = low == (odd_lane == 1)
    own = (ey >= 0) & (ey < BY)
    piece = jnp.where(by_a, 0, 1) + jnp.where(own, 0, 2)
    column = (ey + HALO) % HALO
    inner = piece * SIDE + ex * HALO + column
    from_a = (ex < 0) == (odd_band == 1)
    row = jnp.where(ex < 0, ex + HALO, ex - BX)
    outer = jnp.where(from_a, STARTS[4], STARTS[5]) + piece * QUAD + row * HALO + column
    return jnp.where((ex >= 0) & (ex < BX), inner, outer)


def place_of(piece, i, odd_lane, odd_band):
    if piece < 4:
        part, ex = piece, i // HALO
    else:
        part, row = i // QUAD, i % QUAD // HALO
        up = (odd_band == 1) if piece == 4 else (odd_band == 0)
        ex = jnp.where(up, row - HALO, row + BX)
    by_a = part % 2 == 0
    low = (by_a == (odd_lane == 1)) if not isinstance(by_a, bool) else (odd_lane == int(by_a))
    outside = part >= 2
    base = jnp.where(low, jnp.where(outside, -HALO, 0), jnp.where(outside, BY, BY - HALO))
    return ex, base + i % HALO


def split(meta_ref, zone_ref, x0, x1, a0, b0, a1, b1, row_ref, taken):
    sources, outs = (x0, x1), (a0, b0, a1, b1)
    for z in range(taken.shape[0]):
        taken[z] = 0

    def place(b, _):
        zone = zone_ref[b, 0]
        order = taken[zone]
        taken[zone] = order + 1
        row_ref[b] = zone * CAP + order
        return 0

    lax.fori_loop(0, BX * BY, place, 0)
    low_a = jnp.where(meta_ref[4] == 1, 0, BY - HALO)
    for n, x in enumerate(sources):
        for r in range(BX):
            outs[2 * n][pl.ds(r * HALO, HALO)] = x[pl.ds(r * BY + low_a, HALO)]
            outs[2 * n + 1][pl.ds(r * HALO, HALO)] = x[pl.ds(r * BY + BY - HALO - low_a, HALO)]


def pack(meta_ref, p0, p1, p2, p3, out_a, out_b):
    size = BX * HALO
    from_a = jnp.where(meta_ref[5] == 1, 0, size - QUAD)
    for n, x in enumerate((p0, p1, p2, p3)):
        out_a[pl.ds(n * QUAD, QUAD)] = x[pl.ds(from_a, QUAD)]
        out_b[pl.ds(n * QUAD, QUAD)] = x[pl.ds(size - QUAD - from_a, QUAD)]


def swap(by_a, by_b, axis):
    pairs_a, pairs_b = swaps(lax.axis_size(axis))
    from_b = lax.ppermute(by_b, axis, pairs_b)
    from_a = lax.ppermute(by_a, axis, pairs_a)
    return from_a, from_b


def three_parts(x):
    high = x.astype(bf16).astype(f32)
    rest = x - high
    middle = rest.astype(bf16).astype(f32)
    return high, middle, rest - middle


def coordinates(pos, ex, ey):
    row = lax.broadcasted_iota(i32, (8, pos.shape[-1]), 0)
    padded = jnp.concatenate([pos, jnp.zeros((5, pos.shape[-1]), f32)], axis=0)
    middle = jnp.where(
        row == 0,
        ex.astype(f32) - (BX - 1) / 2,
        jnp.where(row == 1, ey.astype(f32) - (BY - 1) / 2, 0.0),
    )
    return (padded + middle) * SCALE, row


def features(pos, ex, ey, inside, as_target):
    x, row = coordinates(pos, ex, ey)
    norm = jnp.sum(x * x, axis=0, keepdims=True)
    high, middle, low = three_parts(x)
    nh, nm, nl = three_parts(norm)
    last = row == 3
    pick = lambda a, b: jnp.where(last, a, b)
    source = (
        pick(jnp.where(inside, -nh, FAR), high),
        pick(-nm, high),
        pick(-nl, middle),
        pick(1.0, high),
        pick(1.0, low),
        pick(1.0, middle),
    )
    source = jnp.concatenate(source, axis=0).T.astype(bf16)
    if not as_target:
        return source, None
    high, middle, low = 2.0 * high, 2.0 * middle, 2.0 * low
    target = (
        pick(1.0, high),
        pick(1.0, middle),
        pick(1.0, high),
        pick(-nh, low),
        pick(-nm, high),
        pick(-nl, middle),
    )
    return source, jnp.concatenate(target, axis=0).astype(bf16)


def build_rows(near_ref, source, target, w_refs, inv_ref, first_row):
    parts = source.shape[1]
    neighbours = near_ref.shape[0] // (BX * BY)
    for g, w_ref in enumerate(w_refs):

        def one(c, _, g=g, w_ref=w_ref):
            b = (first_row + g) * BY + c
            f = target[b]
            total = jnp.zeros((8, parts), f32)
            for k in range(neighbours):
                q = near_ref[b * neighbours + k]
                w = jnp.exp2(jnp.dot(source[q], f, preferred_element_type=f32))
                total = total + w.reshape(parts // 8, 8, parts).sum(0)
                w_ref[c, pl.ds(k * parts, parts)] = w.astype(bf16)
            inv_ref[pl.ds(g * BY + c, 1)] = 1.0 / jnp.sum(total, axis=0, keepdims=True)
            return 0

        lax.fori_loop(0, BY, one, 0)


def build_first(near_ref, meta_ref, own, c0, c1, r0, r1, w0, w1, inv_ref, source, target):
    odd_lane, odd_band = meta_ref[4], meta_ref[5]

    def put(pos, ex, ey, slot, as_target):
        gx = meta_ref[0] + ex
        gy = meta_ref[1] + ey
        inside = (gx >= 0) & (gx < meta_ref[2]) & (gy >= 0) & (gy < meta_ref[3])
        s, t = features(pos, ex, ey, inside, as_target)
        source[slot] = s
        return t

    def mine(b, _):
        ex, ey = b // BY, b % BY
        target[b] = put(own[b], ex, ey, slot_of(ex, ey, odd_lane, odd_band), True)
        return 0

    lax.fori_loop(0, BX * BY, mine, 0)
    for piece, ref in ((2, c0), (3, c1), (4, r0), (5, r1)):

        def one(i, _, piece=piece, ref=ref):
            ex, ey = place_of(piece, i, odd_lane, odd_band)
            put(ref[i], ex, ey, STARTS[piece] + i, False)
            return 0

        lax.fori_loop(0, COUNTS[piece], one, 0)
    build_rows(near_ref, source, target, (w0, w1), inv_ref, 0)


def build_second(near_ref, source, target, w2, w3, inv_ref):
    build_rows(near_ref, source, target, (w2, w3), inv_ref, BX // 2)


def column(row_ref):
    n = row_ref.shape[1]
    shape = (n, n)
    same = lax.broadcasted_iota(i32, shape, 0) == lax.broadcasted_iota(i32, shape, 1)
    return jnp.sum(jnp.where(same, row_ref[...], 0.0), axis=1, keepdims=True)


def react(mixture, kelvin, factor, onset):
    half = mixture.shape[0] // 2
    u = mixture[:half]
    v = mixture[half:]
    speed = factor * jnp.exp(-onset / kelvin)
    reacted = speed * u * v / (1.0 + speed * (u + v))
    return jnp.concatenate([u - reacted, v - reacted], axis=0).astype(bf16)


def mix(near_ref, species, gathered, w, b):
    neighbours = near_ref.shape[0] // (BX * BY)
    parts = species.shape[2]
    for k in range(neighbours):
        q = near_ref[b * neighbours + k]
        gathered[:, k * parts : (k + 1) * parts] = species[q]
    return jnp.dot(gathered[...], w, preferred_element_type=f32)


def join(pieces, species):
    for start, count, ref in zip(STARTS, COUNTS, pieces):
        species[pl.ds(start, count)] = ref[...]


def inverse_of(inv_refs, g, c):
    half = BX // 2
    return inv_refs[g // half][pl.ds((g % half) * BY + c, 1)]


def step_columns(near_ref, species, gathered, w_refs, inv_refs, consts, low, out_ref):
    kelvin_ref, factor_ref, onset_ref = consts
    factor, onset = column(factor_ref), column(onset_ref)
    for g, w_ref in enumerate(w_refs):

        def one(i, _, g=g, w_ref=w_ref):
            c = low + i
            b = g * BY + c
            mixed = mix(near_ref, species, gathered, w_ref[c], b)
            mixed = mixed * inverse_of(inv_refs, g, c)
            out_ref[g * HALO + i] = react(mixed, kelvin_ref[pl.ds(b, 1)], factor, onset)
            return 0

        lax.fori_loop(0, HALO, one, 0)


def step_b(near_ref, meta_ref, p0, p1, p2, p3, p4, p5, w0, w1, w2, w3, i0, i1, t, a, o, out, species, gathered):
    join((p0, p1, p2, p3, p4, p5), species)
    low = jnp.where(meta_ref[4] == 1, BY - HALO, 0)
    step_columns(near_ref, species, gathered, (w0, w1, w2, w3), (i0, i1), (t, a, o), low, out)


def step_a(near_ref, meta_ref, species, w0, w1, w2, w3, i0, i1, t, a, o, out, gathered):
    low = jnp.where(meta_ref[4] == 1, 0, BY - HALO)
    step_columns(near_ref, species, gathered, (w0, w1, w2, w3), (i0, i1), (t, a, o), low, out)


def last_step(near_ref, row_ref, p0, p1, p2, p3, p4, p5, w0, w1, w2, w3, i0, i1, t, a, o, out, species, gathered):
    join((p0, p1, p2, p3, p4, p5), species)
    if out.shape[0] > BX * BY:
        out[...] = jnp.zeros_like(out)
    factor, onset = column(a), column(o)
    for g, w_ref in enumerate((w0, w1, w2, w3)):

        def one(c, _, g=g, w_ref=w_ref):
            b = g * BY + c
            mixed = mix(near_ref, species, gathered, w_ref[c], b)
            mixed = mixed * inverse_of((i0, i1), g, c)
            out[row_ref[b]] = react(mixed, t[pl.ds(b, 1)], factor, onset)
            return 0

        lax.fori_loop(0, BY, one, 0)


VM = pl.BlockSpec(memory_space=pltpu.VMEM)
SM = pl.BlockSpec(memory_space=pltpu.SMEM)


def call(kernel, operands, scalars, outs, scratch, flops):
    single = not isinstance(outs, (list, tuple))
    return pl.pallas_call(
        kernel,
        out_shape=outs,
        in_specs=[SM] * scalars + [VM] * (len(operands) - scalars),
        out_specs=VM if single else [SM if o.dtype == i32 else VM for o in outs],
        scratch_shapes=scratch,
        compiler_params=pltpu.CompilerParams(vmem_limit_bytes=8 << 20),
        cost_estimate=pl.CostEstimate(
            flops=flops, bytes_accessed=1 << 20, transcendentals=0
        ),
    )(*operands)


def body(
    solute_load,
    walker_displacement,
    local_kelvin,
    couple_kinetic_factor,
    arrhenius_onset,
    adjacent_cell_keys,
    downstream_zone,
):
    lane_count = lax.axis_size("gy")
    bins, kinds, parts = solute_load.shape
    neighbours = adjacent_cell_keys.shape[1]
    band, lane = lax.axis_index("gx"), lax.axis_index("gy")
    odd_band, odd_lane = band % 2, lane % 2

    meta = jnp.stack(
        [
            band * BX,
            lane * BY,
            jnp.int32(lax.axis_size("gx") * BX),
            jnp.int32(lane_count * BY),
            odd_lane,
            odd_band,
        ]
    ).astype(i32)
    like = lambda x, n: pltpu.VMEM((n,) + x.shape[1:], x.dtype)
    pos_a, pos_b, own_a, own_b, row = call(
        split,
        (meta, downstream_zone, walker_displacement, solute_load),
        2,
        [like(walker_displacement, SIDE)] * 2
        + [like(solute_load, SIDE)] * 2
        + [jax.ShapeDtypeStruct((bins,), i32)],
        [pltpu.SMEM((lane_count,), i32)],
        1 << 20,
    )

    def rows(pieces):
        by_a, by_b = call(pack, (meta,) + pieces, 1, [like(pieces[0], BAND)] * 2, [], 1 << 20)
        return swap(by_a, by_b, "gx")

    pos_sides = swap(pos_a, pos_b, "gy")
    pos_bands = rows((pos_a, pos_b) + pos_sides)
    own = (own_a, own_b)
    sides = swap(own_a, own_b, "gy")
    bands = rows(own + sides)

    ids = jnp.arange(bins, dtype=i32)
    near = slot_of(
        (ids // BY)[:, None] + adjacent_cell_keys // WIDTH - HALO,
        (ids % BY)[:, None] + adjacent_cell_keys % WIDTH - HALO,
        odd_lane,
        odd_band,
    ).reshape(-1)
    consts = (local_kelvin, couple_kinetic_factor[None], arrhenius_onset[None])

    w_row = pltpu.VMEM((BY, neighbours * parts, parts), bf16)
    inv_half = pltpu.VMEM((bins // 2, parts), f32)
    half = pltpu.VMEM((SIDE, kinds, parts), bf16)
    gathered = pltpu.VMEM((kinds, neighbours * parts), bf16)
    all_species = pltpu.VMEM((EXT, kinds, parts), bf16)
    work = 2 * bins * neighbours * parts * parts * 128
    w0, w1, inv0, source, target = call(
        build_first,
        (near, meta, walker_displacement) + pos_sides + pos_bands,
        2,
        [
            w_row,
            w_row,
            inv_half,
            pltpu.VMEM((EXT, parts, FEATURES), bf16),
            pltpu.VMEM((bins, FEATURES, parts), bf16),
        ],
        [],
        work,
    )
    w2, w3, inv1 = call(build_second, (near, source, target), 1, [w_row, w_row, inv_half], [], work)
    built = (w0, w1, w2, w3, inv0, inv1) + consts
    by_b, species = call(
        step_b,
        (near, meta) + own + sides + bands + built,
        2,
        [half, all_species],
        [gathered],
        work // 2,
    )
    by_a = call(step_a, (near, meta, species) + built, 2, half, [gathered], work // 2)

    own = (by_a, by_b)
    sides = swap(by_a, by_b, "gy")
    bands = rows(own + sides)
    packed = call(
        last_step,
        (near, row) + own + sides + bands + built,
        2,
        jax.ShapeDtypeStruct((lane_count * CAP, kinds, parts), bf16),
        [all_species, gathered],
        work,
    )
    return lax.all_to_all(packed, "gy", split_axis=0, concat_axis=0, tiled=True)


def solution(mesh):
    in_specs = (
        P(("gx", "gy"), None, None),
        P(("gx", "gy"), None, None),
        P(("gx", "gy"), None),
        P(),
        P(),
        P(("gx", "gy"), None),
        P(("gx", "gy"), None),
    )
    out_specs = P(("gx", "gy"), None, None)
    return jax.shard_map(body, mesh=mesh, in_specs=in_specs, out_specs=out_specs, check_vma=False)
```

```python
import math

import jax
import jax.numpy as jnp
from jax import lax
from jax.experimental import pallas as pl
from jax.experimental.pallas import tpu as pltpu
from jax.sharding import PartitionSpec as P


BX = 4
BY = 4
CAP = 2
HALO = 2
WIDTH = 2 * HALO + 1

inverse_width = 4.0
SCALE = math.sqrt(inverse_width * math.log2(math.e))
FAR = -1e30
FEATURES = 48

f32 = jnp.float32
bf16 = jnp.bfloat16
i32 = jnp.int32

SIDE = BX * HALO
QUAD = HALO * HALO
BAND = 4 * QUAD
EXT = 4 * SIDE + 2 * BAND
COUNTS = (SIDE, SIDE, SIDE, SIDE, BAND, BAND)
UNROLL = QUAD * HALO
STARTS = (0, SIDE, 2 * SIDE, 3 * SIDE, 4 * SIDE, 4 * SIDE + BAND)


def swaps(count):
    def both(first):
        out = []
        for i in range(first, count - 1, 2):
            out += [(i, i + 1), (i + 1, i)]
        return out

    return both(0), both(1)


def slot_of(ex, ey, odd_lane, odd_band):
    low = ey < BY // 2
    by_a = low == (odd_lane == 1)
    own = (ey >= 0) & (ey < BY)
    piece = jnp.where(by_a, 0, 1) + jnp.where(own, 0, 2)
    column = (ey + HALO) % HALO
    inner = piece * SIDE + ex * HALO + column
    from_a = (ex < 0) == (odd_band == 1)
    row = jnp.where(ex < 0, ex + HALO, ex - BX)
    outer = jnp.where(from_a, STARTS[4], STARTS[5]) + piece * QUAD + row * HALO + column
    return jnp.where((ex >= 0) & (ex < BX), inner, outer)


def place_of(piece, i, odd_lane, odd_band):
    if piece < 4:
        part, ex = piece, i // HALO
    else:
        part, row = i // QUAD, i % QUAD // HALO
        up = (odd_band == 1) if piece == 4 else (odd_band == 0)
        ex = jnp.where(up, row - HALO, row + BX)
    by_a = part % 2 == 0
    low = (by_a == (odd_lane == 1)) if not isinstance(by_a, bool) else (odd_lane == int(by_a))
    outside = part >= 2
    base = jnp.where(low, jnp.where(outside, -HALO, 0), jnp.where(outside, BY, BY - HALO))
    return ex, base + i % HALO


def split(meta_ref, x, pos, a, b, pos_a, pos_b, sem):
    low_a = jnp.where(meta_ref[4] == 1, 0, BY - HALO)
    lows = (low_a, BY - HALO - low_a)
    copies = []
    for m, (out, low) in enumerate(zip((a, b), lows)):
        for r in range(BX):
            source = x.at[pl.ds(r * BY + low, HALO)]
            target = out.at[pl.ds(r * HALO, HALO)]
            copies.append(pltpu.make_async_copy(source, target, sem.at[m, r]))
    for copy in copies:
        copy.start()
    for out, low in zip((pos_a, pos_b), lows):
        for r in range(BX):
            for i in range(HALO):
                for c in range(pos.shape[0]):
                    out[r * HALO + i, c : c + 1] = pos[c, pl.ds(r * BY + low + i, 1)]
    for copy in copies:
        copy.wait()


def pack(meta_ref, *refs):
    pieces, (out_a, out_b) = refs[:-2], refs[-2:]
    size = BX * HALO
    from_a = jnp.where(meta_ref[5] == 1, 0, size - QUAD)
    for n, x in enumerate(pieces):
        out_a[pl.ds(n * QUAD, QUAD)] = x[pl.ds(from_a, QUAD)]
        out_b[pl.ds(n * QUAD, QUAD)] = x[pl.ds(size - QUAD - from_a, QUAD)]


def swap(by_a, by_b, axis):
    pairs_a, pairs_b = swaps(lax.axis_size(axis))
    from_b = lax.ppermute(by_b, axis, pairs_b)
    from_a = lax.ppermute(by_a, axis, pairs_a)
    return from_a, from_b


def three_parts(x):
    high = x.astype(bf16).astype(f32)
    rest = x - high
    middle = rest.astype(bf16).astype(f32)
    return high, middle, rest - middle


def coordinates(pos, ex, ey):
    row = lax.broadcasted_iota(i32, (8, pos.shape[-1]), 0)
    padded = jnp.concatenate([pos, jnp.zeros((5, pos.shape[-1]), f32)], axis=0)
    middle = jnp.where(
        row == 0,
        ex.astype(f32) - (BX - 1) / 2,
        jnp.where(row == 1, ey.astype(f32) - (BY - 1) / 2, 0.0),
    )
    return (padded + middle) * SCALE, row


def features(pos, ex, ey, inside, as_target):
    x, row = coordinates(pos, ex, ey)
    norm = jnp.sum(x * x, axis=0, keepdims=True)
    high, middle, low = three_parts(x)
    nh, nm, nl = three_parts(norm)
    last = row == 3
    pick = lambda a, b: jnp.where(last, a, b)
    source = (
        pick(jnp.where(inside, -nh, FAR), high),
        pick(-nm, high),
        pick(-nl, middle),
        pick(1.0, high),
        pick(1.0, low),
        pick(1.0, middle),
    )
    source = jnp.concatenate(source, axis=0).astype(bf16).T
    if not as_target:
        return source, None
    high, middle, low = 2.0 * high, 2.0 * middle, 2.0 * low
    target = (
        pick(1.0, high),
        pick(1.0, middle),
        pick(1.0, high),
        pick(-nh, low),
        pick(-nm, high),
        pick(-nl, middle),
    )
    return source, jnp.concatenate(target, axis=0).astype(bf16)


def build_rows(near_ref, source, target, w_refs, inv_ref, first_row):
    parts = source.shape[1]
    neighbours = near_ref.shape[0] // (BX * BY)
    for g, w_ref in enumerate(w_refs):

        def one(c, _, g=g, w_ref=w_ref):
            b = (first_row + g) * BY + c
            f = target[b]
            total = jnp.zeros((8, parts), f32)
            for k in range(neighbours):
                q = near_ref[b * neighbours + k]
                w = jnp.exp2(jnp.dot(source[q], f, preferred_element_type=f32))
                total = total + w.reshape(parts // 8, 8, parts).sum(0)
                w_ref[c, pl.ds(k * parts, parts)] = w.astype(bf16)
            inv_ref[pl.ds(g * BY + c, 1)] = 1.0 / jnp.sum(total, axis=0, keepdims=True)
            return 0

        lax.fori_loop(0, BY, one, 0)


def build_first(
    near_ref, meta_ref, zone_ref, o0, o1, c0, c1, r0, r1, w0, w1, inv_ref, source, target, row_ref, taken
):
    odd_lane, odd_band = meta_ref[4], meta_ref[5]
    for piece, ref in enumerate((o0, o1, c0, c1, r0, r1)):

        def some(j, _, piece=piece, ref=ref):
            for n in range(UNROLL):
                i = j * UNROLL + n
                ex, ey = place_of(piece, i, odd_lane, odd_band)
                gx = meta_ref[0] + ex
                gy = meta_ref[1] + ey
                inside = (gx >= 0) & (gx < meta_ref[2]) & (gy >= 0) & (gy < meta_ref[3])
                s, t = features(ref[i], ex, ey, inside, piece < 2)
                source[STARTS[piece] + i] = s
                if piece < 2:
                    target[ex * BY + ey] = t
            return 0

        lax.fori_loop(0, COUNTS[piece] // UNROLL, some, 0)
    for z in range(taken.shape[0]):
        taken[z] = 0

    def place(b, _):
        zone = zone_ref[0, b]
        order = taken[zone]
        taken[zone] = order + 1
        row_ref[b] = zone * CAP + order
        return 0

    lax.fori_loop(0, BX * BY, place, 0)
    build_rows(near_ref, source, target, (w0, w1), inv_ref, 0)


def build_second(near_ref, source, target, w2, w3, inv_ref):
    build_rows(near_ref, source, target, (w2, w3), inv_ref, BX // 2)


def column(row_ref):
    n = row_ref.shape[1]
    shape = (n, n)
    same = lax.broadcasted_iota(i32, shape, 0) == lax.broadcasted_iota(i32, shape, 1)
    return jnp.sum(jnp.where(same, row_ref[...], 0.0), axis=1, keepdims=True)


def react(mixture, kelvin, factor, onset):
    half = mixture.shape[0] // 2
    u = mixture[:half]
    v = mixture[half:]
    speed = factor * jnp.exp(-onset / kelvin)
    reacted = speed * u * v / (1.0 + speed * (u + v))
    return jnp.concatenate([u - reacted, v - reacted], axis=0).astype(bf16)


def mix(near_ref, species, gathered, w, b):
    neighbours = near_ref.shape[0] // (BX * BY)
    parts = species.shape[2]
    for k in range(neighbours):
        q = near_ref[b * neighbours + k]
        gathered[:, k * parts : (k + 1) * parts] = species[q]
    return jnp.dot(gathered[...], w, preferred_element_type=f32)


def join(pieces, species):
    start = 0
    for ref in pieces:
        species[pl.ds(start, ref.shape[0])] = ref[...]
        start += ref.shape[0]


def inverse_of(inv_refs, g, c):
    half = BX // 2
    return inv_refs[g // half][pl.ds((g % half) * BY + c, 1)]


def step_columns(near_ref, species, gathered, w_refs, inv_refs, consts, low, out_ref):
    kelvin_ref, factor_ref, onset_ref = consts
    factor, onset = column(factor_ref), column(onset_ref)
    for g, w_ref in enumerate(w_refs):

        def one(i, _, g=g, w_ref=w_ref):
            c = low + i
            b = g * BY + c
            mixed = mix(near_ref, species, gathered, w_ref[c], b)
            mixed = mixed * inverse_of(inv_refs, g, c)
            out_ref[g * HALO + i] = react(mixed, kelvin_ref[pl.ds(b, 1)], factor, onset)
            return 0

        lax.fori_loop(0, HALO, one, 0)


def step_b(near_ref, meta_ref, p0, p1, p2, p3, p4, p5, w0, w1, w2, w3, i0, i1, t, a, o, out, species, gathered):
    join((p0, p1, p2, p3, p4, p5), species)
    low = jnp.where(meta_ref[4] == 1, BY - HALO, 0)
    step_columns(near_ref, species, gathered, (w0, w1, w2, w3), (i0, i1), (t, a, o), low, out)


def step_a(near_ref, meta_ref, species, w0, w1, w2, w3, i0, i1, t, a, o, out, gathered):
    low = jnp.where(meta_ref[4] == 1, 0, BY - HALO)
    step_columns(near_ref, species, gathered, (w0, w1, w2, w3), (i0, i1), (t, a, o), low, out)


def last_step(near_ref, row_ref, p0, p1, p2, p3, p4, p5, p6, p7, w0, w1, w2, w3, i0, i1, t, a, o, out, species, gathered):
    join((p0, p1, p2, p3, p4, p5, p6, p7), species)
    if out.shape[0] > BX * BY:
        out[...] = jnp.zeros_like(out)
    factor, onset = column(a), column(o)
    for g, w_ref in enumerate((w0, w1, w2, w3)):

        def one(c, _, g=g, w_ref=w_ref):
            b = g * BY + c
            mixed = mix(near_ref, species, gathered, w_ref[c], b)
            mixed = mixed * inverse_of((i0, i1), g, c)
            out[row_ref[b]] = react(mixed, t[pl.ds(b, 1)], factor, onset)
            return 0

        lax.fori_loop(0, BY, one, 0)


VM = pl.BlockSpec(memory_space=pltpu.VMEM)
SM = pl.BlockSpec(memory_space=pltpu.SMEM)
HBM = pl.BlockSpec(memory_space=pltpu.HBM)


def call(kernel, operands, scalars, outs, scratch, flops):
    single = not isinstance(outs, (list, tuple))
    return pl.pallas_call(
        kernel,
        out_shape=outs,
        in_specs=[SM] * scalars + [VM] * (len(operands) - scalars),
        out_specs=VM if single else [SM if o.dtype == i32 else VM for o in outs],
        scratch_shapes=scratch,
        compiler_params=pltpu.CompilerParams(vmem_limit_bytes=8 << 20),
        cost_estimate=pl.CostEstimate(
            flops=flops, bytes_accessed=1 << 20, transcendentals=0
        ),
    )(*operands)


def body(
    solute_load,
    walker_displacement,
    local_kelvin,
    couple_kinetic_factor,
    arrhenius_onset,
    adjacent_cell_keys,
    downstream_zone,
):
    lane_count = lax.axis_size("gy")
    bins, kinds, parts = solute_load.shape
    neighbours = adjacent_cell_keys.shape[1]
    band, lane = lax.axis_index("gx"), lax.axis_index("gy")
    odd_band, odd_lane = band % 2, lane % 2

    meta = jnp.stack(
        [
            band * BX,
            lane * BY,
            jnp.int32(lax.axis_size("gx") * BX),
            jnp.int32(lane_count * BY),
            odd_lane,
            odd_band,
        ]
    ).astype(i32)
    like = lambda x, n: pltpu.VMEM((n,) + x.shape[1:], x.dtype)
    axes = walker_displacement.shape[1]
    own_a, own_b, pos_a, pos_b = pl.pallas_call(
        split,
        out_shape=[pltpu.VMEM((SIDE, kinds, parts), bf16)] * 2
        + [pltpu.VMEM((SIDE, axes, parts), f32)] * 2,
        in_specs=[SM, HBM, VM],
        out_specs=[VM] * 4,
        scratch_shapes=[pltpu.SemaphoreType.DMA((2, BX))],
        compiler_params=pltpu.CompilerParams(vmem_limit_bytes=8 << 20),
        name="split",
    )(
        meta,
        pltpu.with_memory_space_constraint(solute_load, pltpu.HBM),
        walker_displacement.transpose(1, 0, 2),
    )

    def rows(pieces):
        size = len(pieces) * QUAD
        by_a, by_b = call(pack, (meta,) + pieces, 1, [like(pieces[0], size)] * 2, [], 1 << 20)
        return swap(by_a, by_b, "gx")

    pos_sides = swap(pos_a, pos_b, "gy")
    pos_bands = rows((pos_a, pos_b) + pos_sides)
    own = (own_a, own_b)
    sides = swap(own_a, own_b, "gy")
    bands = rows(own + sides)

    ids = jnp.arange(bins, dtype=i32)
    near = slot_of(
        (ids // BY)[:, None] + adjacent_cell_keys // WIDTH - HALO,
        (ids % BY)[:, None] + adjacent_cell_keys % WIDTH - HALO,
        odd_lane,
        odd_band,
    ).reshape(-1)
    consts = (local_kelvin, couple_kinetic_factor[None], arrhenius_onset[None])

    w_row = pltpu.VMEM((BY, neighbours * parts, parts), bf16)
    inv_half = pltpu.VMEM((bins // 2, parts), f32)
    half = pltpu.VMEM((SIDE, kinds, parts), bf16)
    gathered = pltpu.VMEM((kinds, neighbours * parts), bf16)
    all_species = pltpu.VMEM((EXT, kinds, parts), bf16)
    work = 2 * bins * neighbours * parts * parts * 128
    w0, w1, inv0, source, target, row = call(
        build_first,
        (near, meta, downstream_zone.T, pos_a, pos_b) + pos_sides + pos_bands,
        3,
        [
            w_row,
            w_row,
            inv_half,
            pltpu.VMEM((EXT, parts, FEATURES), bf16),
            pltpu.VMEM((bins, FEATURES, parts), bf16),
            jax.ShapeDtypeStruct((bins,), i32),
        ],
        [pltpu.SMEM((lane_count,), i32)],
        work,
    )
    w2, w3, inv1 = call(build_second, (near, source, target), 1, [w_row, w_row, inv_half], [], work)
    built = (w0, w1, w2, w3, inv0, inv1) + consts
    by_b, species = call(
        step_b,
        (near, meta) + own + sides + bands + built,
        2,
        [half, all_species],
        [gathered],
        work // 2,
    )
    by_a = call(step_a, (near, meta, species) + built, 2, half, [gathered], work // 2)

    own = (by_a, by_b)
    sides = swap(by_a, by_b, "gy")
    own_bands = rows(own)
    corners = rows(sides)
    pieces = own + sides + (own_bands[0], corners[0], own_bands[1], corners[1])
    packed = call(
        last_step,
        (near, row) + pieces + built,
        2,
        jax.ShapeDtypeStruct((lane_count * CAP, kinds, parts), bf16),
        [all_species, gathered],
        work,
    )
    return lax.all_to_all(packed, "gy", split_axis=0, concat_axis=0, tiled=True)


def solution(mesh):
    in_specs = (
        P(("gx", "gy"), None, None),
        P(("gx", "gy"), None, None),
        P(("gx", "gy"), None),
        P(),
        P(),
        P(("gx", "gy"), None),
        P(("gx", "gy"), None),
    )
    out_specs = P(("gx", "gy"), None, None)
    return jax.shard_map(body, mesh=mesh, in_specs=in_specs, out_specs=out_specs, check_vma=False)
```

```python
import math

import jax
import jax.numpy as jnp
from jax import lax
from jax.experimental import pallas as pl
from jax.experimental.pallas import tpu as pltpu
from jax.sharding import PartitionSpec as P


BX = 4
BY = 4
CAP = 2
HALO = 2
WIDTH = 2 * HALO + 1

inverse_width = 4.0
SCALE = math.sqrt(inverse_width * math.log2(math.e))
FAR = -1e30
FEATURES = 48

f32 = jnp.float32
bf16 = jnp.bfloat16
i32 = jnp.int32

SIDE = BX * HALO
QUAD = HALO * HALO
BAND = 4 * QUAD
EXT = 4 * SIDE + 2 * BAND
COUNTS = (SIDE, SIDE, SIDE, SIDE, BAND, BAND)
UNROLL = QUAD * HALO
STARTS = (0, SIDE, 2 * SIDE, 3 * SIDE, 4 * SIDE, 4 * SIDE + BAND)


def swaps(axis):
    bands, lanes = lax.axis_size("gx"), lax.axis_size("gy")

    def partner(g, l, first):
        i, count = (l, lanes) if axis == "gy" else (g, bands)
        other = i + 1 if (i - first) % 2 == 0 else i - 1
        if 0 <= other < count:
            return (g, other) if axis == "gy" else (other, l)
        if axis == "gy":
            return (g ^ 1, l) if bands % 2 == 0 else None
        return (g, l ^ 2) if lanes % 4 == 0 else None

    out = []
    for first in range(2):
        pairs = []
        for g in range(bands):
            for l in range(lanes):
                to = partner(g, l, first)
                if to is not None:
                    pairs.append((g * lanes + l, to[0] * lanes + to[1]))
        out.append(pairs)
    return out


def slot_of(ex, ey, odd_lane, odd_band):
    low = ey < BY // 2
    by_a = low == (odd_lane == 1)
    own = (ey >= 0) & (ey < BY)
    piece = jnp.where(by_a, 0, 1) + jnp.where(own, 0, 2)
    column = (ey + HALO) % HALO
    inner = piece * SIDE + ex * HALO + column
    from_a = (ex < 0) == (odd_band == 1)
    row = jnp.where(ex < 0, ex + HALO, ex - BX)
    outer = jnp.where(from_a, STARTS[4], STARTS[5]) + piece * QUAD + row * HALO + column
    return jnp.where((ex >= 0) & (ex < BX), inner, outer)


def place_of(piece, i, odd_lane, odd_band):
    if piece < 4:
        part, ex = piece, i // HALO
    else:
        part, row = i // QUAD, i % QUAD // HALO
        up = (odd_band == 1) if piece == 4 else (odd_band == 0)
        ex = jnp.where(up, row - HALO, row + BX)
    by_a = part % 2 == 0
    low = (by_a == (odd_lane == 1)) if not isinstance(by_a, bool) else (odd_lane == int(by_a))
    outside = part >= 2
    base = jnp.where(low, jnp.where(outside, -HALO, 0), jnp.where(outside, BY, BY - HALO))
    return ex, base + i % HALO


def split(meta_ref, x, pos, a, b, pos_a, pos_b, sem):
    low_a = jnp.where(meta_ref[4] == 1, 0, BY - HALO)
    lows = (low_a, BY - HALO - low_a)
    copies = []
    for m, (out, low) in enumerate(zip((a, b), lows)):
        for r in range(BX):
            source = x.at[pl.ds(r * BY + low, HALO)]
            target = out.at[pl.ds(r * HALO, HALO)]
            copies.append(pltpu.make_async_copy(source, target, sem.at[m, r]))
    for copy in copies:
        copy.start()
    for out, low in zip((pos_a, pos_b), lows):
        for r in range(BX):
            for i in range(HALO):
                for c in range(pos.shape[0]):
                    out[r * HALO + i, c : c + 1] = pos[c, pl.ds(r * BY + low + i, 1)]
    for copy in copies:
        copy.wait()


def pack(meta_ref, *refs):
    pieces, (out_a, out_b) = refs[:-2], refs[-2:]
    size = BX * HALO
    from_a = jnp.where(meta_ref[5] == 1, 0, size - QUAD)
    for n, x in enumerate(pieces):
        out_a[pl.ds(n * QUAD, QUAD)] = x[pl.ds(from_a, QUAD)]
        out_b[pl.ds(n * QUAD, QUAD)] = x[pl.ds(size - QUAD - from_a, QUAD)]


def swap(by_a, by_b, axis):
    pairs_a, pairs_b = swaps(axis)
    axis = ("gx", "gy")
    from_b = lax.ppermute(by_b, axis, pairs_b)
    from_a = lax.ppermute(by_a, axis, pairs_a)
    return from_a, from_b


def three_parts(x):
    high = x.astype(bf16).astype(f32)
    rest = x - high
    middle = rest.astype(bf16).astype(f32)
    return high, middle, rest - middle


def coordinates(pos, ex, ey):
    row = lax.broadcasted_iota(i32, (8, pos.shape[-1]), 0)
    padded = jnp.concatenate([pos, jnp.zeros((5, pos.shape[-1]), f32)], axis=0)
    middle = jnp.where(
        row == 0,
        ex.astype(f32) - (BX - 1) / 2,
        jnp.where(row == 1, ey.astype(f32) - (BY - 1) / 2, 0.0),
    )
    return (padded + middle) * SCALE, row


def features(pos, ex, ey, inside, as_target):
    x, row = coordinates(pos, ex, ey)
    norm = jnp.sum(x * x, axis=0, keepdims=True)
    high, middle, low = three_parts(x)
    nh, nm, nl = three_parts(norm)
    last = row == 3
    pick = lambda a, b: jnp.where(last, a, b)
    source = (
        pick(jnp.where(inside, -nh, FAR), high),
        pick(-nm, high),
        pick(-nl, middle),
        pick(1.0, high),
        pick(1.0, low),
        pick(1.0, middle),
    )
    source = jnp.concatenate(source, axis=0).astype(bf16).T
    if not as_target:
        return source, None
    high, middle, low = 2.0 * high, 2.0 * middle, 2.0 * low
    target = (
        pick(1.0, high),
        pick(1.0, middle),
        pick(1.0, high),
        pick(-nh, low),
        pick(-nm, high),
        pick(-nl, middle),
    )
    return source, jnp.concatenate(target, axis=0).astype(bf16)


def neighbours_of(near_ref):
    return near_ref.shape[0] // (BX * BY) - 1


def build_rows(near_ref, source, target, w_refs, inv_ref, first_row):
    parts = source.shape[1]
    neighbours = neighbours_of(near_ref)
    for g, w_ref in enumerate(w_refs):

        def one(c, _, g=g, w_ref=w_ref):
            b = (first_row + g) * BY + c
            f = target[b]
            total = jnp.zeros((8, parts), f32)
            for k in range(neighbours):
                q = near_ref[b * neighbours + k]
                w = jnp.exp2(jnp.dot(source[q], f, preferred_element_type=f32))
                total = total + w.reshape(parts // 8, 8, parts).sum(0)
                w_ref[c, pl.ds(k * parts, parts)] = w.astype(bf16)
            inv_ref[pl.ds(g * BY + c, 1)] = 1.0 / jnp.sum(total, axis=0, keepdims=True)
            return 0

        lax.fori_loop(0, BY, one, 0)


def build_first(
    near_ref, meta_ref, o0, o1, c0, c1, r0, r1, w0, w1, inv_ref, source, target, row_ref, taken
):
    odd_lane, odd_band = meta_ref[4], meta_ref[5]
    for piece, ref in enumerate((o0, o1, c0, c1, r0, r1)):

        def some(j, _, piece=piece, ref=ref):
            for n in range(UNROLL):
                i = j * UNROLL + n
                ex, ey = place_of(piece, i, odd_lane, odd_band)
                gx = meta_ref[0] + ex
                gy = meta_ref[1] + ey
                inside = (gx >= 0) & (gx < meta_ref[2]) & (gy >= 0) & (gy < meta_ref[3])
                s, t = features(ref[i], ex, ey, inside, piece < 2)
                source[STARTS[piece] + i] = s
                if piece < 2:
                    target[ex * BY + ey] = t
            return 0

        lax.fori_loop(0, COUNTS[piece] // UNROLL, some, 0)
    for z in range(taken.shape[0]):
        taken[z] = 0

    def place(b, _):
        zone = near_ref[BX * BY * neighbours_of(near_ref) + b]
        order = taken[zone]
        taken[zone] = order + 1
        row_ref[b] = zone * CAP + order
        return 0

    lax.fori_loop(0, BX * BY, place, 0)
    build_rows(near_ref, source, target, (w0, w1), inv_ref, 0)


def build_second(near_ref, source, target, w2, w3, inv_ref):
    build_rows(near_ref, source, target, (w2, w3), inv_ref, BX // 2)


def column(row_ref):
    n = row_ref.shape[1]
    shape = (n, n)
    same = lax.broadcasted_iota(i32, shape, 0) == lax.broadcasted_iota(i32, shape, 1)
    return jnp.sum(jnp.where(same, row_ref[...], 0.0), axis=1, keepdims=True)


def react(mixture, kelvin, factor, onset):
    half = mixture.shape[0] // 2
    u = mixture[:half]
    v = mixture[half:]
    speed = factor * jnp.exp(-onset / kelvin)
    reacted = speed * u * v / (1.0 + speed * (u + v))
    return jnp.concatenate([u - reacted, v - reacted], axis=0).astype(bf16)


def mix(near_ref, species, gathered, w, b):
    neighbours = neighbours_of(near_ref)
    parts = species.shape[2]
    for k in range(neighbours):
        q = near_ref[b * neighbours + k]
        gathered[:, k * parts : (k + 1) * parts] = species[q]
    return jnp.dot(gathered[...], w, preferred_element_type=f32)


def join(pieces, species):
    start = 0
    for ref in pieces:
        species[pl.ds(start, ref.shape[0])] = ref[...]
        start += ref.shape[0]


def inverse_of(inv_refs, g, c):
    half = BX // 2
    return inv_refs[g // half][pl.ds((g % half) * BY + c, 1)]


def step_columns(near_ref, species, gathered, w_refs, inv_refs, consts, low, out_ref):
    kelvin_ref, factor_ref, onset_ref = consts
    factor, onset = column(factor_ref), column(onset_ref)
    for g, w_ref in enumerate(w_refs):

        def one(i, _, g=g, w_ref=w_ref):
            c = low + i
            b = g * BY + c
            mixed = mix(near_ref, species, gathered, w_ref[c], b)
            mixed = mixed * inverse_of(inv_refs, g, c)
            out_ref[g * HALO + i] = react(mixed, kelvin_ref[pl.ds(b, 1)], factor, onset)
            return 0

        lax.fori_loop(0, HALO, one, 0)


def step_b(near_ref, meta_ref, p0, p1, p2, p3, p4, p5, w0, w1, w2, w3, i0, i1, t, a, o, out, species, gathered):
    join((p0, p1, p2, p3, p4, p5), species)
    low = jnp.where(meta_ref[4] == 1, BY - HALO, 0)
    step_columns(near_ref, species, gathered, (w0, w1, w2, w3), (i0, i1), (t, a, o), low, out)


def step_a(near_ref, meta_ref, species, w0, w1, w2, w3, i0, i1, t, a, o, out, gathered):
    low = jnp.where(meta_ref[4] == 1, 0, BY - HALO)
    step_columns(near_ref, species, gathered, (w0, w1, w2, w3), (i0, i1), (t, a, o), low, out)


def last_step(near_ref, row_ref, p0, p1, p2, p3, p4, p5, p6, p7, w0, w1, w2, w3, i0, i1, t, a, o, out, species, gathered):
    join((p0, p1, p2, p3, p4, p5, p6, p7), species)
    if out.shape[0] > BX * BY:
        out[...] = jnp.zeros_like(out)
    factor, onset = column(a), column(o)
    for g, w_ref in enumerate((w0, w1, w2, w3)):

        def one(c, _, g=g, w_ref=w_ref):
            b = g * BY + c
            mixed = mix(near_ref, species, gathered, w_ref[c], b)
            mixed = mixed * inverse_of((i0, i1), g, c)
            out[row_ref[b]] = react(mixed, t[pl.ds(b, 1)], factor, onset)
            return 0

        lax.fori_loop(0, BY, one, 0)


VM = pl.BlockSpec(memory_space=pltpu.VMEM)
SM = pl.BlockSpec(memory_space=pltpu.SMEM)
HBM = pl.BlockSpec(memory_space=pltpu.HBM)


def call(kernel, operands, scalars, outs, scratch, flops):
    single = not isinstance(outs, (list, tuple))
    return pl.pallas_call(
        kernel,
        out_shape=outs,
        in_specs=[SM] * scalars + [VM] * (len(operands) - scalars),
        out_specs=VM if single else [SM if o.dtype == i32 else VM for o in outs],
        scratch_shapes=scratch,
        compiler_params=pltpu.CompilerParams(vmem_limit_bytes=8 << 20),
        cost_estimate=pl.CostEstimate(
            flops=flops, bytes_accessed=1 << 20, transcendentals=0
        ),
    )(*operands)


def body(
    solute_load,
    walker_displacement,
    local_kelvin,
    couple_kinetic_factor,
    arrhenius_onset,
    adjacent_cell_keys,
    downstream_zone,
):
    lane_count = lax.axis_size("gy")
    bins, kinds, parts = solute_load.shape
    neighbours = adjacent_cell_keys.shape[1]
    band, lane = lax.axis_index("gx"), lax.axis_index("gy")
    odd_band, odd_lane = band % 2, lane % 2

    meta = jnp.stack(
        [
            band * BX,
            lane * BY,
            jnp.int32(lax.axis_size("gx") * BX),
            jnp.int32(lane_count * BY),
            odd_lane,
            odd_band,
        ]
    ).astype(i32)
    like = lambda x, n: pltpu.VMEM((n,) + x.shape[1:], x.dtype)
    axes = walker_displacement.shape[1]
    own_a, own_b, pos_a, pos_b = pl.pallas_call(
        split,
        out_shape=[pltpu.VMEM((SIDE, kinds, parts), bf16)] * 2
        + [pltpu.VMEM((SIDE, axes, parts), f32)] * 2,
        in_specs=[SM, HBM, VM],
        out_specs=[VM] * 4,
        scratch_shapes=[pltpu.SemaphoreType.DMA((2, BX))],
        compiler_params=pltpu.CompilerParams(vmem_limit_bytes=8 << 20),
        name="split",
    )(
        meta,
        pltpu.with_memory_space_constraint(solute_load, pltpu.HBM),
        walker_displacement.transpose(1, 0, 2),
    )

    def rows(pieces):
        size = len(pieces) * QUAD
        by_a, by_b = call(pack, (meta,) + pieces, 1, [like(pieces[0], size)] * 2, [], 1 << 20)
        return swap(by_a, by_b, "gx")

    pos_sides = swap(pos_a, pos_b, "gy")
    pos_bands = rows((pos_a, pos_b) + pos_sides)
    own = (own_a, own_b)
    sides = swap(own_a, own_b, "gy")
    bands = rows(own + sides)

    ids = jnp.arange(bins, dtype=i32)
    near = slot_of(
        (ids // BY)[:, None] + adjacent_cell_keys // WIDTH - HALO,
        (ids % BY)[:, None] + adjacent_cell_keys % WIDTH - HALO,
        odd_lane,
        odd_band,
    ).reshape(-1)
    near = jnp.concatenate([near, downstream_zone[:, 0]])
    consts = (local_kelvin, couple_kinetic_factor[None], arrhenius_onset[None])

    w_row = pltpu.VMEM((BY, neighbours * parts, parts), bf16)
    inv_half = pltpu.VMEM((bins // 2, parts), f32)
    half = pltpu.VMEM((SIDE, kinds, parts), bf16)
    gathered = pltpu.VMEM((kinds, neighbours * parts), bf16)
    all_species = pltpu.VMEM((EXT, kinds, parts), bf16)
    work = 2 * bins * neighbours * parts * parts * 128
    w0, w1, inv0, source, target, row = call(
        build_first,
        (near, meta, pos_a, pos_b) + pos_sides + pos_bands,
        2,
        [
            w_row,
            w_row,
            inv_half,
            pltpu.VMEM((EXT, parts, FEATURES), bf16),
            pltpu.VMEM((bins, FEATURES, parts), bf16),
            jax.ShapeDtypeStruct((bins,), i32),
        ],
        [pltpu.SMEM((lane_count,), i32)],
        work,
    )
    w2, w3, inv1 = call(build_second, (near, source, target), 1, [w_row, w_row, inv_half], [], work)
    built = (w0, w1, w2, w3, inv0, inv1) + consts
    by_b, species = call(
        step_b,
        (near, meta) + own + sides + bands + built,
        2,
        [half, all_species],
        [gathered],
        work // 2,
    )
    by_a = call(step_a, (near, meta, species) + built, 2, half, [gathered], work // 2)

    own = (by_a, by_b)
    sides = swap(by_a, by_b, "gy")
    own_bands = rows(own)
    corners = rows(sides)
    pieces = own + sides + (own_bands[0], corners[0], own_bands[1], corners[1])
    packed = call(
        last_step,
        (near, row) + pieces + built,
        2,
        jax.ShapeDtypeStruct((lane_count * CAP, kinds, parts), bf16),
        [all_species, gathered],
        work,
    )
    return lax.all_to_all(packed, "gy", split_axis=0, concat_axis=0, tiled=True)


def solution(mesh):
    in_specs = (
        P(("gx", "gy"), None, None),
        P(("gx", "gy"), None, None),
        P(("gx", "gy"), None),
        P(),
        P(),
        P(("gx", "gy"), None),
        P(("gx", "gy"), None),
    )
    out_specs = P(("gx", "gy"), None, None)
    return jax.shard_map(body, mesh=mesh, in_specs=in_specs, out_specs=out_specs, check_vma=False)
```

```python
import math

import jax
import jax.numpy as jnp
from jax import lax
from jax.experimental import pallas as pl
from jax.experimental.pallas import tpu as pltpu
from jax.sharding import PartitionSpec as P


BX = 4
BY = 4
CAP = 2
HALO = 2
WIDTH = 2 * HALO + 1

inverse_width = 4.0
SCALE = math.sqrt(inverse_width * math.log2(math.e))
FAR = -1e30
FEATURES = 48


f32 = jnp.float32
bf16 = jnp.bfloat16
i32 = jnp.int32

SIDE = BX * HALO
QUAD = HALO * HALO
BAND = 4 * QUAD
EXT = 4 * SIDE + 2 * BAND
COUNTS = (SIDE, SIDE, SIDE, SIDE, BAND, BAND)
UNROLL = QUAD * HALO
STARTS = (0, SIDE, 2 * SIDE, 3 * SIDE, 4 * SIDE, 4 * SIDE + BAND)


def swaps(axis):
    bands, lanes = lax.axis_size("gx"), lax.axis_size("gy")

    def partner(g, l, first):
        i, count = (l, lanes) if axis == "gy" else (g, bands)
        other = i + 1 if (i - first) % 2 == 0 else i - 1
        if 0 <= other < count:
            return (g, other) if axis == "gy" else (other, l)
        if axis == "gy":
            return (g ^ 1, l) if bands % 2 == 0 else None
        return (g, l ^ 2) if lanes % 4 == 0 else None

    out = []
    for first in range(2):
        pairs = []
        for g in range(bands):
            for l in range(lanes):
                to = partner(g, l, first)
                if to is not None:
                    pairs.append((g * lanes + l, to[0] * lanes + to[1]))
        out.append(pairs)
    return out


def slot_of(ex, ey, odd_lane, odd_band):
    low = ey < BY // 2
    by_a = low == (odd_lane == 1)
    own = (ey >= 0) & (ey < BY)
    piece = jnp.where(by_a, 0, 1) + jnp.where(own, 0, 2)
    column = (ey + HALO) % HALO
    inner = piece * SIDE + ex * HALO + column
    from_a = (ex < 0) == (odd_band == 1)
    row = jnp.where(ex < 0, ex + HALO, ex - BX)
    outer = jnp.where(from_a, STARTS[4], STARTS[5]) + piece * QUAD + row * HALO + column
    return jnp.where((ex >= 0) & (ex < BX), inner, outer)


def place_of(piece, i, odd_lane, odd_band):
    if piece < 4:
        part, ex = piece, i // HALO
    else:
        part, row = i // QUAD, i % QUAD // HALO
        up = (odd_band == 1) if piece == 4 else (odd_band == 0)
        ex = jnp.where(up, row - HALO, row + BX)
    by_a = part % 2 == 0
    low = (by_a == (odd_lane == 1)) if not isinstance(by_a, bool) else (odd_lane == int(by_a))
    outside = part >= 2
    base = jnp.where(low, jnp.where(outside, -HALO, 0), jnp.where(outside, BY, BY - HALO))
    return ex, base + i % HALO


def split(meta_ref, x, pos, a, b, pos_a, pos_b, sem):
    low_a = jnp.where(meta_ref[4] == 1, 0, BY - HALO)
    lows = (low_a, BY - HALO - low_a)
    copies = []
    for m, (out, low) in enumerate(zip((a, b), lows)):
        for r in range(BX):
            source = x.at[pl.ds(r * BY + low, HALO)]
            target = out.at[pl.ds(r * HALO, HALO)]
            copies.append(pltpu.make_async_copy(source, target, sem.at[m, r]))
    for copy in copies:
        copy.start()
    for out, low in zip((pos_a, pos_b), lows):
        for r in range(BX):
            for i in range(HALO):
                for c in range(pos.shape[0]):
                    out[r * HALO + i, c : c + 1] = pos[c, pl.ds(r * BY + low + i, 1)]
    for copy in copies:
        copy.wait()


def pack(meta_ref, *refs):
    pieces, (out_a, out_b) = refs[:-2], refs[-2:]
    size = BX * HALO
    from_a = jnp.where(meta_ref[5] == 1, 0, size - QUAD)
    for n, x in enumerate(pieces):
        out_a[pl.ds(n * QUAD, QUAD)] = x[pl.ds(from_a, QUAD)]
        out_b[pl.ds(n * QUAD, QUAD)] = x[pl.ds(size - QUAD - from_a, QUAD)]


def swap(by_a, by_b, axis):
    pairs_a, pairs_b = swaps(axis)
    axis = ("gx", "gy")
    from_b = lax.ppermute(by_b, axis, pairs_b)
    from_a = lax.ppermute(by_a, axis, pairs_a)
    return from_a, from_b


def three_parts(x):
    high = x.astype(bf16).astype(f32)
    rest = x - high
    middle = rest.astype(bf16).astype(f32)
    return high, middle, rest - middle


def coordinates(pos, ex, ey):
    row = lax.broadcasted_iota(i32, (8, pos.shape[-1]), 0)
    padded = jnp.concatenate([pos, jnp.zeros((5, pos.shape[-1]), f32)], axis=0)
    middle = jnp.where(
        row == 0,
        ex.astype(f32) - (BX - 1) / 2,
        jnp.where(row == 1, ey.astype(f32) - (BY - 1) / 2, 0.0),
    )
    return (padded + middle) * SCALE, row


def features(pos, ex, ey, inside, as_target):
    x, row = coordinates(pos, ex, ey)
    norm = jnp.sum(x * x, axis=0, keepdims=True)
    high, middle, low = three_parts(x)
    nh, nm, nl = three_parts(norm)
    last = row == 3
    pick = lambda a, b: jnp.where(last, a, b)
    source = (
        pick(jnp.where(inside, -nh, FAR), high),
        pick(-nm, high),
        pick(-nl, middle),
        pick(1.0, high),
        pick(1.0, low),
        pick(1.0, middle),
    )
    source = jnp.concatenate(source, axis=0).astype(bf16).T
    if not as_target:
        return source, None
    high, middle, low = 2.0 * high, 2.0 * middle, 2.0 * low
    target = (
        pick(1.0, high),
        pick(1.0, middle),
        pick(1.0, high),
        pick(-nh, low),
        pick(-nm, high),
        pick(-nl, middle),
    )
    return source, jnp.concatenate(target, axis=0).astype(bf16)


def neighbours_of(near_ref):
    return near_ref.shape[0] // (BX * BY) - 1


def build_rows(near_ref, source, target, w_refs, inv_ref, first_row):
    parts = source.shape[1]
    neighbours = neighbours_of(near_ref)
    for g, w_ref in enumerate(w_refs):

        def one(c, _, g=g, w_ref=w_ref):
            b = (first_row + g) * BY + c
            f = target[b]
            total = jnp.zeros((8, parts), f32)
            for k in range(neighbours):
                q = near_ref[b * neighbours + k]
                w = jnp.exp2(jnp.dot(source[q], f, preferred_element_type=f32))
                total = total + w.reshape(parts // 8, 8, parts).sum(0)
                w_ref[c, pl.ds(k * parts, parts)] = w.astype(bf16)
            inv_ref[pl.ds(g * BY + c, 1)] = 1.0 / jnp.sum(total, axis=0, keepdims=True)
            return 0

        lax.fori_loop(0, BY, one, 0)


def build_first(
    near_ref, meta_ref, o0, o1, c0, c1, r0, r1, w0, w1, inv_ref, source, target, row_ref, taken
):
    odd_lane, odd_band = meta_ref[4], meta_ref[5]
    for piece, ref in enumerate((o0, o1, c0, c1, r0, r1)):

        def some(j, _, piece=piece, ref=ref):
            for n in range(UNROLL):
                i = j * UNROLL + n
                ex, ey = place_of(piece, i, odd_lane, odd_band)
                gx = meta_ref[0] + ex
                gy = meta_ref[1] + ey
                inside = (gx >= 0) & (gx < meta_ref[2]) & (gy >= 0) & (gy < meta_ref[3])
                s, t = features(ref[i], ex, ey, inside, piece < 2)
                source[STARTS[piece] + i] = s
                if piece < 2:
                    target[ex * BY + ey] = t
            return 0

        lax.fori_loop(0, COUNTS[piece] // UNROLL, some, 0)
    for z in range(taken.shape[0]):
        taken[z] = 0

    def place(b, _):
        zone = near_ref[BX * BY * neighbours_of(near_ref) + b]
        order = taken[zone]
        taken[zone] = order + 1
        row_ref[b] = zone * CAP + order
        return 0

    lax.fori_loop(0, BX * BY, place, 0)
    build_rows(near_ref, source, target, (w0, w1), inv_ref, 0)


def build_second(near_ref, source, target, w2, w3, inv_ref):
    build_rows(near_ref, source, target, (w2, w3), inv_ref, BX // 2)


def column(row_ref):
    n = row_ref.shape[1]
    shape = (n, n)
    same = lax.broadcasted_iota(i32, shape, 0) == lax.broadcasted_iota(i32, shape, 1)
    return jnp.sum(jnp.where(same, row_ref[...], 0.0), axis=1, keepdims=True)


def react(mixture, kelvin, factor, onset):
    half = mixture.shape[0] // 2
    u = mixture[:half]
    v = mixture[half:]
    speed = factor * jnp.exp(-onset / kelvin)
    reacted = speed * u * v / (1.0 + speed * (u + v))
    return jnp.concatenate([u - reacted, v - reacted], axis=0).astype(bf16)


def mix(near_ref, species, gathered, w, b):
    neighbours = neighbours_of(near_ref)
    parts = species.shape[2]
    for k in range(neighbours):
        q = near_ref[b * neighbours + k]
        gathered[:, k * parts : (k + 1) * parts] = species[q]
    return jnp.dot(gathered[...], w, preferred_element_type=f32)


def join(pieces, species):
    start = 0
    for ref in pieces:
        species[pl.ds(start, ref.shape[0])] = ref[...]
        start += ref.shape[0]


def inverse_of(inv_refs, g, c):
    half = BX // 2
    return inv_refs[g // half][pl.ds((g % half) * BY + c, 1)]


def step_columns(near_ref, species, gathered, w_refs, inv_refs, consts, low, out_ref):
    kelvin_ref, factor_ref, onset_ref = consts
    factor, onset = column(factor_ref), column(onset_ref)
    for g, w_ref in enumerate(w_refs):

        def one(i, _, g=g, w_ref=w_ref):
            c = low + i
            b = g * BY + c
            mixed = mix(near_ref, species, gathered, w_ref[c], b)
            mixed = mixed * inverse_of(inv_refs, g, c)
            out_ref[g * HALO + i] = react(mixed, kelvin_ref[pl.ds(b, 1)], factor, onset)
            return 0

        lax.fori_loop(0, HALO, one, 0)


def step_b(near_ref, meta_ref, p0, p1, p2, p3, p4, p5, w0, w1, w2, w3, i0, i1, t, a, o, out, species, gathered):
    join((p0, p1, p2, p3, p4, p5), species)
    low = jnp.where(meta_ref[4] == 1, BY - HALO, 0)
    step_columns(near_ref, species, gathered, (w0, w1, w2, w3), (i0, i1), (t, a, o), low, out)


def step_a(near_ref, meta_ref, species, w0, w1, w2, w3, i0, i1, t, a, o, out, gathered):
    low = jnp.where(meta_ref[4] == 1, 0, BY - HALO)
    step_columns(near_ref, species, gathered, (w0, w1, w2, w3), (i0, i1), (t, a, o), low, out)


def deliver(tables, species, gathered, staged, w_refs, inv_refs, consts, first, outs):
    near_ref, meta_ref, row_ref = tables
    kelvin_ref, factor_ref, onset_ref = consts
    factor, onset = column(factor_ref), column(onset_ref)
    lane = meta_ref[1] // BY
    if 2 * staged.shape[0] > BX * BY:
        staged[...] = jnp.zeros_like(staged)
    for g, w_ref in enumerate(w_refs):

        def one(c, _, g=g, w_ref=w_ref):
            b = g * BY + c
            row = row_ref[b]
            way = ((row // CAP) ^ lane) - first

            @pl.when((way >= 0) & (way < len(outs)))
            def _():
                mixed = mix(near_ref, species, gathered, w_ref[c], b)
                mixed = mixed * inverse_of(inv_refs, g, c)
                moved = react(mixed, kelvin_ref[pl.ds(b, 1)], factor, onset)
                staged[way * CAP + row % CAP] = moved

            return 0

        lax.fori_loop(0, BY, one, 0)
    for i, out in enumerate(outs):
        out[...] = staged[i * CAP : (i + 1) * CAP]


def last_far(near_ref, meta_ref, row_ref, *refs):
    pieces, rest = refs[:8], refs[8:]
    w, inv, consts, rest = rest[:4], rest[4:6], rest[6:9], rest[9:]
    outs, (species, gathered, staged) = rest[:-3], rest[-3:]
    join(pieces, species)
    tables = (near_ref, meta_ref, row_ref)
    deliver(tables, species, gathered, staged, w, inv, consts, len(outs), outs)


def last_near(near_ref, meta_ref, row_ref, species, *refs):
    w, inv, consts, rest = refs[:4], refs[4:6], refs[6:9], refs[9:]
    outs, (gathered, staged) = rest[:-2], rest[-2:]
    tables = (near_ref, meta_ref, row_ref)
    deliver(tables, species, gathered, staged, w, inv, consts, 0, outs)


def place(meta_ref, *refs):
    blocks, (out, sem) = refs[:-2], refs[-2:]
    lane = meta_ref[1] // BY
    copies = [
        pltpu.make_async_copy(x, out.at[pl.ds((lane ^ way) * CAP, CAP)], sem.at[way])
        for way, x in enumerate(blocks)
    ]
    for copy in copies:
        copy.start()
    for copy in copies:
        copy.wait()


VM = pl.BlockSpec(memory_space=pltpu.VMEM)
SM = pl.BlockSpec(memory_space=pltpu.SMEM)
HBM = pl.BlockSpec(memory_space=pltpu.HBM)


def call(kernel, operands, scalars, outs, scratch, flops):
    single = not isinstance(outs, (list, tuple))
    return pl.pallas_call(
        kernel,
        out_shape=outs,
        in_specs=[SM] * scalars + [VM] * (len(operands) - scalars),
        out_specs=VM if single else [SM if o.dtype == i32 else VM for o in outs],
        scratch_shapes=scratch,
        compiler_params=pltpu.CompilerParams(vmem_limit_bytes=8 << 20),
        cost_estimate=pl.CostEstimate(
            flops=flops, bytes_accessed=1 << 20, transcendentals=0
        ),
    )(*operands)


def body(
    solute_load,
    walker_displacement,
    local_kelvin,
    couple_kinetic_factor,
    arrhenius_onset,
    adjacent_cell_keys,
    downstream_zone,
):
    lane_count = lax.axis_size("gy")
    bins, kinds, parts = solute_load.shape
    neighbours = adjacent_cell_keys.shape[1]
    band, lane = lax.axis_index("gx"), lax.axis_index("gy")
    odd_band, odd_lane = band % 2, lane % 2

    meta = jnp.stack(
        [
            band * BX,
            lane * BY,
            jnp.int32(lax.axis_size("gx") * BX),
            jnp.int32(lane_count * BY),
            odd_lane,
            odd_band,
        ]
    ).astype(i32)
    like = lambda x, n: pltpu.VMEM((n,) + x.shape[1:], x.dtype)
    axes = walker_displacement.shape[1]
    own_a, own_b, pos_a, pos_b = pl.pallas_call(
        split,
        out_shape=[pltpu.VMEM((SIDE, kinds, parts), bf16)] * 2
        + [pltpu.VMEM((SIDE, axes, parts), f32)] * 2,
        in_specs=[SM, HBM, VM],
        out_specs=[VM] * 4,
        scratch_shapes=[pltpu.SemaphoreType.DMA((2, BX))],
        compiler_params=pltpu.CompilerParams(vmem_limit_bytes=8 << 20),
        name="split",
    )(
        meta,
        pltpu.with_memory_space_constraint(solute_load, pltpu.HBM),
        walker_displacement.transpose(1, 0, 2),
    )

    def rows(pieces):
        size = len(pieces) * QUAD
        by_a, by_b = call(pack, (meta,) + pieces, 1, [like(pieces[0], size)] * 2, [], 1 << 20)
        return swap(by_a, by_b, "gx")

    pos_sides = swap(pos_a, pos_b, "gy")
    pos_bands = rows((pos_a, pos_b) + pos_sides)
    own = (own_a, own_b)
    sides = swap(own_a, own_b, "gy")
    bands = rows(own + sides)

    ids = jnp.arange(bins, dtype=i32)
    near = slot_of(
        (ids // BY)[:, None] + adjacent_cell_keys // WIDTH - HALO,
        (ids % BY)[:, None] + adjacent_cell_keys % WIDTH - HALO,
        odd_lane,
        odd_band,
    ).reshape(-1)
    near = jnp.concatenate([near, downstream_zone[:, 0]])
    consts = (local_kelvin, couple_kinetic_factor[None], arrhenius_onset[None])

    w_row = pltpu.VMEM((BY, neighbours * parts, parts), bf16)
    inv_half = pltpu.VMEM((bins // 2, parts), f32)
    half = pltpu.VMEM((SIDE, kinds, parts), bf16)
    gathered = pltpu.VMEM((kinds, neighbours * parts), bf16)
    all_species = pltpu.VMEM((EXT, kinds, parts), bf16)
    work = 2 * bins * neighbours * parts * parts * 128
    w0, w1, inv0, source, target, row = call(
        build_first,
        (near, meta, pos_a, pos_b) + pos_sides + pos_bands,
        2,
        [
            w_row,
            w_row,
            inv_half,
            pltpu.VMEM((EXT, parts, FEATURES), bf16),
            pltpu.VMEM((bins, FEATURES, parts), bf16),
            jax.ShapeDtypeStruct((bins,), i32),
        ],
        [pltpu.SMEM((lane_count,), i32)],
        work,
    )
    w2, w3, inv1 = call(build_second, (near, source, target), 1, [w_row, w_row, inv_half], [], work)
    built = (w0, w1, w2, w3, inv0, inv1) + consts
    by_b, species = call(
        step_b,
        (near, meta) + own + sides + bands + built,
        2,
        [half, all_species],
        [gathered],
        work // 2,
    )
    by_a = call(step_a, (near, meta, species) + built, 2, half, [gathered], work // 2)

    own = (by_a, by_b)
    sides = swap(by_a, by_b, "gy")
    own_bands = rows(own)
    corners = rows(sides)
    pieces = own + sides + (own_bands[0], corners[0], own_bands[1], corners[1])
    half_lanes = lane_count // 2
    block = pltpu.VMEM((CAP, kinds, parts), bf16)
    staged = pltpu.VMEM((half_lanes * CAP, kinds, parts), bf16)
    *far, species = call(
        last_far,
        (near, meta, row) + pieces + built,
        3,
        [block] * half_lanes + [all_species],
        [gathered, staged],
        work // 2,
    )
    close = call(
        last_near,
        (near, meta, row, species) + built,
        3,
        [block] * half_lanes,
        [gathered, staged],
        work // 2,
    )
    blocks = list(close) + far
    for way in list(range(half_lanes, lane_count)) + list(range(1, half_lanes)):
        pairs = [(l, l ^ way) for l in range(lane_count)]
        blocks[way] = lax.ppermute(blocks[way], "gy", pairs)
    return pl.pallas_call(
        place,
        out_shape=jax.ShapeDtypeStruct((lane_count * CAP, kinds, parts), bf16),
        in_specs=[SM] + [VM] * lane_count,
        out_specs=HBM,
        scratch_shapes=[pltpu.SemaphoreType.DMA((lane_count,))],
        compiler_params=pltpu.CompilerParams(vmem_limit_bytes=8 << 20),
        name="place",
    )(meta, *blocks)


def solution(mesh):
    in_specs = (
        P(("gx", "gy"), None, None),
        P(("gx", "gy"), None, None),
        P(("gx", "gy"), None),
        P(),
        P(),
        P(("gx", "gy"), None),
        P(("gx", "gy"), None),
    )
    out_specs = P(("gx", "gy"), None, None)
    return jax.shard_map(body, mesh=mesh, in_specs=in_specs, out_specs=out_specs, check_vma=False)
```

```python
import math

import jax
import jax.numpy as jnp
from jax import lax
from jax.experimental import pallas as pl
from jax.experimental.pallas import tpu as pltpu
from jax.sharding import PartitionSpec as P


BX = 4
BY = 4
CAP = 2
HALO = 2
WIDTH = 2 * HALO + 1

inverse_width = 4.0
SCALE = math.sqrt(inverse_width * math.log2(math.e))
FAR = -1e30
FEATURES = 48


f32 = jnp.float32
bf16 = jnp.bfloat16
i32 = jnp.int32

SIDE = BX * HALO
QUAD = HALO * HALO
BAND = 4 * QUAD
EXT = 4 * SIDE + 2 * BAND
COUNTS = (SIDE, SIDE, SIDE, SIDE, BAND, BAND)
UNROLL = QUAD * HALO
STARTS = (0, SIDE, 2 * SIDE, 3 * SIDE, 4 * SIDE, 4 * SIDE + BAND)


def swaps(axis):
    bands, lanes = lax.axis_size("gx"), lax.axis_size("gy")

    def partner(g, l, first):
        i, count = (l, lanes) if axis == "gy" else (g, bands)
        other = i + 1 if (i - first) % 2 == 0 else i - 1
        if 0 <= other < count:
            return (g, other) if axis == "gy" else (other, l)
        if axis == "gy":
            return (g ^ 1, l) if bands % 2 == 0 else None
        return (g, l ^ 2) if lanes % 4 == 0 else None

    out = []
    for first in range(2):
        pairs = []
        for g in range(bands):
            for l in range(lanes):
                to = partner(g, l, first)
                if to is not None:
                    pairs.append((g * lanes + l, to[0] * lanes + to[1]))
        out.append(pairs)
    return out


def slot_of(ex, ey, odd_lane, odd_band):
    low = ey < BY // 2
    by_a = low == (odd_lane == 1)
    own = (ey >= 0) & (ey < BY)
    piece = jnp.where(by_a, 0, 1) + jnp.where(own, 0, 2)
    column = (ey + HALO) % HALO
    inner = piece * SIDE + ex * HALO + column
    from_a = (ex < 0) == (odd_band == 1)
    row = jnp.where(ex < 0, ex + HALO, ex - BX)
    outer = jnp.where(from_a, STARTS[4], STARTS[5]) + piece * QUAD + row * HALO + column
    return jnp.where((ex >= 0) & (ex < BX), inner, outer)


def place_of(piece, i, odd_lane, odd_band):
    if piece < 4:
        part, ex = piece, i // HALO
    else:
        part, row = i // QUAD, i % QUAD // HALO
        up = (odd_band == 1) if piece == 4 else (odd_band == 0)
        ex = jnp.where(up, row - HALO, row + BX)
    by_a = part % 2 == 0
    low = (by_a == (odd_lane == 1)) if not isinstance(by_a, bool) else (odd_lane == int(by_a))
    outside = part >= 2
    base = jnp.where(low, jnp.where(outside, -HALO, 0), jnp.where(outside, BY, BY - HALO))
    return ex, base + i % HALO


def split(meta_ref, x, pos, a, b, pos_a, pos_b, sem):
    low_a = jnp.where(meta_ref[4] == 1, 0, BY - HALO)
    lows = (low_a, BY - HALO - low_a)
    copies = []
    for m, (out, low) in enumerate(zip((a, b), lows)):
        for r in range(BX):
            source = x.at[pl.ds(r * BY + low, HALO)]
            target = out.at[pl.ds(r * HALO, HALO)]
            copies.append(pltpu.make_async_copy(source, target, sem.at[m, r]))
    for copy in copies:
        copy.start()
    for out, low in zip((pos_a, pos_b), lows):
        for r in range(BX):
            for i in range(HALO):
                for c in range(pos.shape[0]):
                    out[r * HALO + i, c : c + 1] = pos[c, pl.ds(r * BY + low + i, 1)]
    for copy in copies:
        copy.wait()


def pack(meta_ref, *refs):
    pieces, (out_a, out_b) = refs[:-2], refs[-2:]
    size = BX * HALO
    from_a = jnp.where(meta_ref[5] == 1, 0, size - QUAD)
    for n, x in enumerate(pieces):
        out_a[pl.ds(n * QUAD, QUAD)] = x[pl.ds(from_a, QUAD)]
        out_b[pl.ds(n * QUAD, QUAD)] = x[pl.ds(size - QUAD - from_a, QUAD)]


def swap(by_a, by_b, axis):
    pairs_a, pairs_b = swaps(axis)
    axis = ("gx", "gy")
    from_b = lax.ppermute(by_b, axis, pairs_b)
    from_a = lax.ppermute(by_a, axis, pairs_a)
    return from_a, from_b


def three_parts(x):
    high = x.astype(bf16).astype(f32)
    rest = x - high
    middle = rest.astype(bf16).astype(f32)
    return high, middle, rest - middle


def coordinates(pos, ex, ey):
    row = lax.broadcasted_iota(i32, (8, pos.shape[-1]), 0)
    padded = jnp.concatenate([pos, jnp.zeros((5, pos.shape[-1]), f32)], axis=0)
    middle = jnp.where(
        row == 0,
        ex.astype(f32) - (BX - 1) / 2,
        jnp.where(row == 1, ey.astype(f32) - (BY - 1) / 2, 0.0),
    )
    return (padded + middle) * SCALE, row


def features(pos, ex, ey, inside, as_target):
    x, row = coordinates(pos, ex, ey)
    norm = jnp.sum(x * x, axis=0, keepdims=True)
    high, middle, low = three_parts(x)
    nh, nm, nl = three_parts(norm)
    last = row == 3
    pick = lambda a, b: jnp.where(last, a, b)
    source = (
        pick(jnp.where(inside, -nh, FAR), high),
        pick(-nm, high),
        pick(-nl, middle),
        pick(1.0, high),
        pick(1.0, low),
        pick(1.0, middle),
    )
    source = jnp.concatenate(source, axis=0).astype(bf16).T
    if not as_target:
        return source, None
    high, middle, low = 2.0 * high, 2.0 * middle, 2.0 * low
    target = (
        pick(1.0, high),
        pick(1.0, middle),
        pick(1.0, high),
        pick(-nh, low),
        pick(-nm, high),
        pick(-nl, middle),
    )
    return source, jnp.concatenate(target, axis=0).astype(bf16)


def neighbours_of(near_ref):
    return near_ref.shape[0] // (BX * BY) - 1


def build_rows(near_ref, source, target, w_refs, inv_ref, first_row):
    parts = source.shape[1]
    neighbours = neighbours_of(near_ref)
    for g, w_ref in enumerate(w_refs):

        def one(c, _, g=g, w_ref=w_ref):
            b = (first_row + g) * BY + c
            f = target[b]
            total = jnp.zeros((8, parts), f32)
            for k in range(neighbours):
                q = near_ref[b * neighbours + k]
                w = jnp.exp2(jnp.dot(source[q], f, preferred_element_type=f32))
                total = total + w.reshape(parts // 8, 8, parts).sum(0)
                w_ref[c, pl.ds(k * parts, parts)] = w.astype(bf16)
            inv_ref[pl.ds(g * BY + c, 1)] = 1.0 / jnp.sum(total, axis=0, keepdims=True)
            return 0

        lax.fori_loop(0, BY, one, 0)


def build_first(
    near_ref, meta_ref, o0, o1, c0, c1, r0, r1, w0, w1, inv_ref, source, target, row_ref, taken
):
    odd_lane, odd_band = meta_ref[4], meta_ref[5]
    for piece, ref in enumerate((o0, o1, c0, c1, r0, r1)):

        def some(j, _, piece=piece, ref=ref):
            for n in range(UNROLL):
                i = j * UNROLL + n
                ex, ey = place_of(piece, i, odd_lane, odd_band)
                gx = meta_ref[0] + ex
                gy = meta_ref[1] + ey
                inside = (gx >= 0) & (gx < meta_ref[2]) & (gy >= 0) & (gy < meta_ref[3])
                s, t = features(ref[i], ex, ey, inside, piece < 2)
                source[STARTS[piece] + i] = s
                if piece < 2:
                    target[ex * BY + ey] = t
            return 0

        lax.fori_loop(0, COUNTS[piece] // UNROLL, some, 0)
    for z in range(taken.shape[0]):
        taken[z] = 0

    def place(b, _):
        zone = near_ref[BX * BY * neighbours_of(near_ref) + b]
        order = taken[zone]
        taken[zone] = order + 1
        row_ref[b] = zone * CAP + order
        return 0

    lax.fori_loop(0, BX * BY, place, 0)
    build_rows(near_ref, source, target, (w0, w1), inv_ref, 0)


def build_second(near_ref, source, target, w2, w3, inv_ref):
    build_rows(near_ref, source, target, (w2, w3), inv_ref, BX // 2)


def column(row_ref):
    n = row_ref.shape[1]
    shape = (n, n)
    same = lax.broadcasted_iota(i32, shape, 0) == lax.broadcasted_iota(i32, shape, 1)
    return jnp.sum(jnp.where(same, row_ref[...], 0.0), axis=1, keepdims=True)


def react(mixture, kelvin, factor, onset):
    half = mixture.shape[0] // 2
    u = mixture[:half]
    v = mixture[half:]
    speed = factor * jnp.exp(-onset / kelvin)
    reacted = speed * u * v / (1.0 + speed * (u + v))
    return jnp.concatenate([u - reacted, v - reacted], axis=0).astype(bf16)


def mix(near_ref, species, gathered, w, b):
    neighbours = neighbours_of(near_ref)
    parts = species.shape[2]
    for k in range(neighbours):
        q = near_ref[b * neighbours + k]
        gathered[:, k * parts : (k + 1) * parts] = species[q]
    return jnp.dot(gathered[...], w, preferred_element_type=f32)


def join(pieces, species):
    start = 0
    for ref in pieces:
        species[pl.ds(start, ref.shape[0])] = ref[...]
        start += ref.shape[0]


def inverse_of(inv_refs, g, c):
    half = BX // 2
    return inv_refs[g // half][pl.ds((g % half) * BY + c, 1)]


def step_columns(near_ref, species, gathered, w_refs, inv_refs, consts, low, out_ref):
    kelvin_ref, factor_ref, onset_ref = consts
    factor, onset = column(factor_ref), column(onset_ref)
    for g, w_ref in enumerate(w_refs):

        for i in range(HALO):
            c = low + i
            b = g * BY + c
            mixed = mix(near_ref, species, gathered.at[i], w_ref[c], b)
            mixed = mixed * inverse_of(inv_refs, g, c)
            out_ref[g * HALO + i] = react(mixed, kelvin_ref[pl.ds(b, 1)], factor, onset)


def step_b(near_ref, meta_ref, p0, p1, p2, p3, p4, p5, w0, w1, w2, w3, i0, i1, t, a, o, out, species, gathered):
    join((p0, p1, p2, p3, p4, p5), species)
    low = jnp.where(meta_ref[4] == 1, BY - HALO, 0)
    step_columns(near_ref, species, gathered, (w0, w1, w2, w3), (i0, i1), (t, a, o), low, out)


def step_a(near_ref, meta_ref, species, w0, w1, w2, w3, i0, i1, t, a, o, out, gathered):
    low = jnp.where(meta_ref[4] == 1, 0, BY - HALO)
    step_columns(near_ref, species, gathered, (w0, w1, w2, w3), (i0, i1), (t, a, o), low, out)


def last_step(near_ref, meta_ref, row_ref, *refs):
    pieces, refs = refs[:8], refs[8:]
    w_refs, inv_refs, refs = refs[:4], refs[4:6], refs[6:]
    (kelvin_ref, factor_ref, onset_ref), refs = refs[:3], refs[3:]
    outs, (species, gathered, staged) = refs[:-3], refs[-3:]
    join(pieces, species)
    factor, onset = column(factor_ref), column(onset_ref)
    lane = meta_ref[1] // BY
    if staged.shape[0] > BX * BY:
        staged[...] = jnp.zeros_like(staged)
    for g, w_ref in enumerate(w_refs):

        def some(j, _, g=g, w_ref=w_ref):
            for i in range(HALO):
                c = j * HALO + i
                b = g * BY + c
                row = row_ref[b]
                mixed = mix(near_ref, species, gathered.at[i], w_ref[c], b)
                mixed = mixed * inverse_of(inv_refs, g, c)
                moved = react(mixed, kelvin_ref[pl.ds(b, 1)], factor, onset)
                staged[((row // CAP) ^ lane) * CAP + row % CAP] = moved
            return 0

        lax.fori_loop(0, BY // HALO, some, 0)
    for i, out in enumerate(outs):
        out[...] = staged[i * CAP : (i + 1) * CAP]


def place(meta_ref, *refs):
    blocks, (out, sem) = refs[:-2], refs[-2:]
    lane = meta_ref[1] // BY
    copies = [
        pltpu.make_async_copy(x, out.at[pl.ds((lane ^ way) * CAP, CAP)], sem.at[way])
        for way, x in enumerate(blocks)
    ]
    for copy in copies:
        copy.start()
    for copy in copies:
        copy.wait()


VM = pl.BlockSpec(memory_space=pltpu.VMEM)
SM = pl.BlockSpec(memory_space=pltpu.SMEM)
HBM = pl.BlockSpec(memory_space=pltpu.HBM)


def call(kernel, operands, scalars, outs, scratch, flops):
    single = not isinstance(outs, (list, tuple))
    return pl.pallas_call(
        kernel,
        out_shape=outs,
        in_specs=[SM] * scalars + [VM] * (len(operands) - scalars),
        out_specs=VM if single else [SM if o.dtype == i32 else VM for o in outs],
        scratch_shapes=scratch,
        compiler_params=pltpu.CompilerParams(vmem_limit_bytes=8 << 20),
        cost_estimate=pl.CostEstimate(
            flops=flops, bytes_accessed=1 << 20, transcendentals=0
        ),
    )(*operands)


def body(
    solute_load,
    walker_displacement,
    local_kelvin,
    couple_kinetic_factor,
    arrhenius_onset,
    adjacent_cell_keys,
    downstream_zone,
):
    lane_count = lax.axis_size("gy")
    bins, kinds, parts = solute_load.shape
    neighbours = adjacent_cell_keys.shape[1]
    band, lane = lax.axis_index("gx"), lax.axis_index("gy")
    odd_band, odd_lane = band % 2, lane % 2

    meta = jnp.stack(
        [
            band * BX,
            lane * BY,
            jnp.int32(lax.axis_size("gx") * BX),
            jnp.int32(lane_count * BY),
            odd_lane,
            odd_band,
        ]
    ).astype(i32)
    like = lambda x, n: pltpu.VMEM((n,) + x.shape[1:], x.dtype)
    axes = walker_displacement.shape[1]
    own_a, own_b, pos_a, pos_b = pl.pallas_call(
        split,
        out_shape=[pltpu.VMEM((SIDE, kinds, parts), bf16)] * 2
        + [pltpu.VMEM((SIDE, axes, parts), f32)] * 2,
        in_specs=[SM, HBM, VM],
        out_specs=[VM] * 4,
        scratch_shapes=[pltpu.SemaphoreType.DMA((2, BX))],
        compiler_params=pltpu.CompilerParams(vmem_limit_bytes=8 << 20),
        name="split",
    )(
        meta,
        pltpu.with_memory_space_constraint(solute_load, pltpu.HBM),
        walker_displacement.transpose(1, 0, 2),
    )

    def rows(pieces):
        size = len(pieces) * QUAD
        by_a, by_b = call(pack, (meta,) + pieces, 1, [like(pieces[0], size)] * 2, [], 1 << 20)
        return swap(by_a, by_b, "gx")

    pos_sides = swap(pos_a, pos_b, "gy")
    pos_bands = rows((pos_a, pos_b) + pos_sides)
    own = (own_a, own_b)
    sides = swap(own_a, own_b, "gy")
    bands = rows(own + sides)

    ids = jnp.arange(bins, dtype=i32)
    near = slot_of(
        (ids // BY)[:, None] + adjacent_cell_keys // WIDTH - HALO,
        (ids % BY)[:, None] + adjacent_cell_keys % WIDTH - HALO,
        odd_lane,
        odd_band,
    ).reshape(-1)
    near = jnp.concatenate([near, downstream_zone[:, 0]])
    consts = (local_kelvin, couple_kinetic_factor[None], arrhenius_onset[None])

    w_row = pltpu.VMEM((BY, neighbours * parts, parts), bf16)
    inv_half = pltpu.VMEM((bins // 2, parts), f32)
    half = pltpu.VMEM((SIDE, kinds, parts), bf16)
    gathered = pltpu.VMEM((HALO, kinds, neighbours * parts), bf16)
    all_species = pltpu.VMEM((EXT, kinds, parts), bf16)
    work = 2 * bins * neighbours * parts * parts * 128
    w0, w1, inv0, source, target, row = call(
        build_first,
        (near, meta, pos_a, pos_b) + pos_sides + pos_bands,
        2,
        [
            w_row,
            w_row,
            inv_half,
            pltpu.VMEM((EXT, parts, FEATURES), bf16),
            pltpu.VMEM((bins, FEATURES, parts), bf16),
            jax.ShapeDtypeStruct((bins,), i32),
        ],
        [pltpu.SMEM((lane_count,), i32)],
        work,
    )
    w2, w3, inv1 = call(build_second, (near, source, target), 1, [w_row, w_row, inv_half], [], work)
    built = (w0, w1, w2, w3, inv0, inv1) + consts
    by_b, species = call(
        step_b,
        (near, meta) + own + sides + bands + built,
        2,
        [half, all_species],
        [gathered],
        work // 2,
    )
    by_a = call(step_a, (near, meta, species) + built, 2, half, [gathered], work // 2)

    own = (by_a, by_b)
    sides = swap(by_a, by_b, "gy")
    own_bands = rows(own)
    corners = rows(sides)
    pieces = own + sides + (own_bands[0], corners[0], own_bands[1], corners[1])
    blocks = list(
        call(
            last_step,
            (near, meta, row) + pieces + built,
            3,
            [pltpu.VMEM((CAP, kinds, parts), bf16)] * lane_count,
            [all_species, gathered, pltpu.VMEM((lane_count * CAP, kinds, parts), bf16)],
            work,
        )
    )
    for way in range(lane_count - 1, 0, -1):
        pairs = [(l, l ^ way) for l in range(lane_count)]
        blocks[way] = lax.ppermute(blocks[way], "gy", pairs)
    return pl.pallas_call(
        place,
        out_shape=jax.ShapeDtypeStruct((lane_count * CAP, kinds, parts), bf16),
        in_specs=[SM] + [VM] * lane_count,
        out_specs=HBM,
        scratch_shapes=[pltpu.SemaphoreType.DMA((lane_count,))],
        compiler_params=pltpu.CompilerParams(vmem_limit_bytes=8 << 20),
        name="place",
    )(meta, *blocks)


def solution(mesh):
    in_specs = (
        P(("gx", "gy"), None, None),
        P(("gx", "gy"), None, None),
        P(("gx", "gy"), None),
        P(),
        P(),
        P(("gx", "gy"), None),
        P(("gx", "gy"), None),
    )
    out_specs = P(("gx", "gy"), None, None)
    return jax.shard_map(body, mesh=mesh, in_specs=in_specs, out_specs=out_specs, check_vma=False)
```

```python
import math

import jax
import jax.numpy as jnp
from jax import lax
from jax.experimental import pallas as pl
from jax.experimental.pallas import tpu as pltpu
from jax.sharding import PartitionSpec as P


BX = 4
BY = 4
CAP = 2
HALO = 2
WIDTH = 2 * HALO + 1

inverse_width = 4.0
SCALE = math.sqrt(inverse_width * math.log2(math.e))
FAR = -1e30
FEATURES = 48


f32 = jnp.float32
bf16 = jnp.bfloat16
i32 = jnp.int32

SIDE = BX * HALO
QUAD = HALO * HALO
BAND = 4 * QUAD
EXT = 4 * SIDE + 2 * BAND
COUNTS = (SIDE, SIDE, SIDE, SIDE, BAND, BAND)
UNROLL = QUAD * HALO
STARTS = (0, SIDE, 2 * SIDE, 3 * SIDE, 4 * SIDE, 4 * SIDE + BAND)


def swaps(axis):
    bands, lanes = lax.axis_size("gx"), lax.axis_size("gy")

    def partner(g, l, first):
        i, count = (l, lanes) if axis == "gy" else (g, bands)
        other = i + 1 if (i - first) % 2 == 0 else i - 1
        if 0 <= other < count:
            return (g, other) if axis == "gy" else (other, l)
        if axis == "gy":
            return (g ^ 1, l) if bands % 2 == 0 else None
        return (g, l ^ 2) if lanes % 4 == 0 else None

    out = []
    for first in range(2):
        pairs = []
        for g in range(bands):
            for l in range(lanes):
                to = partner(g, l, first)
                if to is not None:
                    pairs.append((g * lanes + l, to[0] * lanes + to[1]))
        out.append(pairs)
    return out


def slot_of(ex, ey, odd_lane, odd_band):
    low = ey < BY // 2
    by_a = low == (odd_lane == 1)
    own = (ey >= 0) & (ey < BY)
    piece = jnp.where(by_a, 0, 1) + jnp.where(own, 0, 2)
    column = (ey + HALO) % HALO
    inner = piece * SIDE + ex * HALO + column
    from_a = (ex < 0) == (odd_band == 1)
    row = jnp.where(ex < 0, ex + HALO, ex - BX)
    outer = jnp.where(from_a, STARTS[4], STARTS[5]) + piece * QUAD + row * HALO + column
    return jnp.where((ex >= 0) & (ex < BX), inner, outer)


def place_of(piece, i, odd_lane, odd_band):
    if piece < 4:
        part, ex = piece, i // HALO
    else:
        part, row = i // QUAD, i % QUAD // HALO
        up = (odd_band == 1) if piece == 4 else (odd_band == 0)
        ex = jnp.where(up, row - HALO, row + BX)
    by_a = part % 2 == 0
    low = (by_a == (odd_lane == 1)) if not isinstance(by_a, bool) else (odd_lane == int(by_a))
    outside = part >= 2
    base = jnp.where(low, jnp.where(outside, -HALO, 0), jnp.where(outside, BY, BY - HALO))
    return ex, base + i % HALO


def split(meta_ref, x, pos, a, b, pos_a, pos_b, sem):
    low_a = jnp.where(meta_ref[4] == 1, 0, BY - HALO)
    lows = (low_a, BY - HALO - low_a)
    copies = []
    for m, (out, low) in enumerate(zip((a, b), lows)):
        for r in range(BX):
            source = x.at[pl.ds(r * BY + low, HALO)]
            target = out.at[pl.ds(r * HALO, HALO)]
            copies.append(pltpu.make_async_copy(source, target, sem.at[m, r]))
    for copy in copies:
        copy.start()
    for out, low in zip((pos_a, pos_b), lows):
        for r in range(BX):
            for i in range(HALO):
                for c in range(pos.shape[0]):
                    out[r * HALO + i, c : c + 1] = pos[c, pl.ds(r * BY + low + i, 1)]
    for copy in copies:
        copy.wait()


def pack(meta_ref, *refs):
    pieces, (out_a, out_b) = refs[:-2], refs[-2:]
    size = BX * HALO
    from_a = jnp.where(meta_ref[5] == 1, 0, size - QUAD)
    for n, x in enumerate(pieces):
        out_a[pl.ds(n * QUAD, QUAD)] = x[pl.ds(from_a, QUAD)]
        out_b[pl.ds(n * QUAD, QUAD)] = x[pl.ds(size - QUAD - from_a, QUAD)]


def swap(by_a, by_b, axis):
    pairs_a, pairs_b = swaps(axis)
    axis = ("gx", "gy")
    from_b = lax.ppermute(by_b, axis, pairs_b)
    from_a = lax.ppermute(by_a, axis, pairs_a)
    return from_a, from_b


def three_parts(x):
    high = x.astype(bf16).astype(f32)
    rest = x - high
    middle = rest.astype(bf16).astype(f32)
    return high, middle, rest - middle


def coordinates(pos, ex, ey):
    row = lax.broadcasted_iota(i32, (8, pos.shape[-1]), 0)
    padded = jnp.concatenate([pos, jnp.zeros((5, pos.shape[-1]), f32)], axis=0)
    middle = jnp.where(
        row == 0,
        ex.astype(f32) - (BX - 1) / 2,
        jnp.where(row == 1, ey.astype(f32) - (BY - 1) / 2, 0.0),
    )
    return (padded + middle) * SCALE, row


def features(pos, ex, ey, inside, as_target):
    x, row = coordinates(pos, ex, ey)
    norm = jnp.sum(x * x, axis=0, keepdims=True)
    high, middle, low = three_parts(x)
    nh, nm, nl = three_parts(norm)
    last = row == 3
    pick = lambda a, b: jnp.where(last, a, b)
    source = (
        pick(jnp.where(inside, -nh, FAR), high),
        pick(-nm, high),
        pick(-nl, middle),
        pick(1.0, high),
        pick(1.0, low),
        pick(1.0, middle),
    )
    source = jnp.concatenate(source, axis=0).astype(bf16).T
    if not as_target:
        return source, None
    high, middle, low = 2.0 * high, 2.0 * middle, 2.0 * low
    target = (
        pick(1.0, high),
        pick(1.0, middle),
        pick(1.0, high),
        pick(-nh, low),
        pick(-nm, high),
        pick(-nl, middle),
    )
    return source, jnp.concatenate(target, axis=0).astype(bf16)


def neighbours_of(near_ref):
    return near_ref.shape[0] // (BX * BY) - 1


def build_rows(near_ref, source, target, w_refs, first_row):
    parts = source.shape[1]
    neighbours = neighbours_of(near_ref)
    for g, w_ref in enumerate(w_refs):

        def one(c, _, g=g, w_ref=w_ref):
            b = (first_row + g) * BY + c
            f = target[b]
            for k in range(neighbours):
                q = near_ref[b * neighbours + k]
                e = jnp.dot(source[q], f, preferred_element_type=f32)
                w_ref[c, pl.ds(k * parts, parts)] = jnp.exp2(e.astype(bf16))
            return 0

        lax.fori_loop(0, BY, one, 0)


def build_first(
    near_ref, meta_ref, o0, o1, c0, c1, r0, r1, w0, w1, source, target, row_ref, taken
):
    odd_lane, odd_band = meta_ref[4], meta_ref[5]
    for piece, ref in enumerate((o0, o1, c0, c1, r0, r1)):

        def some(j, _, piece=piece, ref=ref):
            for n in range(UNROLL):
                i = j * UNROLL + n
                ex, ey = place_of(piece, i, odd_lane, odd_band)
                gx = meta_ref[0] + ex
                gy = meta_ref[1] + ey
                inside = (gx >= 0) & (gx < meta_ref[2]) & (gy >= 0) & (gy < meta_ref[3])
                s, t = features(ref[i], ex, ey, inside, piece < 2)
                source[STARTS[piece] + i] = s
                if piece < 2:
                    target[ex * BY + ey] = t
            return 0

        lax.fori_loop(0, COUNTS[piece] // UNROLL, some, 0)
    for z in range(taken.shape[0]):
        taken[z] = 0

    def place(b, _):
        zone = near_ref[BX * BY * neighbours_of(near_ref) + b]
        order = taken[zone]
        taken[zone] = order + 1
        row_ref[b] = zone * CAP + order
        return 0

    lax.fori_loop(0, BX * BY, place, 0)
    build_rows(near_ref, source, target, (w0, w1), 0)


def build_second(near_ref, source, target, w2, w3):
    build_rows(near_ref, source, target, (w2, w3), BX // 2)


def column(row_ref):
    n = row_ref.shape[1]
    shape = (n, n)
    same = lax.broadcasted_iota(i32, shape, 0) == lax.broadcasted_iota(i32, shape, 1)
    return jnp.sum(jnp.where(same, row_ref[...], 0.0), axis=1, keepdims=True)


def react(mixture, kelvin, factor, onset):
    half = mixture.shape[0] // 2
    u = mixture[:half]
    v = mixture[half:]
    speed = factor * jnp.exp(-onset / kelvin)
    reacted = speed * u * v / (1.0 + speed * (u + v))
    return jnp.concatenate([u - reacted, v - reacted], axis=0).astype(bf16)


def mix(near_ref, species, gathered, w, b):
    neighbours = neighbours_of(near_ref)
    parts = species.shape[2]
    kinds = species.shape[1]
    for k in range(neighbours):
        q = near_ref[b * neighbours + k]
        gathered[:kinds, k * parts : (k + 1) * parts] = species[q]
    return jnp.dot(gathered[...], w, preferred_element_type=f32)


def join(pieces, species):
    start = 0
    for ref in pieces:
        species[pl.ds(start, ref.shape[0])] = ref[...]
        start += ref.shape[0]


def step_columns(near_ref, species, gathered, w_refs, consts, low, out_ref, inv_ref):
    kinds = species.shape[1]
    gathered[:, kinds:] = jnp.ones_like(gathered[:, kinds:])
    kelvin_ref, factor_ref, onset_ref = consts
    factor, onset = column(factor_ref), column(onset_ref)
    for g, w_ref in enumerate(w_refs):

        for i in range(HALO):
            c = low + i
            b = g * BY + c
            mixed = mix(near_ref, species, gathered.at[i], w_ref[c], b)
            inv = 1.0 / mixed[kinds : kinds + 1]
            inv_ref[pl.ds(g * HALO + i, 1)] = inv
            mixed = mixed[:kinds] * inv
            out_ref[g * HALO + i] = react(mixed, kelvin_ref[pl.ds(b, 1)], factor, onset)


def step_b(near_ref, meta_ref, *refs):
    pieces, w_refs, consts = refs[:6], refs[6:10], refs[10:13]
    out, inv_ref, species, gathered = refs[13:]
    join(pieces, species)
    low = jnp.where(meta_ref[4] == 1, BY - HALO, 0)
    step_columns(near_ref, species, gathered, w_refs, consts, low, out, inv_ref)


def step_a(near_ref, meta_ref, species, *refs):
    w_refs, consts = refs[:4], refs[4:7]
    out, inv_ref, gathered = refs[7:]
    low = jnp.where(meta_ref[4] == 1, 0, BY - HALO)
    step_columns(near_ref, species, gathered, w_refs, consts, low, out, inv_ref)


def last_step(near_ref, meta_ref, row_ref, *refs):
    pieces, refs = refs[:8], refs[8:]
    w_refs, (inv_a, inv_b), refs = refs[:4], refs[4:6], refs[6:]
    (kelvin_ref, factor_ref, onset_ref), refs = refs[:3], refs[3:]
    outs, (species, gathered, staged) = refs[:-3], refs[-3:]
    join(pieces, species)
    factor, onset = column(factor_ref), column(onset_ref)
    lane = meta_ref[1] // BY
    a_first = meta_ref[4] == 1
    if staged.shape[0] > BX * BY:
        staged[...] = jnp.zeros_like(staged)
    for g, w_ref in enumerate(w_refs):

        def some(j, _, g=g, w_ref=w_ref):
            by_a = (j == 0) == a_first
            for i in range(HALO):
                c = j * HALO + i
                at = pl.ds(g * HALO + i, 1)
                b = g * BY + c
                row = row_ref[b]
                mixed = mix(near_ref, species, gathered.at[i], w_ref[c], b)
                mixed = mixed * jnp.where(by_a, inv_a[at], inv_b[at])
                moved = react(mixed, kelvin_ref[pl.ds(b, 1)], factor, onset)
                staged[((row // CAP) ^ lane) * CAP + row % CAP] = moved
            return 0

        lax.fori_loop(0, BY // HALO, some, 0)
    for i, out in enumerate(outs):
        out[...] = staged[i * CAP : (i + 1) * CAP]


def place(meta_ref, *refs):
    blocks, (out, sem) = refs[:-2], refs[-2:]
    lane = meta_ref[1] // BY
    copies = [
        pltpu.make_async_copy(x, out.at[pl.ds((lane ^ way) * CAP, CAP)], sem.at[way])
        for way, x in enumerate(blocks)
    ]
    for copy in copies:
        copy.start()
    for copy in copies:
        copy.wait()


VM = pl.BlockSpec(memory_space=pltpu.VMEM)
SM = pl.BlockSpec(memory_space=pltpu.SMEM)
HBM = pl.BlockSpec(memory_space=pltpu.HBM)


def call(kernel, operands, scalars, outs, scratch, flops):
    single = not isinstance(outs, (list, tuple))
    return pl.pallas_call(
        kernel,
        out_shape=outs,
        in_specs=[SM] * scalars + [VM] * (len(operands) - scalars),
        out_specs=VM if single else [SM if o.dtype == i32 else VM for o in outs],
        scratch_shapes=scratch,
        compiler_params=pltpu.CompilerParams(vmem_limit_bytes=8 << 20),
        cost_estimate=pl.CostEstimate(
            flops=flops, bytes_accessed=1 << 20, transcendentals=0
        ),
    )(*operands)


def body(
    solute_load,
    walker_displacement,
    local_kelvin,
    couple_kinetic_factor,
    arrhenius_onset,
    adjacent_cell_keys,
    downstream_zone,
):
    lane_count = lax.axis_size("gy")
    bins, kinds, parts = solute_load.shape
    neighbours = adjacent_cell_keys.shape[1]
    band, lane = lax.axis_index("gx"), lax.axis_index("gy")
    odd_band, odd_lane = band % 2, lane % 2

    meta = jnp.stack(
        [
            band * BX,
            lane * BY,
            jnp.int32(lax.axis_size("gx") * BX),
            jnp.int32(lane_count * BY),
            odd_lane,
            odd_band,
        ]
    ).astype(i32)
    like = lambda x, n: pltpu.VMEM((n,) + x.shape[1:], x.dtype)
    axes = walker_displacement.shape[1]
    own_a, own_b, pos_a, pos_b = pl.pallas_call(
        split,
        out_shape=[pltpu.VMEM((SIDE, kinds, parts), bf16)] * 2
        + [pltpu.VMEM((SIDE, axes, parts), f32)] * 2,
        in_specs=[SM, HBM, VM],
        out_specs=[VM] * 4,
        scratch_shapes=[pltpu.SemaphoreType.DMA((2, BX))],
        compiler_params=pltpu.CompilerParams(vmem_limit_bytes=8 << 20),
        name="split",
    )(
        meta,
        pltpu.with_memory_space_constraint(solute_load, pltpu.HBM),
        walker_displacement.transpose(1, 0, 2),
    )

    def rows(pieces):
        size = len(pieces) * QUAD
        by_a, by_b = call(
            pack, (meta,) + pieces, 1, [like(pieces[0], size)] * 2, [], 1 << 20
        )
        return swap(by_a, by_b, "gx")

    pos_sides = swap(pos_a, pos_b, "gy")
    pos_bands = rows((pos_a, pos_b) + pos_sides)
    own = (own_a, own_b)
    sides = swap(own_a, own_b, "gy")
    bands = rows(own + sides)

    ids = jnp.arange(bins, dtype=i32)
    near = slot_of(
        (ids // BY)[:, None] + adjacent_cell_keys // WIDTH - HALO,
        (ids % BY)[:, None] + adjacent_cell_keys % WIDTH - HALO,
        odd_lane,
        odd_band,
    ).reshape(-1)
    near = jnp.concatenate([near, downstream_zone[:, 0]])
    consts = (local_kelvin, couple_kinetic_factor[None], arrhenius_onset[None])

    w_row = pltpu.VMEM((BY, neighbours * parts, parts), bf16)
    inv = pltpu.VMEM((SIDE, parts), f32)
    counted = pltpu.VMEM((HALO, kinds + 16, neighbours * parts), bf16)
    half = pltpu.VMEM((SIDE, kinds, parts), bf16)
    gathered = pltpu.VMEM((HALO, kinds, neighbours * parts), bf16)
    all_species = pltpu.VMEM((EXT, kinds, parts), bf16)
    work = 2 * bins * neighbours * parts * parts * 128
    w0, w1, source, target, row = call(
        build_first,
        (near, meta, pos_a, pos_b) + pos_sides + pos_bands,
        2,
        [
            w_row,
            w_row,
            pltpu.VMEM((EXT, parts, FEATURES), bf16),
            pltpu.VMEM((bins, FEATURES, parts), bf16),
            jax.ShapeDtypeStruct((bins,), i32),
        ],
        [pltpu.SMEM((lane_count,), i32)],
        work,
    )
    w2, w3 = call(build_second, (near, source, target), 1, [w_row, w_row], [], work)
    built = (w0, w1, w2, w3)
    by_b, inv_b, species = call(
        step_b,
        (near, meta) + own + sides + bands + built + consts,
        2,
        [half, inv, all_species],
        [counted],
        work // 2,
    )
    by_a, inv_a = call(
        step_a,
        (near, meta, species) + built + consts,
        2,
        [half, inv],
        [counted],
        work // 2,
    )

    own = (by_a, by_b)
    sides = swap(by_a, by_b, "gy")
    own_bands = rows(own)
    corners = rows(sides)
    pieces = own + sides + (own_bands[0], corners[0], own_bands[1], corners[1])
    blocks = list(
        call(
            last_step,
            (near, meta, row) + pieces + built + (inv_a, inv_b) + consts,
            3,
            [pltpu.VMEM((CAP, kinds, parts), bf16)] * lane_count,
            [all_species, gathered, pltpu.VMEM((lane_count * CAP, kinds, parts), bf16)],
            work,
        )
    )
    for way in range(lane_count - 1, 0, -1):
        pairs = [(l, l ^ way) for l in range(lane_count)]
        blocks[way] = lax.ppermute(blocks[way], "gy", pairs)
    return pl.pallas_call(
        place,
        out_shape=jax.ShapeDtypeStruct((lane_count * CAP, kinds, parts), bf16),
        in_specs=[SM] + [VM] * lane_count,
        out_specs=HBM,
        scratch_shapes=[pltpu.SemaphoreType.DMA((lane_count,))],
        compiler_params=pltpu.CompilerParams(vmem_limit_bytes=8 << 20),
        name="place",
    )(meta, *blocks)


def solution(mesh):
    in_specs = (
        P(("gx", "gy"), None, None),
        P(("gx", "gy"), None, None),
        P(("gx", "gy"), None),
        P(),
        P(),
        P(("gx", "gy"), None),
        P(("gx", "gy"), None),
    )
    out_specs = P(("gx", "gy"), None, None)
    return jax.shard_map(
        body, mesh=mesh, in_specs=in_specs, out_specs=out_specs, check_vma=False
    )
```

```python
import math

import jax
import jax.numpy as jnp
from jax import lax
from jax.experimental import pallas as pl
from jax.experimental.pallas import tpu as pltpu
from jax.sharding import PartitionSpec as P


BX = 4
BY = 4
CAP = 2
HALO = 2
WIDTH = 2 * HALO + 1

inverse_width = 4.0
SCALE = math.sqrt(inverse_width * math.log2(math.e))
FAR = -1e30
FEATURES = 48


f32 = jnp.float32
bf16 = jnp.bfloat16
i32 = jnp.int32

SIDE = BX * HALO
QUAD = HALO * HALO
BAND = 4 * QUAD
EXT = 4 * SIDE + 2 * BAND
COUNTS = (SIDE, SIDE, SIDE, SIDE, BAND, BAND)
UNROLL = QUAD * HALO
STARTS = (0, SIDE, 2 * SIDE, 3 * SIDE, 4 * SIDE, 4 * SIDE + BAND)


def swaps(axis):
    bands, lanes = lax.axis_size("gx"), lax.axis_size("gy")

    def partner(g, l, first):
        i, count = (l, lanes) if axis == "gy" else (g, bands)
        other = i + 1 if (i - first) % 2 == 0 else i - 1
        if 0 <= other < count:
            return (g, other) if axis == "gy" else (other, l)
        if axis == "gy":
            return (g ^ 1, l) if bands % 2 == 0 else None
        return (g, l ^ 2) if lanes % 4 == 0 else None

    out = []
    for first in range(2):
        pairs = []
        for g in range(bands):
            for l in range(lanes):
                to = partner(g, l, first)
                if to is not None:
                    pairs.append((g * lanes + l, to[0] * lanes + to[1]))
        out.append(pairs)
    return out


def slot_of(ex, ey, odd_lane, odd_band):
    low = ey < BY // 2
    by_a = low == (odd_lane == 1)
    own = (ey >= 0) & (ey < BY)
    piece = jnp.where(own, jnp.where(by_a, 0, 1), jnp.where(by_a, 3, 2))
    column = (ey + HALO) % HALO
    inner = piece * SIDE + ex * HALO + column
    from_a = (ex < 0) == (odd_band == 1)
    row = jnp.where(ex < 0, ex + HALO, ex - BX)
    outer = jnp.where(from_a, STARTS[4], STARTS[5]) + piece * QUAD + row * HALO + column
    return jnp.where((ex >= 0) & (ex < BX), inner, outer)


def place_of(piece, i, odd_lane, odd_band):
    if piece < 4:
        part, ex = piece, i // HALO
    else:
        part, row = i // QUAD, i % QUAD // HALO
        up = (odd_band == 1) if piece == 4 else (odd_band == 0)
        ex = jnp.where(up, row - HALO, row + BX)
    by_a = (part == 0) | (part == 3)
    low = (by_a == (odd_lane == 1)) if not isinstance(by_a, bool) else (odd_lane == int(by_a))
    outside = part >= 2
    base = jnp.where(low, jnp.where(outside, -HALO, 0), jnp.where(outside, BY, BY - HALO))
    return ex, base + i % HALO


def split(meta_ref, x, pos_hbm, a, b, pos_a, pos_b, pos, sem, pos_sem):
    pos_copy = pltpu.make_async_copy(pos_hbm, pos, pos_sem)
    pos_copy.start()
    low_a = jnp.where(meta_ref[4] == 1, 0, BY - HALO)
    lows = (low_a, BY - HALO - low_a)
    copies = []
    for m, (out, low) in enumerate(zip((a, b), lows)):
        for r in range(BX):
            source = x.at[pl.ds(r * BY + low, HALO)]
            target = out.at[pl.ds(r * HALO, HALO)]
            copies.append(pltpu.make_async_copy(source, target, sem.at[m, r]))
    for copy in copies:
        copy.start()
    pos_copy.wait()
    for out, low in zip((pos_a, pos_b), lows):
        for r in range(BX):
            for i in range(HALO):
                for c in range(pos.shape[0]):
                    out[r * HALO + i, c : c + 1] = pos[c, pl.ds(r * BY + low + i, 1)]
    for copy in copies:
        copy.wait()


def pack(meta_ref, *refs):
    pieces, (out_a, out_b) = refs[:-2], refs[-2:]
    size = BX * HALO
    from_a = jnp.where(meta_ref[5] == 1, 0, size - QUAD)
    for n, x in enumerate(pieces):
        out_a[pl.ds(n * QUAD, QUAD)] = x[pl.ds(from_a, QUAD)]
        out_b[pl.ds(n * QUAD, QUAD)] = x[pl.ds(size - QUAD - from_a, QUAD)]


def swap(by_a, by_b, axis):
    pairs_a, pairs_b = swaps(axis)
    axis = ("gx", "gy")
    from_b = lax.ppermute(by_b, axis, pairs_b)
    from_a = lax.ppermute(by_a, axis, pairs_a)
    return from_a, from_b


def three_parts(x):
    high = x.astype(bf16).astype(f32)
    rest = x - high
    middle = rest.astype(bf16).astype(f32)
    return high, middle, rest - middle


def coordinates(pos, ex, ey):
    row = lax.broadcasted_iota(i32, (8, pos.shape[-1]), 0)
    padded = jnp.concatenate([pos, jnp.zeros((5, pos.shape[-1]), f32)], axis=0)
    middle = jnp.where(
        row == 0,
        ex.astype(f32) - (BX - 1) / 2,
        jnp.where(row == 1, ey.astype(f32) - (BY - 1) / 2, 0.0),
    )
    return (padded + middle) * SCALE, row


def features(pos, ex, ey, inside, as_target):
    x, row = coordinates(pos, ex, ey)
    norm = jnp.sum(x * x, axis=0, keepdims=True)
    high, middle, low = three_parts(x)
    nh, nm, nl = three_parts(norm)
    last = row == 3
    pick = lambda a, b: jnp.where(last, a, b)
    source = (
        pick(jnp.where(inside, -nh, FAR), high),
        pick(-nm, high),
        pick(-nl, middle),
        pick(1.0, high),
        pick(1.0, low),
        pick(1.0, middle),
    )
    source = jnp.concatenate(source, axis=0).astype(bf16).T
    if not as_target:
        return source, None
    high, middle, low = 2.0 * high, 2.0 * middle, 2.0 * low
    target = (
        pick(1.0, high),
        pick(1.0, middle),
        pick(1.0, high),
        pick(-nh, low),
        pick(-nm, high),
        pick(-nl, middle),
    )
    return source, jnp.concatenate(target, axis=0).astype(bf16)


def neighbours_of(near_ref):
    return near_ref.shape[0] // (BX * BY) - 1


def build_rows(near_ref, source, target, w_refs, first_row):
    parts = source.shape[1]
    neighbours = neighbours_of(near_ref)
    for g, w_ref in enumerate(w_refs):

        def one(c, _, g=g, w_ref=w_ref):
            b = (first_row + g) * BY + c
            f = target[b]
            for k in range(neighbours):
                q = near_ref[b * neighbours + k]
                e = jnp.dot(source[q], f, preferred_element_type=f32)
                w_ref[c, pl.ds(k * parts, parts)] = jnp.exp2(e.astype(bf16))
            return 0

        lax.fori_loop(0, BY, one, 0)


def build_first(
    near_ref, meta_ref, o0, o1, c0, c1, r0, r1, w0, w1, source, target, row_ref, taken
):
    odd_lane, odd_band = meta_ref[4], meta_ref[5]
    for piece, ref in enumerate((o0, o1, c0, c1, r0, r1)):

        def some(j, _, piece=piece, ref=ref):
            for n in range(UNROLL):
                i = j * UNROLL + n
                ex, ey = place_of(piece, i, odd_lane, odd_band)
                gx = meta_ref[0] + ex
                gy = meta_ref[1] + ey
                inside = (gx >= 0) & (gx < meta_ref[2]) & (gy >= 0) & (gy < meta_ref[3])
                s, t = features(ref[i], ex, ey, inside, piece < 2)
                source[STARTS[piece] + i] = s
                if piece < 2:
                    target[ex * BY + ey] = t
            return 0

        lax.fori_loop(0, COUNTS[piece] // UNROLL, some, 0)
    for z in range(taken.shape[0]):
        taken[z] = 0

    def place(b, _):
        zone = near_ref[BX * BY * neighbours_of(near_ref) + b]
        order = taken[zone]
        taken[zone] = order + 1
        row_ref[b] = zone * CAP + order
        return 0

    lax.fori_loop(0, BX * BY, place, 0)
    build_rows(near_ref, source, target, (w0, w1), 0)


def build_second(near_ref, source, target, w2, w3):
    build_rows(near_ref, source, target, (w2, w3), BX // 2)


def column(row_ref):
    n = row_ref.shape[1]
    shape = (n, n)
    same = lax.broadcasted_iota(i32, shape, 0) == lax.broadcasted_iota(i32, shape, 1)
    return jnp.sum(jnp.where(same, row_ref[...], 0.0), axis=1, keepdims=True)


def react(mixture, kelvin, factor, onset):
    half = mixture.shape[0] // 2
    u = mixture[:half]
    v = mixture[half:]
    speed = factor * jnp.exp(-onset / kelvin)
    reacted = speed * u * v / (1.0 + speed * (u + v))
    return jnp.concatenate([u - reacted, v - reacted], axis=0).astype(bf16)


def mix(near_ref, species, gathered, w, b):
    neighbours = neighbours_of(near_ref)
    parts = species.shape[2]
    kinds = species.shape[1]
    for k in range(neighbours):
        q = near_ref[b * neighbours + k]
        gathered[:kinds, k * parts : (k + 1) * parts] = species[q]
    return jnp.dot(gathered[...], w, preferred_element_type=f32)


def join(pieces, species):
    start = 0
    for ref in pieces:
        species[pl.ds(start, ref.shape[0])] = ref[...]
        start += ref.shape[0]


def step_columns(near_ref, species, gathered, w_refs, consts, low, out_ref, inv_ref):
    kinds = species.shape[1]
    gathered[:, kinds:] = jnp.ones_like(gathered[:, kinds:])
    kelvin_ref, factor_ref, onset_ref = consts
    factor, onset = column(factor_ref), column(onset_ref)
    for g, w_ref in enumerate(w_refs):

        for i in range(HALO):
            c = low + i
            b = g * BY + c
            mixed = mix(near_ref, species, gathered.at[i], w_ref[c], b)
            inv = 1.0 / mixed[kinds : kinds + 1]
            inv_ref[pl.ds(g * HALO + i, 1)] = inv
            mixed = mixed[:kinds] * inv
            out_ref[g * HALO + i] = react(mixed, kelvin_ref[pl.ds(b, 1)], factor, onset)


def step_b(near_ref, meta_ref, *refs):
    pieces, w_refs, consts = refs[:6], refs[6:10], refs[10:13]
    out, inv_ref, species, gathered = refs[13:]
    join(pieces, species)
    low = jnp.where(meta_ref[4] == 1, BY - HALO, 0)
    step_columns(near_ref, species, gathered, w_refs, consts, low, out, inv_ref)


def step_a(near_ref, meta_ref, species, *refs):
    w_refs, consts = refs[:4], refs[4:7]
    out, inv_ref, gathered = refs[7:]
    low = jnp.where(meta_ref[4] == 1, 0, BY - HALO)
    step_columns(near_ref, species, gathered, w_refs, consts, low, out, inv_ref)


def last_step(near_ref, meta_ref, row_ref, *refs):
    pieces, refs = refs[:8], refs[8:]
    w_refs, (inv_a, inv_b), refs = refs[:4], refs[4:6], refs[6:]
    (kelvin_ref, factor_ref, onset_ref), refs = refs[:3], refs[3:]
    outs, (species, gathered, staged) = refs[:-3], refs[-3:]
    join(pieces, species)
    factor, onset = column(factor_ref), column(onset_ref)
    lane = meta_ref[1] // BY
    a_first = meta_ref[4] == 1
    if staged.shape[0] > BX * BY:
        staged[...] = jnp.zeros_like(staged)
    for g, w_ref in enumerate(w_refs):

        def some(j, _, g=g, w_ref=w_ref):
            by_a = (j == 0) == a_first
            for i in range(HALO):
                c = j * HALO + i
                at = pl.ds(g * HALO + i, 1)
                b = g * BY + c
                row = row_ref[b]
                mixed = mix(near_ref, species, gathered.at[i], w_ref[c], b)
                mixed = mixed * jnp.where(by_a, inv_a[at], inv_b[at])
                moved = react(mixed, kelvin_ref[pl.ds(b, 1)], factor, onset)
                staged[((row // CAP) ^ lane) * CAP + row % CAP] = moved
            return 0

        lax.fori_loop(0, BY // HALO, some, 0)
    for i, out in enumerate(outs):
        out[...] = staged[i * CAP : (i + 1) * CAP]


def place(meta_ref, *refs):
    blocks, (out, sem) = refs[:-2], refs[-2:]
    lane = meta_ref[1] // BY
    copies = [
        pltpu.make_async_copy(x, out.at[pl.ds((lane ^ way) * CAP, CAP)], sem.at[way])
        for way, x in enumerate(blocks)
    ]
    for copy in copies:
        copy.start()
    for copy in copies:
        copy.wait()


VM = pl.BlockSpec(memory_space=pltpu.VMEM)
SM = pl.BlockSpec(memory_space=pltpu.SMEM)
HBM = pl.BlockSpec(memory_space=pltpu.HBM)


def call(kernel, operands, scalars, outs, scratch, flops):
    single = not isinstance(outs, (list, tuple))
    return pl.pallas_call(
        kernel,
        out_shape=outs,
        in_specs=[SM] * scalars + [VM] * (len(operands) - scalars),
        out_specs=VM if single else [SM if o.dtype == i32 else VM for o in outs],
        scratch_shapes=scratch,
        compiler_params=pltpu.CompilerParams(vmem_limit_bytes=8 << 20),
        cost_estimate=pl.CostEstimate(
            flops=flops, bytes_accessed=1 << 20, transcendentals=0
        ),
    )(*operands)


def body(
    solute_load,
    walker_displacement,
    local_kelvin,
    couple_kinetic_factor,
    arrhenius_onset,
    adjacent_cell_keys,
    downstream_zone,
):
    lane_count = lax.axis_size("gy")
    bins, kinds, parts = solute_load.shape
    neighbours = adjacent_cell_keys.shape[1]
    band, lane = lax.axis_index("gx"), lax.axis_index("gy")
    odd_band, odd_lane = band % 2, lane % 2

    meta = jnp.stack(
        [
            band * BX,
            lane * BY,
            jnp.int32(lax.axis_size("gx") * BX),
            jnp.int32(lane_count * BY),
            odd_lane,
            odd_band,
        ]
    ).astype(i32)
    like = lambda x, n: pltpu.VMEM((n,) + x.shape[1:], x.dtype)
    axes = walker_displacement.shape[1]
    own_a, own_b, pos_a, pos_b = pl.pallas_call(
        split,
        out_shape=[pltpu.VMEM((SIDE, kinds, parts), bf16)] * 2
        + [pltpu.VMEM((SIDE, axes, parts), f32)] * 2,
        in_specs=[SM, HBM, HBM],
        out_specs=[VM] * 4,
        scratch_shapes=[
            pltpu.VMEM((axes, bins, parts), f32),
            pltpu.SemaphoreType.DMA((2, BX)),
            pltpu.SemaphoreType.DMA,
        ],
        compiler_params=pltpu.CompilerParams(vmem_limit_bytes=8 << 20),
        name="split",
    )(
        meta,
        pltpu.with_memory_space_constraint(solute_load, pltpu.HBM),
        pltpu.with_memory_space_constraint(walker_displacement.transpose(1, 0, 2), pltpu.HBM),
    )

    def rows(pieces):
        size = len(pieces) * QUAD
        by_a, by_b = call(
            pack, (meta,) + pieces, 1, [like(pieces[0], size)] * 2, [], 1 << 20
        )
        return swap(by_a, by_b, "gx")

    pos_sides = swap(pos_a, pos_b, "gy")[::-1]
    pos_bands = rows((pos_a, pos_b) + pos_sides)
    own = (own_a, own_b)
    sides = swap(own_a, own_b, "gy")[::-1]
    bands = rows(own + sides)

    ids = jnp.arange(bins, dtype=i32)
    near = slot_of(
        (ids // BY)[:, None] + adjacent_cell_keys // WIDTH - HALO,
        (ids % BY)[:, None] + adjacent_cell_keys % WIDTH - HALO,
        odd_lane,
        odd_band,
    ).reshape(-1)
    near = jnp.concatenate([near, downstream_zone[:, 0]])
    consts = (local_kelvin, couple_kinetic_factor[None], arrhenius_onset[None])

    w_row = pltpu.VMEM((BY, neighbours * parts, parts), bf16)
    inv = pltpu.VMEM((SIDE, parts), f32)
    counted = pltpu.VMEM((HALO, kinds + 16, neighbours * parts), bf16)
    half = pltpu.VMEM((SIDE, kinds, parts), bf16)
    gathered = pltpu.VMEM((HALO, kinds, neighbours * parts), bf16)
    all_species = pltpu.VMEM((EXT, kinds, parts), bf16)
    work = 2 * bins * neighbours * parts * parts * 128
    w0, w1, source, target, row = call(
        build_first,
        (near, meta, pos_a, pos_b) + pos_sides + pos_bands,
        2,
        [
            w_row,
            w_row,
            pltpu.VMEM((EXT, parts, FEATURES), bf16),
            pltpu.VMEM((bins, FEATURES, parts), bf16),
            jax.ShapeDtypeStruct((bins,), i32),
        ],
        [pltpu.SMEM((lane_count,), i32)],
        work,
    )
    w2, w3 = call(build_second, (near, source, target), 1, [w_row, w_row], [], work)
    built = (w0, w1, w2, w3)
    by_b, inv_b, species = call(
        step_b,
        (near, meta) + own + sides + bands + built + consts,
        2,
        [half, inv, all_species],
        [counted],
        work // 2,
    )
    by_a, inv_a = call(
        step_a,
        (near, meta, species) + built + consts,
        2,
        [half, inv],
        [counted],
        work // 2,
    )

    own = (by_a, by_b)
    sides = swap(by_a, by_b, "gy")[::-1]
    early = rows(own + sides[:1])
    corners = rows(sides[1:])
    pieces = own + sides + (early[0], corners[0], early[1], corners[1])
    blocks = list(
        call(
            last_step,
            (near, meta, row) + pieces + built + (inv_a, inv_b) + consts,
            3,
            [pltpu.VMEM((CAP, kinds, parts), bf16)] * lane_count,
            [all_species, gathered, pltpu.VMEM((lane_count * CAP, kinds, parts), bf16)],
            work,
        )
    )
    for way in range(lane_count - 1, 0, -1):
        pairs = [(l, l ^ way) for l in range(lane_count)]
        blocks[way] = lax.ppermute(blocks[way], "gy", pairs)
    return pl.pallas_call(
        place,
        out_shape=jax.ShapeDtypeStruct((lane_count * CAP, kinds, parts), bf16),
        in_specs=[SM] + [VM] * lane_count,
        out_specs=HBM,
        scratch_shapes=[pltpu.SemaphoreType.DMA((lane_count,))],
        compiler_params=pltpu.CompilerParams(vmem_limit_bytes=8 << 20),
        name="place",
    )(meta, *blocks)


def solution(mesh):
    in_specs = (
        P(("gx", "gy"), None, None),
        P(("gx", "gy"), None, None),
        P(("gx", "gy"), None),
        P(),
        P(),
        P(("gx", "gy"), None),
        P(("gx", "gy"), None),
    )
    out_specs = P(("gx", "gy"), None, None)
    return jax.shard_map(
        body, mesh=mesh, in_specs=in_specs, out_specs=out_specs, check_vma=False
    )
```

```python
import math

import jax
import jax.numpy as jnp
from jax import lax
from jax.experimental import pallas as pl
from jax.experimental.pallas import tpu as pltpu
from jax.sharding import PartitionSpec as P


BX = 4
BY = 4
CAP = 2
HALO = 2
WIDTH = 2 * HALO + 1

inverse_width = 4.0
SCALE = math.sqrt(inverse_width * math.log2(math.e))
FAR = -1e30
FEATURES = 48


f32 = jnp.float32
bf16 = jnp.bfloat16
i32 = jnp.int32

SIDE = BX * HALO
QUAD = HALO * HALO
BAND = 4 * QUAD
EXT = 4 * SIDE + 2 * BAND
COUNTS = (SIDE, SIDE, SIDE, SIDE, BAND, BAND)
UNROLL = QUAD * HALO
STARTS = (0, SIDE, 2 * SIDE, 3 * SIDE, 4 * SIDE, 4 * SIDE + BAND)


def swaps(axis):
    bands, lanes = lax.axis_size("gx"), lax.axis_size("gy")

    def partner(g, l, first):
        i, count = (l, lanes) if axis == "gy" else (g, bands)
        other = i + 1 if (i - first) % 2 == 0 else i - 1
        if 0 <= other < count:
            return (g, other) if axis == "gy" else (other, l)
        if axis == "gy":
            return (g ^ 1, l) if bands % 2 == 0 else None
        return (g, l ^ 2) if lanes % 4 == 0 else None

    out = []
    for first in range(2):
        pairs = []
        for g in range(bands):
            for l in range(lanes):
                to = partner(g, l, first)
                if to is not None:
                    pairs.append((g * lanes + l, to[0] * lanes + to[1]))
        out.append(pairs)
    return out


def slot_of(ex, ey, odd_lane, odd_band):
    low = ey < BY // 2
    by_a = low == (odd_lane == 1)
    own = (ey >= 0) & (ey < BY)
    piece = jnp.where(own, jnp.where(by_a, 0, 1), jnp.where(by_a, 3, 2))
    column = (ey + HALO) % HALO
    inner = piece * SIDE + ex * HALO + column
    from_a = (ex < 0) == (odd_band == 1)
    row = jnp.where(ex < 0, ex + HALO, ex - BX)
    outer = jnp.where(from_a, STARTS[4], STARTS[5]) + piece * QUAD + row * HALO + column
    return jnp.where((ex >= 0) & (ex < BX), inner, outer)


def place_of(piece, i, odd_lane, odd_band):
    if piece < 4:
        part, ex = piece, i // HALO
    else:
        part, row = i // QUAD, i % QUAD // HALO
        up = (odd_band == 1) if piece == 4 else (odd_band == 0)
        ex = jnp.where(up, row - HALO, row + BX)
    by_a = (part == 0) | (part == 3)
    low = (by_a == (odd_lane == 1)) if not isinstance(by_a, bool) else (odd_lane == int(by_a))
    outside = part >= 2
    base = jnp.where(low, jnp.where(outside, -HALO, 0), jnp.where(outside, BY, BY - HALO))
    return ex, base + i % HALO


def split(meta_ref, x, pos_hbm, a, b, pos_a, pos_b, pos, sem, pos_sem):
    pos_copy = pltpu.make_async_copy(pos_hbm, pos, pos_sem)
    pos_copy.start()
    low_a = jnp.where(meta_ref[4] == 1, 0, BY - HALO)
    lows = (low_a, BY - HALO - low_a)
    copies = []
    for m, (out, low) in enumerate(zip((a, b), lows)):
        for r in range(BX):
            source = x.at[pl.ds(r * BY + low, HALO)]
            target = out.at[pl.ds(r * HALO, HALO)]
            copies.append(pltpu.make_async_copy(source, target, sem.at[m, r]))
    for copy in copies:
        copy.start()
    pos_copy.wait()
    for out, low in zip((pos_a, pos_b), lows):
        for r in range(BX):
            for i in range(HALO):
                for c in range(pos.shape[0]):
                    out[r * HALO + i, c : c + 1] = pos[c, pl.ds(r * BY + low + i, 1)]
    for copy in copies:
        copy.wait()


def pack(meta_ref, *refs):
    pieces, (out_a, out_b) = refs[:-2], refs[-2:]
    size = BX * HALO
    from_a = jnp.where(meta_ref[5] == 1, 0, size - QUAD)
    for n, x in enumerate(pieces):
        out_a[pl.ds(n * QUAD, QUAD)] = x[pl.ds(from_a, QUAD)]
        out_b[pl.ds(n * QUAD, QUAD)] = x[pl.ds(size - QUAD - from_a, QUAD)]


def swap(by_a, by_b, axis):
    pairs_a, pairs_b = swaps(axis)
    axis = ("gx", "gy")
    from_b = lax.ppermute(by_b, axis, pairs_b)
    from_a = lax.ppermute(by_a, axis, pairs_a)
    return from_a, from_b


def three_parts(x):
    high = x.astype(bf16).astype(f32)
    rest = x - high
    middle = rest.astype(bf16).astype(f32)
    return high, middle, rest - middle


def coordinates(pos, ex, ey):
    row = lax.broadcasted_iota(i32, (8, pos.shape[-1]), 0)
    padded = jnp.concatenate([pos, jnp.zeros((5, pos.shape[-1]), f32)], axis=0)
    middle = jnp.where(
        row == 0,
        ex.astype(f32) - (BX - 1) / 2,
        jnp.where(row == 1, ey.astype(f32) - (BY - 1) / 2, 0.0),
    )
    return (padded + middle) * SCALE, row


def features(pos, ex, ey, inside, as_target):
    x, row = coordinates(pos, ex, ey)
    norm = jnp.sum(x * x, axis=0, keepdims=True)
    high, middle, low = three_parts(x)
    nh, nm, nl = three_parts(norm)
    last = row == 3
    pick = lambda a, b: jnp.where(last, a, b)
    source = (
        pick(jnp.where(inside, -nh, FAR), high),
        pick(-nm, high),
        pick(-nl, middle),
        pick(1.0, high),
        pick(1.0, low),
        pick(1.0, middle),
    )
    source = jnp.concatenate(source, axis=0).astype(bf16).T
    if not as_target:
        return source, None
    high, middle, low = 2.0 * high, 2.0 * middle, 2.0 * low
    target = (
        pick(1.0, high),
        pick(1.0, middle),
        pick(1.0, high),
        pick(-nh, low),
        pick(-nm, high),
        pick(-nl, middle),
    )
    return source, jnp.concatenate(target, axis=0).astype(bf16)


def neighbours_of(near_ref):
    return near_ref.shape[0] // (BX * BY) - 1


def build_rows(near_ref, source, target, w_refs, first_row):
    parts = source.shape[1]
    neighbours = neighbours_of(near_ref)
    for g, w_ref in enumerate(w_refs):

        def one(c, _, g=g, w_ref=w_ref):
            b = (first_row + g) * BY + c
            f = target[b]
            for k in range(neighbours):
                q = near_ref[b * neighbours + k]
                e = jnp.dot(source[q], f, preferred_element_type=f32)
                w_ref[c, pl.ds(k * parts, parts)] = jnp.exp2(e.astype(bf16))
            return 0

        lax.fori_loop(0, BY, one, 0)


def build_first(
    near_ref, meta_ref, o0, o1, c0, c1, r0, r1, w0, w1, source, target, row_ref, taken
):
    odd_lane, odd_band = meta_ref[4], meta_ref[5]
    for piece, ref in enumerate((o0, o1, c0, c1, r0, r1)):

        def some(j, _, piece=piece, ref=ref):
            for n in range(UNROLL):
                i = j * UNROLL + n
                ex, ey = place_of(piece, i, odd_lane, odd_band)
                gx = meta_ref[0] + ex
                gy = meta_ref[1] + ey
                inside = (gx >= 0) & (gx < meta_ref[2]) & (gy >= 0) & (gy < meta_ref[3])
                s, t = features(ref[i], ex, ey, inside, piece < 2)
                source[STARTS[piece] + i] = s
                if piece < 2:
                    target[ex * BY + ey] = t
            return 0

        lax.fori_loop(0, COUNTS[piece] // UNROLL, some, 0)
    for z in range(taken.shape[0]):
        taken[z] = 0

    def place(b, _):
        zone = near_ref[BX * BY * neighbours_of(near_ref) + b]
        order = taken[zone]
        taken[zone] = order + 1
        row_ref[b] = zone * CAP + order
        return 0

    lax.fori_loop(0, BX * BY, place, 0)
    build_rows(near_ref, source, target, (w0, w1), 0)


def build_second(near_ref, source, target, w2, w3):
    build_rows(near_ref, source, target, (w2, w3), BX // 2)


def column(row_ref):
    n = row_ref.shape[1]
    shape = (n, n)
    same = lax.broadcasted_iota(i32, shape, 0) == lax.broadcasted_iota(i32, shape, 1)
    return jnp.sum(jnp.where(same, row_ref[...], 0.0), axis=1, keepdims=True)


def react(mixture, kelvin, factor, onset):
    half = mixture.shape[0] // 2
    u = mixture[:half]
    v = mixture[half:]
    speed = factor * jnp.exp(-onset / kelvin)
    reacted = speed * u * v / (1.0 + speed * (u + v))
    return jnp.concatenate([u - reacted, v - reacted], axis=0).astype(bf16)


def mix(near_ref, species, gathered, w, b):
    neighbours = neighbours_of(near_ref)
    parts = species.shape[2]
    kinds = species.shape[1]
    for k in range(neighbours):
        q = near_ref[b * neighbours + k]
        gathered[:kinds, k * parts : (k + 1) * parts] = species[q]
    return jnp.dot(gathered[...], w, preferred_element_type=f32)


def join(pieces, species):
    start = 0
    for ref in pieces:
        species[pl.ds(start, ref.shape[0])] = ref[...]
        start += ref.shape[0]


def step_columns(near_ref, species, gathered, w_refs, consts, low, out_ref, inv_ref):
    kinds = species.shape[1]
    gathered[:, kinds:] = jnp.ones_like(gathered[:, kinds:])
    kelvin_ref, factor_ref, onset_ref = consts
    factor, onset = column(factor_ref), column(onset_ref)
    for g, w_ref in enumerate(w_refs):

        for i in range(HALO):
            c = low + i
            b = g * BY + c
            mixed = mix(near_ref, species, gathered.at[i], w_ref[c], b)
            inv = 1.0 / mixed[kinds : kinds + 1]
            inv_ref[pl.ds(g * HALO + i, 1)] = inv
            mixed = mixed[:kinds] * inv
            out_ref[g * HALO + i] = react(mixed, kelvin_ref[pl.ds(b, 1)], factor, onset)


def step_b(near_ref, meta_ref, *refs):
    pieces, w_refs, consts = refs[:6], refs[6:10], refs[10:13]
    out, inv_ref, species, gathered = refs[13:]
    join(pieces, species)
    low = jnp.where(meta_ref[4] == 1, BY - HALO, 0)
    step_columns(near_ref, species, gathered, w_refs, consts, low, out, inv_ref)


def step_a(near_ref, meta_ref, species, *refs):
    w_refs, consts = refs[:4], refs[4:7]
    out, inv_ref, gathered = refs[7:]
    low = jnp.where(meta_ref[4] == 1, 0, BY - HALO)
    step_columns(near_ref, species, gathered, w_refs, consts, low, out, inv_ref)


def last_step(near_ref, meta_ref, row_ref, *refs):
    pieces, refs = refs[:8], refs[8:]
    w_refs, (inv_a, inv_b), refs = refs[:4], refs[4:6], refs[6:]
    (kelvin_ref, factor_ref, onset_ref), refs = refs[:3], refs[3:]
    outs, (species, gathered, staged) = refs[:-3], refs[-3:]
    join(pieces, species)
    factor, onset = column(factor_ref), column(onset_ref)
    lane = meta_ref[1] // BY
    a_first = meta_ref[4] == 1
    if staged.shape[0] > BX * BY:
        staged[...] = jnp.zeros_like(staged)
    for g, w_ref in enumerate(w_refs):

        def some(g=g, w_ref=w_ref):
            for i in range(BY):
                c = i
                by_a = a_first if i < HALO else ~a_first
                at = pl.ds(g * HALO + i % HALO, 1)
                b = g * BY + c
                row = row_ref[b]
                mixed = mix(near_ref, species, gathered.at[i], w_ref[c], b)
                mixed = mixed * jnp.where(by_a, inv_a[at], inv_b[at])
                moved = react(mixed, kelvin_ref[pl.ds(b, 1)], factor, onset)
                staged[((row // CAP) ^ lane) * CAP + row % CAP] = moved
            return 0

        some()
    for i, out in enumerate(outs):
        out[...] = staged[i * CAP : (i + 1) * CAP]


def place(meta_ref, *refs):
    blocks, (out, sem) = refs[:-2], refs[-2:]
    lane = meta_ref[1] // BY
    copies = [
        pltpu.make_async_copy(x, out.at[pl.ds((lane ^ way) * CAP, CAP)], sem.at[way])
        for way, x in enumerate(blocks)
    ]
    for copy in copies:
        copy.start()
    for copy in copies:
        copy.wait()


VM = pl.BlockSpec(memory_space=pltpu.VMEM)
SM = pl.BlockSpec(memory_space=pltpu.SMEM)
HBM = pl.BlockSpec(memory_space=pltpu.HBM)


def call(kernel, operands, scalars, outs, scratch, flops):
    single = not isinstance(outs, (list, tuple))
    return pl.pallas_call(
        kernel,
        out_shape=outs,
        in_specs=[SM] * scalars + [VM] * (len(operands) - scalars),
        out_specs=VM if single else [SM if o.dtype == i32 else VM for o in outs],
        scratch_shapes=scratch,
        compiler_params=pltpu.CompilerParams(vmem_limit_bytes=8 << 20),
        cost_estimate=pl.CostEstimate(
            flops=flops, bytes_accessed=1 << 20, transcendentals=0
        ),
    )(*operands)


def body(
    solute_load,
    walker_displacement,
    local_kelvin,
    couple_kinetic_factor,
    arrhenius_onset,
    adjacent_cell_keys,
    downstream_zone,
):
    lane_count = lax.axis_size("gy")
    bins, kinds, parts = solute_load.shape
    neighbours = adjacent_cell_keys.shape[1]
    band, lane = lax.axis_index("gx"), lax.axis_index("gy")
    odd_band, odd_lane = band % 2, lane % 2

    meta = jnp.stack(
        [
            band * BX,
            lane * BY,
            jnp.int32(lax.axis_size("gx") * BX),
            jnp.int32(lane_count * BY),
            odd_lane,
            odd_band,
        ]
    ).astype(i32)
    like = lambda x, n: pltpu.VMEM((n,) + x.shape[1:], x.dtype)
    axes = walker_displacement.shape[1]
    own_a, own_b, pos_a, pos_b = pl.pallas_call(
        split,
        out_shape=[pltpu.VMEM((SIDE, kinds, parts), bf16)] * 2
        + [pltpu.VMEM((SIDE, axes, parts), f32)] * 2,
        in_specs=[SM, HBM, HBM],
        out_specs=[VM] * 4,
        scratch_shapes=[
            pltpu.VMEM((axes, bins, parts), f32),
            pltpu.SemaphoreType.DMA((2, BX)),
            pltpu.SemaphoreType.DMA,
        ],
        compiler_params=pltpu.CompilerParams(vmem_limit_bytes=8 << 20),
        name="split",
    )(
        meta,
        pltpu.with_memory_space_constraint(solute_load, pltpu.HBM),
        pltpu.with_memory_space_constraint(walker_displacement.transpose(1, 0, 2), pltpu.HBM),
    )

    def rows(pieces):
        size = len(pieces) * QUAD
        by_a, by_b = call(
            pack, (meta,) + pieces, 1, [like(pieces[0], size)] * 2, [], 1 << 20
        )
        return swap(by_a, by_b, "gx")

    pos_sides = swap(pos_a, pos_b, "gy")[::-1]
    pos_bands = rows((pos_a, pos_b) + pos_sides)
    own = (own_a, own_b)
    sides = swap(own_a, own_b, "gy")[::-1]
    bands = rows(own + sides)

    ids = jnp.arange(bins, dtype=i32)
    near = slot_of(
        (ids // BY)[:, None] + adjacent_cell_keys // WIDTH - HALO,
        (ids % BY)[:, None] + adjacent_cell_keys % WIDTH - HALO,
        odd_lane,
        odd_band,
    ).reshape(-1)
    near = jnp.concatenate([near, downstream_zone[:, 0]])
    consts = (local_kelvin, couple_kinetic_factor[None], arrhenius_onset[None])

    w_row = pltpu.VMEM((BY, neighbours * parts, parts), bf16)
    inv = pltpu.VMEM((SIDE, parts), f32)
    counted = pltpu.VMEM((HALO, kinds + 16, neighbours * parts), bf16)
    half = pltpu.VMEM((SIDE, kinds, parts), bf16)
    gathered = pltpu.VMEM((HALO, kinds, neighbours * parts), bf16)
    all_species = pltpu.VMEM((EXT, kinds, parts), bf16)
    work = 2 * bins * neighbours * parts * parts * 128
    w0, w1, source, target, row = call(
        build_first,
        (near, meta, pos_a, pos_b) + pos_sides + pos_bands,
        2,
        [
            w_row,
            w_row,
            pltpu.VMEM((EXT, parts, FEATURES), bf16),
            pltpu.VMEM((bins, FEATURES, parts), bf16),
            jax.ShapeDtypeStruct((bins,), i32),
        ],
        [pltpu.SMEM((lane_count,), i32)],
        work,
    )
    w2, w3 = call(build_second, (near, source, target), 1, [w_row, w_row], [], work)
    built = (w0, w1, w2, w3)
    by_b, inv_b, species = call(
        step_b,
        (near, meta) + own + sides + bands + built + consts,
        2,
        [half, inv, all_species],
        [counted],
        work // 2,
    )
    by_a, inv_a = call(
        step_a,
        (near, meta, species) + built + consts,
        2,
        [half, inv],
        [counted],
        work // 2,
    )

    own = (by_a, by_b)
    sides = swap(by_a, by_b, "gy")[::-1]
    early = rows(own + sides[:1])
    corners = rows(sides[1:])
    pieces = own + sides + (early[0], corners[0], early[1], corners[1])
    blocks = list(
        call(
            last_step,
            (near, meta, row) + pieces + built + (inv_a, inv_b) + consts,
            3,
            [pltpu.VMEM((CAP, kinds, parts), bf16)] * lane_count,
            [all_species, pltpu.VMEM((BY, kinds, neighbours * parts), bf16), pltpu.VMEM((lane_count * CAP, kinds, parts), bf16)],
            work,
        )
    )
    for way in range(lane_count - 1, 0, -1):
        pairs = [(l, l ^ way) for l in range(lane_count)]
        blocks[way] = lax.ppermute(blocks[way], "gy", pairs)
    return pl.pallas_call(
        place,
        out_shape=jax.ShapeDtypeStruct((lane_count * CAP, kinds, parts), bf16),
        in_specs=[SM] + [VM] * lane_count,
        out_specs=HBM,
        scratch_shapes=[pltpu.SemaphoreType.DMA((lane_count,))],
        compiler_params=pltpu.CompilerParams(vmem_limit_bytes=8 << 20),
        name="place",
    )(meta, *blocks)


def solution(mesh):
    in_specs = (
        P(("gx", "gy"), None, None),
        P(("gx", "gy"), None, None),
        P(("gx", "gy"), None),
        P(),
        P(),
        P(("gx", "gy"), None),
        P(("gx", "gy"), None),
    )
    out_specs = P(("gx", "gy"), None, None)
    return jax.shard_map(
        body, mesh=mesh, in_specs=in_specs, out_specs=out_specs, check_vma=False
    )
```

```python
import math

import jax
import jax.numpy as jnp
from jax import lax
from jax.experimental import pallas as pl
from jax.experimental.pallas import tpu as pltpu
from jax.sharding import PartitionSpec as P


BX = 4
BY = 4
CAP = 2
HALO = 2
WIDTH = 2 * HALO + 1

inverse_width = 4.0
SCALE = math.sqrt(inverse_width * math.log2(math.e))
FAR = -1e30
FEATURES = 48


f32 = jnp.float32
bf16 = jnp.bfloat16
i32 = jnp.int32

SIDE = BX * HALO
QUAD = HALO * HALO
BAND = 4 * QUAD
EXT = 4 * SIDE + 2 * BAND
COUNTS = (SIDE, SIDE, SIDE, SIDE, BAND, BAND)
UNROLL = QUAD * HALO
STARTS = (0, SIDE, 2 * SIDE, 3 * SIDE, 4 * SIDE, 4 * SIDE + BAND)


def swaps(axis):
    bands, lanes = lax.axis_size("gx"), lax.axis_size("gy")

    def partner(g, l, first):
        i, count = (l, lanes) if axis == "gy" else (g, bands)
        other = i + 1 if (i - first) % 2 == 0 else i - 1
        if 0 <= other < count:
            return (g, other) if axis == "gy" else (other, l)
        if axis == "gy":
            return (g ^ 1, l) if bands % 2 == 0 else None
        return (g, l ^ 2) if lanes % 4 == 0 else None

    out = []
    for first in range(2):
        pairs = []
        for g in range(bands):
            for l in range(lanes):
                to = partner(g, l, first)
                if to is not None:
                    pairs.append((g * lanes + l, to[0] * lanes + to[1]))
        out.append(pairs)
    return out


def slot_of(ex, ey, odd_lane, odd_band):
    low = ey < BY // 2
    by_a = low == (odd_lane == 1)
    own = (ey >= 0) & (ey < BY)
    piece = jnp.where(own, jnp.where(by_a, 0, 1), jnp.where(by_a, 3, 2))
    column = (ey + HALO) % HALO
    inner = piece * SIDE + ex * HALO + column
    from_a = (ex < 0) == (odd_band == 1)
    row = jnp.where(ex < 0, ex + HALO, ex - BX)
    outer = jnp.where(from_a, STARTS[4], STARTS[5]) + piece * QUAD + row * HALO + column
    return jnp.where((ex >= 0) & (ex < BX), inner, outer)


def place_of(piece, i, odd_lane, odd_band):
    if piece < 4:
        part, ex = piece, i // HALO
    else:
        part, row = i // QUAD, i % QUAD // HALO
        up = (odd_band == 1) if piece == 4 else (odd_band == 0)
        ex = jnp.where(up, row - HALO, row + BX)
    by_a = (part == 0) | (part == 3)
    low = (by_a == (odd_lane == 1)) if not isinstance(by_a, bool) else (odd_lane == int(by_a))
    outside = part >= 2
    base = jnp.where(low, jnp.where(outside, -HALO, 0), jnp.where(outside, BY, BY - HALO))
    return ex, base + i % HALO


def split(meta_ref, x, pos_hbm, a, b, pos_a, pos_b, pos, sem, pos_sem):
    pos_copy = pltpu.make_async_copy(pos_hbm, pos, pos_sem)
    pos_copy.start()
    low_a = jnp.where(meta_ref[4] == 1, 0, BY - HALO)
    lows = (low_a, BY - HALO - low_a)
    copies = []
    for m, (out, low) in enumerate(zip((a, b), lows)):
        for r in range(BX):
            source = x.at[pl.ds(r * BY + low, HALO)]
            target = out.at[pl.ds(r * HALO, HALO)]
            copies.append(pltpu.make_async_copy(source, target, sem.at[m, r]))
    for copy in copies:
        copy.start()
    pos_copy.wait()
    for out, low in zip((pos_a, pos_b), lows):
        for r in range(BX):
            for i in range(HALO):
                for c in range(pos.shape[0]):
                    out[r * HALO + i, c : c + 1] = pos[c, pl.ds(r * BY + low + i, 1)]
    for copy in copies:
        copy.wait()


def pack(meta_ref, *refs):
    pieces, (out_a, out_b) = refs[:-2], refs[-2:]
    size = BX * HALO
    from_a = jnp.where(meta_ref[5] == 1, 0, size - QUAD)
    for n, x in enumerate(pieces):
        out_a[pl.ds(n * QUAD, QUAD)] = x[pl.ds(from_a, QUAD)]
        out_b[pl.ds(n * QUAD, QUAD)] = x[pl.ds(size - QUAD - from_a, QUAD)]


def swap(by_a, by_b, axis):
    pairs_a, pairs_b = swaps(axis)
    axis = ("gx", "gy")
    from_b = lax.ppermute(by_b, axis, pairs_b)
    from_a = lax.ppermute(by_a, axis, pairs_a)
    return from_a, from_b


def three_parts(x):
    high = x.astype(bf16).astype(f32)
    rest = x - high
    middle = rest.astype(bf16).astype(f32)
    return high, middle, rest - middle


def coordinates(pos, ex, ey):
    row = lax.broadcasted_iota(i32, (8, pos.shape[-1]), 0)
    padded = jnp.concatenate([pos, jnp.zeros((5, pos.shape[-1]), f32)], axis=0)
    middle = jnp.where(
        row == 0,
        ex.astype(f32) - (BX - 1) / 2,
        jnp.where(row == 1, ey.astype(f32) - (BY - 1) / 2, 0.0),
    )
    return (padded + middle) * SCALE, row


def features(pos, ex, ey, inside, as_target):
    x, row = coordinates(pos, ex, ey)
    norm = jnp.sum(x * x, axis=0, keepdims=True)
    high, middle, low = three_parts(x)
    nh, nm, nl = three_parts(norm)
    last = row == 3
    pick = lambda a, b: jnp.where(last, a, b)
    source = (
        pick(jnp.where(inside, -nh, FAR), high),
        pick(-nm, high),
        pick(-nl, middle),
        pick(1.0, high),
        pick(1.0, low),
        pick(1.0, middle),
    )
    source = jnp.concatenate(source, axis=0).astype(bf16).T
    if not as_target:
        return source, None
    high, middle, low = 2.0 * high, 2.0 * middle, 2.0 * low
    target = (
        pick(1.0, high),
        pick(1.0, middle),
        pick(1.0, high),
        pick(-nh, low),
        pick(-nm, high),
        pick(-nl, middle),
    )
    return source, jnp.concatenate(target, axis=0).astype(bf16)


def neighbours_of(near_ref):
    return near_ref.shape[0] // (BX * BY) - 1


def build_rows(near_ref, source, target, w_refs, first_row):
    parts = source.shape[1]
    neighbours = neighbours_of(near_ref)
    for g, w_ref in enumerate(w_refs):

        def one(c, _, g=g, w_ref=w_ref):
            b = (first_row + g) * BY + c
            f = target[b]
            for k in range(neighbours):
                q = near_ref[b * neighbours + k]
                e = jnp.dot(source[q], f, preferred_element_type=f32)
                w_ref[c, pl.ds(k * parts, parts)] = jnp.exp2(e.astype(bf16))
            return 0

        lax.fori_loop(0, BY, one, 0)


def build_first(
    near_ref, meta_ref, o0, o1, c0, c1, r0, r1, w0, source, target, row_ref, taken
):
    odd_lane, odd_band = meta_ref[4], meta_ref[5]
    for piece, ref in enumerate((o0, o1, c0, c1, r0, r1)):

        def some(j, _, piece=piece, ref=ref):
            for n in range(UNROLL):
                i = j * UNROLL + n
                ex, ey = place_of(piece, i, odd_lane, odd_band)
                gx = meta_ref[0] + ex
                gy = meta_ref[1] + ey
                inside = (gx >= 0) & (gx < meta_ref[2]) & (gy >= 0) & (gy < meta_ref[3])
                s, t = features(ref[i], ex, ey, inside, piece < 2)
                source[STARTS[piece] + i] = s
                if piece < 2:
                    target[ex * BY + ey] = t
            return 0

        lax.fori_loop(0, COUNTS[piece] // UNROLL, some, 0)
    for z in range(taken.shape[0]):
        taken[z] = 0

    def place(b, _):
        zone = near_ref[BX * BY * neighbours_of(near_ref) + b]
        order = taken[zone]
        taken[zone] = order + 1
        row_ref[b] = zone * CAP + order
        return 0

    lax.fori_loop(0, BX * BY, place, 0)
    build_rows(near_ref, source, target, (w0,), 0)


def build_second(near_ref, source, target, *w_refs):
    build_rows(near_ref, source, target, w_refs, BX - len(w_refs))


def column(row_ref):
    n = row_ref.shape[1]
    shape = (n, n)
    same = lax.broadcasted_iota(i32, shape, 0) == lax.broadcasted_iota(i32, shape, 1)
    return jnp.sum(jnp.where(same, row_ref[...], 0.0), axis=1, keepdims=True)


def react(mixture, kelvin, factor, onset):
    half = mixture.shape[0] // 2
    u = mixture[:half]
    v = mixture[half:]
    speed = factor * jnp.exp(-onset / kelvin)
    reacted = speed * u * v / (1.0 + speed * (u + v))
    return jnp.concatenate([u - reacted, v - reacted], axis=0).astype(bf16)


def mix(near_ref, species, gathered, w, b):
    neighbours = neighbours_of(near_ref)
    parts = species.shape[2]
    kinds = species.shape[1]
    for k in range(neighbours):
        q = near_ref[b * neighbours + k]
        gathered[:kinds, k * parts : (k + 1) * parts] = species[q]
    return jnp.dot(gathered[...], w, preferred_element_type=f32)


def join(pieces, species):
    start = 0
    for ref in pieces:
        species[pl.ds(start, ref.shape[0])] = ref[...]
        start += ref.shape[0]


def step_columns(near_ref, species, gathered, w_refs, consts, low, out_ref, inv_ref):
    kinds = species.shape[1]
    gathered[:, kinds:] = jnp.ones_like(gathered[:, kinds:])
    kelvin_ref, factor_ref, onset_ref = consts
    factor, onset = column(factor_ref), column(onset_ref)
    for g, w_ref in enumerate(w_refs):

        for i in range(HALO):
            c = low + i
            b = g * BY + c
            mixed = mix(near_ref, species, gathered.at[i], w_ref[c], b)
            inv = 1.0 / mixed[kinds : kinds + 1]
            inv_ref[pl.ds(g * HALO + i, 1)] = inv
            mixed = mixed[:kinds] * inv
            out_ref[g * HALO + i] = react(mixed, kelvin_ref[pl.ds(b, 1)], factor, onset)


def step_b(near_ref, meta_ref, *refs):
    pieces, w_refs, consts = refs[:6], refs[6:10], refs[10:13]
    out, inv_ref, species, gathered = refs[13:]
    join(pieces, species)
    low = jnp.where(meta_ref[4] == 1, BY - HALO, 0)
    step_columns(near_ref, species, gathered, w_refs, consts, low, out, inv_ref)


def step_a(near_ref, meta_ref, species, *refs):
    w_refs, consts = refs[:4], refs[4:7]
    out, inv_ref, gathered = refs[7:]
    low = jnp.where(meta_ref[4] == 1, 0, BY - HALO)
    step_columns(near_ref, species, gathered, w_refs, consts, low, out, inv_ref)


def last_step(near_ref, meta_ref, row_ref, *refs):
    pieces, refs = refs[:8], refs[8:]
    w_refs, (inv_a, inv_b), refs = refs[:4], refs[4:6], refs[6:]
    (kelvin_ref, factor_ref, onset_ref), refs = refs[:3], refs[3:]
    outs, (species, gathered, staged) = refs[:-3], refs[-3:]
    join(pieces, species)
    factor, onset = column(factor_ref), column(onset_ref)
    lane = meta_ref[1] // BY
    a_first = meta_ref[4] == 1
    if staged.shape[0] > BX * BY:
        staged[...] = jnp.zeros_like(staged)
    for g, w_ref in enumerate(w_refs):

        def some(g=g, w_ref=w_ref):
            for i in range(BY):
                c = i
                by_a = a_first if i < HALO else ~a_first
                at = pl.ds(g * HALO + i % HALO, 1)
                b = g * BY + c
                row = row_ref[b]
                mixed = mix(near_ref, species, gathered.at[i], w_ref[c], b)
                mixed = mixed * jnp.where(by_a, inv_a[at], inv_b[at])
                moved = react(mixed, kelvin_ref[pl.ds(b, 1)], factor, onset)
                staged[((row // CAP) ^ lane) * CAP + row % CAP] = moved
            return 0

        some()
    for i, out in enumerate(outs):
        out[...] = staged[i * CAP : (i + 1) * CAP]


def place(meta_ref, *refs):
    blocks, (out, sem) = refs[:-2], refs[-2:]
    lane = meta_ref[1] // BY
    copies = [
        pltpu.make_async_copy(x, out.at[pl.ds((lane ^ way) * CAP, CAP)], sem.at[way])
        for way, x in enumerate(blocks)
    ]
    for copy in copies:
        copy.start()
    for copy in copies:
        copy.wait()


VM = pl.BlockSpec(memory_space=pltpu.VMEM)
SM = pl.BlockSpec(memory_space=pltpu.SMEM)
HBM = pl.BlockSpec(memory_space=pltpu.HBM)


def call(kernel, operands, scalars, outs, scratch, flops):
    single = not isinstance(outs, (list, tuple))
    return pl.pallas_call(
        kernel,
        out_shape=outs,
        in_specs=[SM] * scalars + [VM] * (len(operands) - scalars),
        out_specs=VM if single else [SM if o.dtype == i32 else VM for o in outs],
        scratch_shapes=scratch,
        compiler_params=pltpu.CompilerParams(vmem_limit_bytes=8 << 20),
        cost_estimate=pl.CostEstimate(
            flops=flops, bytes_accessed=1 << 20, transcendentals=0
        ),
    )(*operands)


def body(
    solute_load,
    walker_displacement,
    local_kelvin,
    couple_kinetic_factor,
    arrhenius_onset,
    adjacent_cell_keys,
    downstream_zone,
):
    lane_count = lax.axis_size("gy")
    bins, kinds, parts = solute_load.shape
    neighbours = adjacent_cell_keys.shape[1]
    band, lane = lax.axis_index("gx"), lax.axis_index("gy")
    odd_band, odd_lane = band % 2, lane % 2

    meta = jnp.stack(
        [
            band * BX,
            lane * BY,
            jnp.int32(lax.axis_size("gx") * BX),
            jnp.int32(lane_count * BY),
            odd_lane,
            odd_band,
        ]
    ).astype(i32)
    like = lambda x, n: pltpu.VMEM((n,) + x.shape[1:], x.dtype)
    axes = walker_displacement.shape[1]
    own_a, own_b, pos_a, pos_b = pl.pallas_call(
        split,
        out_shape=[pltpu.VMEM((SIDE, kinds, parts), bf16)] * 2
        + [pltpu.VMEM((SIDE, axes, parts), f32)] * 2,
        in_specs=[SM, HBM, HBM],
        out_specs=[VM] * 4,
        scratch_shapes=[
            pltpu.VMEM((axes, bins, parts), f32),
            pltpu.SemaphoreType.DMA((2, BX)),
            pltpu.SemaphoreType.DMA,
        ],
        compiler_params=pltpu.CompilerParams(vmem_limit_bytes=8 << 20),
        name="split",
    )(
        meta,
        pltpu.with_memory_space_constraint(solute_load, pltpu.HBM),
        pltpu.with_memory_space_constraint(walker_displacement.transpose(1, 0, 2), pltpu.HBM),
    )

    def rows(pieces):
        size = len(pieces) * QUAD
        by_a, by_b = call(
            pack, (meta,) + pieces, 1, [like(pieces[0], size)] * 2, [], 1 << 20
        )
        return swap(by_a, by_b, "gx")

    pos_sides = swap(pos_a, pos_b, "gy")[::-1]
    pos_bands = rows((pos_a, pos_b) + pos_sides)
    own = (own_a, own_b)
    sides = swap(own_a, own_b, "gy")[::-1]
    bands = rows(own + sides)

    ids = jnp.arange(bins, dtype=i32)
    near = slot_of(
        (ids // BY)[:, None] + adjacent_cell_keys // WIDTH - HALO,
        (ids % BY)[:, None] + adjacent_cell_keys % WIDTH - HALO,
        odd_lane,
        odd_band,
    ).reshape(-1)
    near = jnp.concatenate([near, downstream_zone[:, 0]])
    consts = (local_kelvin, couple_kinetic_factor[None], arrhenius_onset[None])

    w_row = pltpu.VMEM((BY, neighbours * parts, parts), bf16)
    inv = pltpu.VMEM((SIDE, parts), f32)
    counted = pltpu.VMEM((HALO, kinds + 16, neighbours * parts), bf16)
    half = pltpu.VMEM((SIDE, kinds, parts), bf16)
    gathered = pltpu.VMEM((HALO, kinds, neighbours * parts), bf16)
    all_species = pltpu.VMEM((EXT, kinds, parts), bf16)
    work = 2 * bins * neighbours * parts * parts * 128
    w0, source, target, row = call(
        build_first,
        (near, meta, pos_a, pos_b) + pos_sides + pos_bands,
        2,
        [
            w_row,
            pltpu.VMEM((EXT, parts, FEATURES), bf16),
            pltpu.VMEM((bins, FEATURES, parts), bf16),
            jax.ShapeDtypeStruct((bins,), i32),
        ],
        [pltpu.SMEM((lane_count,), i32)],
        work,
    )
    w1, w2, w3 = call(build_second, (near, source, target), 1, [w_row] * 3, [], work)
    built = (w0, w1, w2, w3)
    by_b, inv_b, species = call(
        step_b,
        (near, meta) + own + sides + bands + built + consts,
        2,
        [half, inv, all_species],
        [counted],
        work // 2,
    )
    by_a, inv_a = call(
        step_a,
        (near, meta, species) + built + consts,
        2,
        [half, inv],
        [counted],
        work // 2,
    )

    own = (by_a, by_b)
    sides = swap(by_a, by_b, "gy")[::-1]
    early = rows(own + sides[:1])
    corners = rows(sides[1:])
    pieces = own + sides + (early[0], corners[0], early[1], corners[1])
    blocks = list(
        call(
            last_step,
            (near, meta, row) + pieces + built + (inv_a, inv_b) + consts,
            3,
            [pltpu.VMEM((CAP, kinds, parts), bf16)] * lane_count,
            [all_species, pltpu.VMEM((BY, kinds, neighbours * parts), bf16), pltpu.VMEM((lane_count * CAP, kinds, parts), bf16)],
            work,
        )
    )
    for way in range(lane_count - 1, 0, -1):
        pairs = [(l, l ^ way) for l in range(lane_count)]
        blocks[way] = lax.ppermute(blocks[way], "gy", pairs)
    return pl.pallas_call(
        place,
        out_shape=jax.ShapeDtypeStruct((lane_count * CAP, kinds, parts), bf16),
        in_specs=[SM] + [VM] * lane_count,
        out_specs=HBM,
        scratch_shapes=[pltpu.SemaphoreType.DMA((lane_count,))],
        compiler_params=pltpu.CompilerParams(vmem_limit_bytes=8 << 20),
        name="place",
    )(meta, *blocks)


def solution(mesh):
    in_specs = (
        P(("gx", "gy"), None, None),
        P(("gx", "gy"), None, None),
        P(("gx", "gy"), None),
        P(),
        P(),
        P(("gx", "gy"), None),
        P(("gx", "gy"), None),
    )
    out_specs = P(("gx", "gy"), None, None)
    return jax.shard_map(
        body, mesh=mesh, in_specs=in_specs, out_specs=out_specs, check_vma=False
    )
```

```python
import math

import jax
import jax.numpy as jnp
from jax import lax
from jax.experimental import pallas as pl
from jax.experimental.pallas import tpu as pltpu
from jax.sharding import PartitionSpec as P


BX = 4
BY = 4
CAP = 2
HALO = 2
WIDTH = 2 * HALO + 1

inverse_width = 4.0
SCALE = math.sqrt(inverse_width * math.log2(math.e))
FAR = -1e30
FEATURES = 48


f32 = jnp.float32
bf16 = jnp.bfloat16
i32 = jnp.int32

SIDE = BX * HALO
QUAD = HALO * HALO
BAND = 4 * QUAD
EXT = 4 * SIDE + 2 * BAND
COUNTS = (SIDE, SIDE, SIDE, SIDE, BAND, BAND)
UNROLL = QUAD * HALO
STARTS = (0, SIDE, 2 * SIDE, 3 * SIDE, 4 * SIDE, 4 * SIDE + BAND)


def swaps(axis):
    bands, lanes = lax.axis_size("gx"), lax.axis_size("gy")

    def partner(g, l, first):
        i, count = (l, lanes) if axis == "gy" else (g, bands)
        other = i + 1 if (i - first) % 2 == 0 else i - 1
        if 0 <= other < count:
            return (g, other) if axis == "gy" else (other, l)
        if axis == "gy":
            return (g ^ 1, l) if bands % 2 == 0 else None
        return (g, l ^ 2) if lanes % 4 == 0 else None

    out = []
    for first in range(2):
        pairs = []
        for g in range(bands):
            for l in range(lanes):
                to = partner(g, l, first)
                if to is not None:
                    pairs.append((g * lanes + l, to[0] * lanes + to[1]))
        out.append(pairs)
    return out


def slot_of(ex, ey, odd_lane, odd_band):
    low = ey < BY // 2
    by_a = low == (odd_lane == 1)
    own = (ey >= 0) & (ey < BY)
    piece = jnp.where(own, jnp.where(by_a, 0, 1), jnp.where(by_a, 3, 2))
    column = (ey + HALO) % HALO
    inner = piece * SIDE + ex * HALO + column
    from_a = (ex < 0) == (odd_band == 1)
    row = jnp.where(ex < 0, ex + HALO, ex - BX)
    outer = jnp.where(from_a, STARTS[4], STARTS[5]) + piece * QUAD + row * HALO + column
    return jnp.where((ex >= 0) & (ex < BX), inner, outer)


def place_of(piece, i, odd_lane, odd_band):
    if piece < 4:
        part, ex = piece, i // HALO
    else:
        part, row = i // QUAD, i % QUAD // HALO
        up = (odd_band == 1) if piece == 4 else (odd_band == 0)
        ex = jnp.where(up, row - HALO, row + BX)
    by_a = (part == 0) | (part == 3)
    low = (by_a == (odd_lane == 1)) if not isinstance(by_a, bool) else (odd_lane == int(by_a))
    outside = part >= 2
    base = jnp.where(low, jnp.where(outside, -HALO, 0), jnp.where(outside, BY, BY - HALO))
    return ex, base + i % HALO


def split(meta_ref, x, pos_hbm, a, b, pos_a, pos_b, pos, sem, pos_sem):
    pos_copy = pltpu.make_async_copy(pos_hbm, pos, pos_sem)
    pos_copy.start()
    low_a = jnp.where(meta_ref[4] == 1, 0, BY - HALO)
    lows = (low_a, BY - HALO - low_a)
    copies = []
    for m, (out, low) in enumerate(zip((a, b), lows)):
        for r in range(BX):
            source = x.at[pl.ds(r * BY + low, HALO)]
            target = out.at[pl.ds(r * HALO, HALO)]
            copies.append(pltpu.make_async_copy(source, target, sem.at[m, r]))
    for copy in copies:
        copy.start()
    pos_copy.wait()
    for out, low in zip((pos_a, pos_b), lows):
        for r in range(BX):
            for i in range(HALO):
                for c in range(pos.shape[0]):
                    out[r * HALO + i, c : c + 1] = pos[c, pl.ds(r * BY + low + i, 1)]
    for copy in copies:
        copy.wait()


def pack(meta_ref, *refs):
    pieces, (out_a, out_b) = refs[:-2], refs[-2:]
    size = BX * HALO
    from_a = jnp.where(meta_ref[5] == 1, 0, size - QUAD)
    for n, x in enumerate(pieces):
        out_a[pl.ds(n * QUAD, QUAD)] = x[pl.ds(from_a, QUAD)]
        out_b[pl.ds(n * QUAD, QUAD)] = x[pl.ds(size - QUAD - from_a, QUAD)]


def swap(by_a, by_b, axis):
    pairs_a, pairs_b = swaps(axis)
    axis = ("gx", "gy")
    from_b = lax.ppermute(by_b, axis, pairs_b)
    from_a = lax.ppermute(by_a, axis, pairs_a)
    return from_a, from_b


def three_parts(x):
    high = x.astype(bf16).astype(f32)
    rest = x - high
    middle = rest.astype(bf16).astype(f32)
    return high, middle, rest - middle


def coordinates(pos, ex, ey):
    row = lax.broadcasted_iota(i32, (8, pos.shape[-1]), 0)
    padded = jnp.concatenate([pos, jnp.zeros((5, pos.shape[-1]), f32)], axis=0)
    middle = jnp.where(
        row == 0,
        ex.astype(f32) - (BX - 1) / 2,
        jnp.where(row == 1, ey.astype(f32) - (BY - 1) / 2, 0.0),
    )
    return (padded + middle) * SCALE, row


def features(pos, ex, ey, inside, as_target):
    x, row = coordinates(pos, ex, ey)
    norm = jnp.sum(x * x, axis=0, keepdims=True)
    high, middle, low = three_parts(x)
    nh, nm, nl = three_parts(norm)
    last = row == 3
    pick = lambda a, b: jnp.where(last, a, b)
    source = (
        pick(jnp.where(inside, -nh, FAR), high),
        pick(-nm, high),
        pick(-nl, middle),
        pick(1.0, high),
        pick(1.0, low),
        pick(1.0, middle),
    )
    source = jnp.concatenate(source, axis=0).astype(bf16).T
    if not as_target:
        return source, None
    high, middle, low = 2.0 * high, 2.0 * middle, 2.0 * low
    target = (
        pick(1.0, high),
        pick(1.0, middle),
        pick(1.0, high),
        pick(-nh, low),
        pick(-nm, high),
        pick(-nl, middle),
    )
    return source, jnp.concatenate(target, axis=0).astype(bf16)


def neighbours_of(near_ref):
    return near_ref.shape[0] // (BX * BY) - 1


def build_rows(near_ref, source, target, w_refs, first_row):
    parts = source.shape[1]
    neighbours = neighbours_of(near_ref)
    for g, w_ref in enumerate(w_refs):

        def one(c, _, g=g, w_ref=w_ref):
            b = (first_row + g) * BY + c
            f = target[b]
            for k in range(neighbours):
                q = near_ref[b * neighbours + k]
                e = jnp.dot(source[q], f, preferred_element_type=f32)
                w_ref[c, pl.ds(k * parts, parts)] = jnp.exp2(e.astype(bf16))
            return 0

        lax.fori_loop(0, BY, one, 0)


def put_features(meta_ref, first, refs, source, target):
    odd_lane, odd_band = meta_ref[4], meta_ref[5]
    for piece, ref in enumerate(refs, first):

        def some(j, _, piece=piece, ref=ref):
            for n in range(UNROLL):
                i = j * UNROLL + n
                ex, ey = place_of(piece, i, odd_lane, odd_band)
                gx = meta_ref[0] + ex
                gy = meta_ref[1] + ey
                inside = (gx >= 0) & (gx < meta_ref[2]) & (gy >= 0) & (gy < meta_ref[3])
                s, t = features(ref[i], ex, ey, inside, piece < 2)
                source[STARTS[piece] + i] = s
                if piece < 2:
                    target[ex * BY + ey] = t
            return 0

        lax.fori_loop(0, COUNTS[piece] // UNROLL, some, 0)


def prepare(meta_ref, o0, o1, c0, c1, source, target):
    put_features(meta_ref, 0, (o0, o1, c0, c1), source, target)


def build_first(near_ref, meta_ref, _, target, r0, r1, w0, source, row_ref, taken):
    put_features(meta_ref, 4, (r0, r1), source, None)
    for z in range(taken.shape[0]):
        taken[z] = 0

    def place(b, _):
        zone = near_ref[BX * BY * neighbours_of(near_ref) + b]
        order = taken[zone]
        taken[zone] = order + 1
        row_ref[b] = zone * CAP + order
        return 0

    lax.fori_loop(0, BX * BY, place, 0)
    build_rows(near_ref, source, target, (w0,), 0)


def build_second(near_ref, source, target, *w_refs):
    build_rows(near_ref, source, target, w_refs, BX - len(w_refs))


def column(row_ref):
    n = row_ref.shape[1]
    shape = (n, n)
    same = lax.broadcasted_iota(i32, shape, 0) == lax.broadcasted_iota(i32, shape, 1)
    return jnp.sum(jnp.where(same, row_ref[...], 0.0), axis=1, keepdims=True)


def react(mixture, kelvin, factor, onset):
    half = mixture.shape[0] // 2
    u = mixture[:half]
    v = mixture[half:]
    speed = factor * jnp.exp(-onset / kelvin)
    reacted = speed * u * v / (1.0 + speed * (u + v))
    return jnp.concatenate([u - reacted, v - reacted], axis=0).astype(bf16)


def mix(near_ref, species, gathered, w, b):
    neighbours = neighbours_of(near_ref)
    parts = species.shape[2]
    kinds = species.shape[1]
    for k in range(neighbours):
        q = near_ref[b * neighbours + k]
        gathered[:kinds, k * parts : (k + 1) * parts] = species[q]
    return jnp.dot(gathered[...], w, preferred_element_type=f32)


def join(pieces, species):
    start = 0
    for ref in pieces:
        species[pl.ds(start, ref.shape[0])] = ref[...]
        start += ref.shape[0]


def step_columns(near_ref, species, gathered, w_refs, consts, low, out_ref, inv_ref):
    kinds = species.shape[1]
    gathered[:, kinds:] = jnp.ones_like(gathered[:, kinds:])
    kelvin_ref, factor_ref, onset_ref = consts
    factor, onset = column(factor_ref), column(onset_ref)
    for g, w_ref in enumerate(w_refs):

        for i in range(HALO):
            c = low + i
            b = g * BY + c
            mixed = mix(near_ref, species, gathered.at[i], w_ref[c], b)
            inv = 1.0 / mixed[kinds : kinds + 1]
            inv_ref[pl.ds(g * HALO + i, 1)] = inv
            mixed = mixed[:kinds] * inv
            out_ref[g * HALO + i] = react(mixed, kelvin_ref[pl.ds(b, 1)], factor, onset)


def step_b(near_ref, meta_ref, *refs):
    pieces, w_refs, consts = refs[:6], refs[6:10], refs[10:13]
    out, inv_ref, species, gathered = refs[13:]
    join(pieces, species)
    low = jnp.where(meta_ref[4] == 1, BY - HALO, 0)
    step_columns(near_ref, species, gathered, w_refs, consts, low, out, inv_ref)


def step_a(near_ref, meta_ref, species, *refs):
    w_refs, consts = refs[:4], refs[4:7]
    out, inv_ref, gathered = refs[7:]
    low = jnp.where(meta_ref[4] == 1, 0, BY - HALO)
    step_columns(near_ref, species, gathered, w_refs, consts, low, out, inv_ref)


def last_step(near_ref, meta_ref, row_ref, *refs):
    pieces, refs = refs[:8], refs[8:]
    w_refs, (inv_a, inv_b), refs = refs[:4], refs[4:6], refs[6:]
    (kelvin_ref, factor_ref, onset_ref), refs = refs[:3], refs[3:]
    outs, (species, gathered, staged) = refs[:-3], refs[-3:]
    join(pieces, species)
    factor, onset = column(factor_ref), column(onset_ref)
    lane = meta_ref[1] // BY
    a_first = meta_ref[4] == 1
    if staged.shape[0] > BX * BY:
        staged[...] = jnp.zeros_like(staged)
    for g, w_ref in enumerate(w_refs):

        def some(g=g, w_ref=w_ref):
            for i in range(BY):
                c = i
                by_a = a_first if i < HALO else ~a_first
                at = pl.ds(g * HALO + i % HALO, 1)
                b = g * BY + c
                row = row_ref[b]
                mixed = mix(near_ref, species, gathered.at[i], w_ref[c], b)
                mixed = mixed * jnp.where(by_a, inv_a[at], inv_b[at])
                moved = react(mixed, kelvin_ref[pl.ds(b, 1)], factor, onset)
                staged[((row // CAP) ^ lane) * CAP + row % CAP] = moved
            return 0

        some()
    for i, out in enumerate(outs):
        out[...] = staged[i * CAP : (i + 1) * CAP]


def place(meta_ref, *refs):
    blocks, (out, sem) = refs[:-2], refs[-2:]
    lane = meta_ref[1] // BY
    copies = [
        pltpu.make_async_copy(x, out.at[pl.ds((lane ^ way) * CAP, CAP)], sem.at[way])
        for way, x in enumerate(blocks)
    ]
    for copy in copies:
        copy.start()
    for copy in copies:
        copy.wait()


VM = pl.BlockSpec(memory_space=pltpu.VMEM)
SM = pl.BlockSpec(memory_space=pltpu.SMEM)
HBM = pl.BlockSpec(memory_space=pltpu.HBM)


def call(kernel, operands, scalars, outs, scratch, flops, aliases=None):
    single = not isinstance(outs, (list, tuple))
    return pl.pallas_call(
        kernel,
        out_shape=outs,
        in_specs=[SM] * scalars + [VM] * (len(operands) - scalars),
        out_specs=VM if single else [SM if o.dtype == i32 else VM for o in outs],
        scratch_shapes=scratch,
        input_output_aliases=aliases or {},
        compiler_params=pltpu.CompilerParams(vmem_limit_bytes=8 << 20),
        cost_estimate=pl.CostEstimate(
            flops=flops, bytes_accessed=1 << 20, transcendentals=0
        ),
    )(*operands)


def body(
    solute_load,
    walker_displacement,
    local_kelvin,
    couple_kinetic_factor,
    arrhenius_onset,
    adjacent_cell_keys,
    downstream_zone,
):
    lane_count = lax.axis_size("gy")
    bins, kinds, parts = solute_load.shape
    neighbours = adjacent_cell_keys.shape[1]
    band, lane = lax.axis_index("gx"), lax.axis_index("gy")
    odd_band, odd_lane = band % 2, lane % 2

    meta = jnp.stack(
        [
            band * BX,
            lane * BY,
            jnp.int32(lax.axis_size("gx") * BX),
            jnp.int32(lane_count * BY),
            odd_lane,
            odd_band,
        ]
    ).astype(i32)
    like = lambda x, n: pltpu.VMEM((n,) + x.shape[1:], x.dtype)
    axes = walker_displacement.shape[1]
    own_a, own_b, pos_a, pos_b = pl.pallas_call(
        split,
        out_shape=[pltpu.VMEM((SIDE, kinds, parts), bf16)] * 2
        + [pltpu.VMEM((SIDE, axes, parts), f32)] * 2,
        in_specs=[SM, HBM, HBM],
        out_specs=[VM] * 4,
        scratch_shapes=[
            pltpu.VMEM((axes, bins, parts), f32),
            pltpu.SemaphoreType.DMA((2, BX)),
            pltpu.SemaphoreType.DMA,
        ],
        compiler_params=pltpu.CompilerParams(vmem_limit_bytes=8 << 20),
        name="split",
    )(
        meta,
        pltpu.with_memory_space_constraint(solute_load, pltpu.HBM),
        pltpu.with_memory_space_constraint(walker_displacement.transpose(1, 0, 2), pltpu.HBM),
    )

    def rows(pieces):
        size = len(pieces) * QUAD
        by_a, by_b = call(
            pack, (meta,) + pieces, 1, [like(pieces[0], size)] * 2, [], 1 << 20
        )
        return by_a, by_b

    def swap_rows(pieces):
        return swap(*rows(pieces), "gx")

    pos_sides = swap(pos_a, pos_b, "gy")[::-1]
    packed_a, packed_b = rows((pos_a, pos_b) + pos_sides)
    packed_a, keys = lax.optimization_barrier((packed_a, adjacent_cell_keys))
    pos_bands = swap(packed_a, packed_b, "gx")
    own = (own_a, own_b)
    sides = swap(own_a, own_b, "gy")[::-1]
    bands = swap_rows(own + sides)

    ids = jnp.arange(bins, dtype=i32)
    near = slot_of(
        (ids // BY)[:, None] + keys // WIDTH - HALO,
        (ids % BY)[:, None] + keys % WIDTH - HALO,
        odd_lane,
        odd_band,
    ).reshape(-1)
    near = jnp.concatenate([near, downstream_zone[:, 0]])
    consts = (local_kelvin, couple_kinetic_factor[None], arrhenius_onset[None])

    w_row = pltpu.VMEM((BY, neighbours * parts, parts), bf16)
    inv = pltpu.VMEM((SIDE, parts), f32)
    counted = pltpu.VMEM((HALO, kinds + 16, neighbours * parts), bf16)
    half = pltpu.VMEM((SIDE, kinds, parts), bf16)
    gathered = pltpu.VMEM((HALO, kinds, neighbours * parts), bf16)
    all_species = pltpu.VMEM((EXT, kinds, parts), bf16)
    work = 2 * bins * neighbours * parts * parts * 128
    source_space = pltpu.VMEM((EXT, parts, FEATURES), bf16)
    source, target = call(
        prepare,
        (meta, pos_a, pos_b) + pos_sides,
        1,
        [source_space, pltpu.VMEM((bins, FEATURES, parts), bf16)],
        [],
        1 << 20,
    )
    w0, source, row = call(
        build_first,
        (near, meta, source, target) + pos_bands,
        2,
        [w_row, source_space, jax.ShapeDtypeStruct((bins,), i32)],
        [pltpu.SMEM((lane_count,), i32)],
        work,
        {2: 1},
    )
    w1, w2, w3 = call(build_second, (near, source, target), 1, [w_row] * 3, [], work)
    built = (w0, w1, w2, w3)
    by_b, inv_b, species = call(
        step_b,
        (near, meta) + own + sides + bands + built + consts,
        2,
        [half, inv, all_species],
        [counted],
        work // 2,
    )
    by_a, inv_a = call(
        step_a,
        (near, meta, species) + built + consts,
        2,
        [half, inv],
        [counted],
        work // 2,
    )

    own = (by_a, by_b)
    sides = swap(by_a, by_b, "gy")[::-1]
    early = swap_rows(own + sides[:1])
    corners = swap_rows(sides[1:])
    pieces = own + sides + (early[0], corners[0], early[1], corners[1])
    blocks = list(
        call(
            last_step,
            (near, meta, row) + pieces + built + (inv_a, inv_b) + consts,
            3,
            [pltpu.VMEM((CAP, kinds, parts), bf16)] * lane_count,
            [all_species, pltpu.VMEM((BY, kinds, neighbours * parts), bf16), pltpu.VMEM((lane_count * CAP, kinds, parts), bf16)],
            work,
        )
    )
    for way in range(lane_count - 1, 0, -1):
        pairs = [(l, l ^ way) for l in range(lane_count)]
        blocks[way] = lax.ppermute(blocks[way], "gy", pairs)
    return pl.pallas_call(
        place,
        out_shape=jax.ShapeDtypeStruct((lane_count * CAP, kinds, parts), bf16),
        in_specs=[SM] + [VM] * lane_count,
        out_specs=HBM,
        scratch_shapes=[pltpu.SemaphoreType.DMA((lane_count,))],
        compiler_params=pltpu.CompilerParams(vmem_limit_bytes=8 << 20),
        name="place",
    )(meta, *blocks)


def solution(mesh):
    in_specs = (
        P(("gx", "gy"), None, None),
        P(("gx", "gy"), None, None),
        P(("gx", "gy"), None),
        P(),
        P(),
        P(("gx", "gy"), None),
        P(("gx", "gy"), None),
    )
    out_specs = P(("gx", "gy"), None, None)
    return jax.shard_map(
        body, mesh=mesh, in_specs=in_specs, out_specs=out_specs, check_vma=False
    )
```
